32 devices in a mesh: dp: 4 (over y, x), tensor: 8 (over z, core).
Axes of the slice: x: 2, y: 2, z: 4, core: 2. Of those that a mesh axis runs over, the one named last changes fastest.
Arguments:
- activations: bfloat16 [1024, 16384], P('dp', 'tensor'), may hold values from -6 to 6
- angles: float32 [14, 8192], P(None, 'tensor'), may hold values from -3.140625 to 3.140625
- clip_bits: int32 [64, 16384], P('dp', 'tensor'), may hold values from 0 to 65535, as said below
- codes: bfloat16 [16384, 10240], P('tensor', 'dp'), may hold values from -127 to 127, as said below
- exponents: int32 [10240], replicated, may hold values from -16 to -13
- cotangent: bfloat16 [1024, 10240], P('dp', 'tensor'), may hold values from -6 to 6
Outputs:
- input_grad: bfloat16 [1024, 16384], P('dp', 'tensor')
- angle_grad: float32 [14, 8192], P(None, 'tensor')
The draws below stay inside these ranges and needn't reach their ends.
Inputs may be any that keep to these rules, and one draw needn't show every extreme that they name: Bit k (0 to 15) of clip_bits[w, i] is the clip mask of token 16 w + k at feature i; higher bits are zero. `codes`: every entry is a whole number.
All inputs are finite; a program needn't handle non-finite values.
Results may differ from the reference program's by a relative error of at most 0.003.
Values may be sent and summed in bfloat16 or wider, within the bound.
No kernel may reach another device: no remote copies, remote signals or barrier semaphores. Data moves between devices by JAX's collectives and lax.ppermute only.
A program may use at most 128 MiB of HBM per device.

```python
import jax
import jax.numpy as jnp
from jax import lax

D = 16384
OUT = 10240
SECTIONS = 14
TOK_DEV = 256
TOKENS = 1024


def draw_clip_bits(key, part):
    shape = (TOKENS // 16, D)

    def add_bit(k, total):
        level = jax.random.randint(jax.random.fold_in(key, k), shape, 0, 8)
        bit = jnp.where(level != 0, 1, 0).astype(jnp.int32)
        return total + jnp.left_shift(bit, k)
    total = lax.fori_loop(0, 16, add_bit, jnp.zeros(shape, jnp.int32))
    return total.at[0, :].set(65535)


def draw_codes(key, part):
    first = jax.random.fold_in(key, 11)
    second = jax.random.fold_in(key, 12)
    values = jax.random.randint(first, (D, OUT), -64, 64) + jax.random.randint(second, (D, OUT), -63, 64)
    return values.astype(jnp.float32).astype(jnp.bfloat16)


def set_ends(array, key, smallest, top_value):
    shape = array.shape
    index_at = [jax.random.randint(jax.random.fold_in(key, axis), (), 0, shape[axis]) for axis in range(len(shape))]
    array = array.at[tuple(index_at)].set(smallest)
    longest = shape.index(max(shape))
    index_at[longest] = (index_at[longest] + 1) % shape[longest]
    return array.at[tuple(index_at)].set(top_value)


def block_scale(stream_key, dims, split, smallest, top_value):
    gain = 1.0
    for position, shards_of in split:
        steps = jax.random.uniform(jax.random.fold_in(jax.random.fold_in(stream_key, 6), position), (shards_of,), jnp.float32, smallest / len(split), top_value / len(split))
        gain = gain * jnp.repeat(jnp.exp(steps), dims[position] // shards_of).reshape((-1,) + (1,) * (len(dims) - 1 - position))
    return gain


def bell_draw(stream_key, shape, scale, most, split=(), held_as=jnp.bfloat16):
    gain = block_scale(stream_key, shape, split, -0.22, 0.18) if split else 1.0
    values = jax.random.normal(stream_key, shape, jnp.float32) * scale * gain
    return jnp.minimum(jnp.maximum(values, -most), most).astype(held_as)


def setup_inputs(seed: int = 0) -> dict:
    seeds = jax.random.split(jax.random.key(seed), 7)
    activations = bell_draw(seeds[0], (TOKENS, D), 1.0, 6.0, ((0, 4), (1, 8)))
    angles = jnp.clip(jax.random.uniform(seeds[1], (SECTIONS, D // 2), jnp.float32, -3.140625, 3.140625), -3.140625, 3.140625)
    clip_bits = draw_clip_bits(jax.random.fold_in(seeds[6], 71), 0)
    codes = draw_codes(jax.random.fold_in(seeds[6], 71), 0)
    exponents = set_ends(jax.random.randint(seeds[4], (OUT,), -16, -12), jax.random.fold_in(seeds[4], 1), -16, (-12) - 1).astype(jnp.int32)
    cotangent = bell_draw(seeds[5], (TOKENS, OUT), 1.0, 6.0, ((0, 4), (1, 8)))
    return dict(activations=activations, angles=angles, clip_bits=clip_bits, codes=codes, exponents=exponents, cotangent=cotangent)


def unpack_mask(words, rows):
    shifts = jnp.arange(16, dtype=jnp.int32)
    bits = jnp.bitwise_and(jnp.right_shift(words[:, None, :], shifts[None, :, None]), 1)
    return bits.reshape(rows, words.shape[1]).astype(jnp.float32)


def split_pairs(field, angle_row, section):
    rows, width = field.shape
    half = 2 ** section
    shaped = field.reshape(rows, width // (2 * half), 2, half)
    theta = angle_row.reshape(width // (2 * half), half)
    return jnp.cos(theta), jnp.sin(theta), shaped[:, :, 0, :], shaped[:, :, 1, :]


def forward_section(field, angle_row, section):
    cosine, sine, lower, upper = split_pairs(field, angle_row, section)
    new_lower = cosine * lower - sine * upper
    new_upper = sine * lower + cosine * upper
    return jnp.stack([new_lower, new_upper], axis=2).reshape(field.shape)


def block_pass(acts, words, cots, weight, angles):
    rows = acts.shape[0]
    passed = unpack_mask(words, rows)
    projected = lax.dot_general(cots, weight, (((1,), (1,)), ((), ())), preferred_element_type=jnp.float32)
    grad = projected * passed
    states = [acts.astype(jnp.float32)]
    for section in range(SECTIONS):
        states.append(forward_section(states[-1], angles[section], section))
    terms = [None] * SECTIONS
    for section in reversed(range(SECTIONS)):
        cosine, sine, out_lower, out_upper = split_pairs(states[section + 1], angles[section], section)
        unused_c, unused_s, grad_lower, grad_upper = split_pairs(grad, angles[section], section)
        terms[section] = jnp.sum(grad_upper * out_lower - grad_lower * out_upper, axis=0).reshape(-1)
        prev_lower = cosine * grad_lower + sine * grad_upper
        prev_upper = cosine * grad_upper - sine * grad_lower
        grad = jnp.stack([prev_lower, prev_upper], axis=2).reshape(grad.shape)
    return grad.astype(jnp.bfloat16), jnp.stack(terms)


def reference(activations, angles, clip_bits, codes, exponents, cotangent):
    scale = jnp.exp2(exponents.astype(jnp.float32))
    weight = (codes.astype(jnp.float32) * scale[None, :]).astype(jnp.bfloat16)
    blocks = TOKENS // TOK_DEV
    acts = activations.reshape(blocks, TOK_DEV, D)
    words = clip_bits.reshape(blocks, TOK_DEV // 16, D)
    cots = cotangent.reshape(blocks, TOK_DEV, OUT)

    def step(total, items):
        grad, terms = block_pass(items[0], items[1], items[2], weight, angles)
        return total + terms, grad

    total, grads = lax.scan(step, jnp.zeros((SECTIONS, D // 2), jnp.float32), (acts, words, cots))
    return grads.reshape(TOKENS, D), total
```

```python
import functools

import jax
import jax.numpy as jnp
from jax import lax
from jax.experimental import pallas as pl
from jax.experimental.pallas import tpu as pltpu
from jax.sharding import PartitionSpec as P

LANES = 128
LANE_BITS = 7
HIGH = lax.Precision.HIGHEST


def swap(value, axis, mask):
    pairs = [(source, source ^ mask) for source in range(lax.axis_size(axis))]
    return lax.ppermute(value, axis, pairs)


def pick(stacked, index):
    return lax.dynamic_index_in_dim(stacked, index, 0, keepdims=False)


def drop_bit(index, bit):
    return ((index >> (bit + 1)) << bit) | (index & ((1 << bit) - 1))


def lane_selectors(sections):
    lane = jnp.arange(LANES, dtype=jnp.int32)
    rows = []
    signs = []
    for section in range(sections):
        pair = drop_bit(lane, section)
        hot = pair[None, :] == jnp.arange(LANES // 2, dtype=jnp.int32)[:, None]
        rows.append(hot.astype(jnp.float32))
        signs.append(jnp.where((lane >> section) & 1 == 0, -1.0, 1.0).astype(jnp.float32))
    return jnp.stack(rows), jnp.stack(signs)


def local_tables(cosine, sine, width):
    local = cosine.shape[0]
    tiles = width // LANES
    hot, signs = lane_selectors(LANE_BITS)

    def lanes(values):
        shaped = values[:LANE_BITS].reshape(LANE_BITS, tiles, LANES // 2)
        return jnp.einsum("stk,skl->stl", shaped, hot, precision=HIGH)

    def whole(section, values, sign):
        step = 1 << (section - LANE_BITS)
        shaped = values.reshape(tiles // (2 * step), 1, step, LANES)
        return jnp.concatenate([sign * shaped, shaped], axis=1).reshape(1, tiles, LANES)

    cos_rows = [lanes(cosine)]
    sin_rows = [lanes(sine) * signs[:, None, :]]
    for section in range(LANE_BITS, local):
        cos_rows.append(whole(section, cosine[section], 1.0))
        sin_rows.append(whole(section, sine[section], -1.0))
    cos_table = jnp.concatenate(cos_rows, axis=0).reshape(local, width)
    sin_table = jnp.concatenate(sin_rows, axis=0).reshape(local, width)
    return cos_table, sin_table


def lane_partner(value, section):
    half = 1 << section
    lane = lax.broadcasted_iota(jnp.int32, value.shape, 1)
    up = pltpu.roll(value, half, 1)
    if 2 * half == LANES:
        return up
    down = pltpu.roll(value, LANES - half, 1)
    return jnp.where((lane & half) == 0, down, up)


def tile_at(tile):
    return pl.ds(tile * LANES, LANES)


def forward_kernel(local, act_ref, cos_ref, sin_ref, states_ref, last_ref):
    rows, width = act_ref.shape
    tiles = width // LANES
    step = 16

    def block(index, carry):
        at = pl.ds(pl.multiple_of(index * step, step), step)
        field = []
        for tile in range(tiles):
            value = act_ref[at, tile_at(tile)].astype(jnp.float32)
            for section in range(LANE_BITS):
                other = lane_partner(value, section)
                cosine = cos_ref[section : section + 1, tile_at(tile)]
                signed = sin_ref[section : section + 1, tile_at(tile)]
                value = cosine * value + signed * other
                states_ref[section, at, tile_at(tile)] = value
            field.append(value)
        for section in range(LANE_BITS, local):
            gap = 1 << (section - LANE_BITS)
            for tile in range(tiles):
                if tile & gap:
                    continue
                cosine = cos_ref[section : section + 1, tile_at(tile)]
                signed = sin_ref[section : section + 1, tile_at(tile)]
                low, high = field[tile], field[tile + gap]
                field[tile] = cosine * low + signed * high
                field[tile + gap] = cosine * high - signed * low
            for tile in range(tiles):
                states_ref[section, at, tile_at(tile)] = field[tile]
        for tile in range(tiles):
            last_ref[at, tile_at(tile)] = field[tile].astype(last_ref.dtype)
        return carry

    lax.fori_loop(0, rows // step, block, 0)


def forward_local(acts, cos_table, sin_table):
    rows, width = acts.shape
    local = cos_table.shape[0]
    block = min(rows, 32)
    table = pl.BlockSpec((local, width), lambda i: (0, 0))
    return pl.pallas_call(
        functools.partial(forward_kernel, local),
        grid=(rows // block,),
        in_specs=[pl.BlockSpec((block, width), lambda i: (i, 0)), table, table],
        out_specs=[
            pl.BlockSpec((local, block, width), lambda i: (0, i, 0)),
            pl.BlockSpec((block, width), lambda i: (i, 0)),
        ],
        out_shape=[
            jax.ShapeDtypeStruct((local, rows, width), jnp.float32),
            jax.ShapeDtypeStruct((rows, width), jnp.bfloat16),
        ],
        cost_estimate=pl.CostEstimate(
            flops=6 * local * rows * width,
            bytes_accessed=4 * (local + 1) * rows * width,
            transcendentals=0,
        ),
        name="forward_local",
    )(acts, cos_table, sin_table)


def backward_kernel(
    local, me_ref, grad_ref, states_ref, cos_ref, sin_ref, hot_ref,
    out_ref, lane_out, tile_out, lane_sum, tile_sum,
):
    rows, width = out_ref.shape
    tiles = width // LANES
    step = 16
    index = pl.program_id(0)

    @pl.when(index == 0)
    def _():
        lane_sum[...] = jnp.zeros_like(lane_sum)
        tile_sum[...] = jnp.zeros_like(tile_sum)

    def folded(value):
        return jnp.sum(value.reshape(step // 8, 8, LANES), axis=0)

    def block(number, carry):
        at = pl.ds(pl.multiple_of(number * step, step), step)
        grad = [grad_ref[0, at, tile_at(tile)] for tile in range(tiles)]
        for section in reversed(range(LANE_BITS, local)):
            gap = 1 << (section - LANE_BITS)
            for tile in range(tiles):
                if tile & gap:
                    continue
                cosine = cos_ref[section : section + 1, tile_at(tile)]
                signed = sin_ref[section : section + 1, tile_at(tile)]
                low, high = grad[tile], grad[tile + gap]
                before_low = states_ref[section, at, tile_at(tile)]
                before_high = states_ref[section, at, tile_at(tile + gap)]
                term = folded(high * before_low - low * before_high)
                place = drop_bit(tile, section - LANE_BITS)
                tile_sum[section - LANE_BITS, place] += term
                grad[tile] = cosine * low - signed * high
                grad[tile + gap] = cosine * high + signed * low
        for tile in range(tiles):
            value = grad[tile]
            for section in reversed(range(LANE_BITS)):
                cosine = cos_ref[section : section + 1, tile_at(tile)]
                signed = sin_ref[section : section + 1, tile_at(tile)]
                other = lane_partner(value, section)
                state = states_ref[section, at, tile_at(tile)]
                lane_sum[section, tile] += folded(other * state)
                value = cosine * value - signed * other
            out_ref[at, tile_at(tile)] = value.astype(out_ref.dtype)
        return carry

    lax.fori_loop(0, rows // step, block, 0)

    @pl.when(index == pl.num_programs(0) - 1)
    def _():
        for section in range(LANE_BITS):
            summed = jnp.sum(lane_sum[section], axis=1)
            lane_out[section] = lax.dot_general(
                summed,
                hot_ref[section],
                (((1,), (1,)), ((), ())),
                precision=HIGH,
                preferred_element_type=jnp.float32,
            )
        for section in range(local - LANE_BITS):
            tile_out[section] = jnp.sum(tile_sum[section], axis=1)


def backward_local(me, grads, states, cos_table, sin_table):
    pieces, rows, width = grads.shape
    local = cos_table.shape[0]
    tiles = width // LANES
    high = local - LANE_BITS
    hot, signs = lane_selectors(LANE_BITS)
    hot = -hot * signs[:, None, :]
    table = pl.BlockSpec((local, width), lambda i, m: (0, 0))
    return pl.pallas_call(
        functools.partial(backward_kernel, local),
        grid_spec=pltpu.PrefetchScalarGridSpec(
            num_scalar_prefetch=1,
            grid=(pieces,),
            in_specs=[
                pl.BlockSpec((1, rows, width), lambda i, m: (i, 0, 0)),
                pl.BlockSpec((local, rows, width), lambda i, m: (0, m[0] ^ i, 0)),
                table,
                table,
                pl.BlockSpec(hot.shape, lambda i, m: (0, 0, 0)),
            ],
            out_specs=[
                pl.BlockSpec((rows, width), lambda i, m: (m[0] ^ i, 0)),
                pl.BlockSpec((LANE_BITS, tiles, LANES // 2), lambda i, m: (0, 0, 0)),
                pl.BlockSpec((high, tiles // 2, LANES), lambda i, m: (0, 0, 0)),
            ],
            scratch_shapes=[
                pltpu.VMEM((LANE_BITS, tiles, 8, LANES), jnp.float32),
                pltpu.VMEM((high, tiles // 2, 8, LANES), jnp.float32),
            ],
        ),
        out_shape=[
            jax.ShapeDtypeStruct((pieces * rows, width), jnp.bfloat16),
            jax.ShapeDtypeStruct((LANE_BITS, tiles, LANES // 2), jnp.float32),
            jax.ShapeDtypeStruct((high, tiles // 2, LANES), jnp.float32),
        ],
        cost_estimate=pl.CostEstimate(
            flops=8 * local * pieces * rows * width,
            bytes_accessed=4 * (local + 2) * pieces * rows * width,
            transcendentals=0,
        ),
        name="backward_local",
    )(me, grads, states, cos_table, sin_table, hot)


def cross_kernel(count, bits, *refs):
    grad_refs = refs[:count]
    field_refs = refs[count : 2 * count]
    cos_ref, sin_ref = refs[2 * count : 2 * count + 2]
    out_refs = refs[2 * count + 2 : 3 * count + 2]
    term_ref = refs[3 * count + 2]
    rows, width = out_refs[0].shape
    step = 8
    for tile in range(width // LANES):
        at = tile_at(tile)
        totals = [[None] * (count // 2) for _ in range(bits)]
        for number in range(rows // step):
            part = pl.ds(number * step, step)
            field = [ref[part, at].astype(jnp.float32) for ref in field_refs]
            levels = [field]
            for bit in range(bits - 1):
                field = list(levels[-1])
                for low in range(count):
                    if low & (1 << bit):
                        continue
                    high = low | (1 << bit)
                    pair = drop_bit(low, bit)
                    cosine = cos_ref[bit, pair : pair + 1, at]
                    sine = sin_ref[bit, pair : pair + 1, at]
                    v_low, v_high = field[low], field[high]
                    field[low] = cosine * v_low - sine * v_high
                    field[high] = sine * v_low + cosine * v_high
                levels.append(field)
            grad = [ref[part, at].astype(jnp.float32) for ref in grad_refs]
            for bit in reversed(range(bits)):
                before = levels[bit]
                for low in range(count):
                    if low & (1 << bit):
                        continue
                    high = low | (1 << bit)
                    pair = drop_bit(low, bit)
                    cosine = cos_ref[bit, pair : pair + 1, at]
                    sine = sin_ref[bit, pair : pair + 1, at]
                    g_low, g_high = grad[low], grad[high]
                    grad[low] = cosine * g_low + sine * g_high
                    grad[high] = cosine * g_high - sine * g_low
                    term = grad[high] * before[low] - grad[low] * before[high]
                    held = totals[bit][pair]
                    totals[bit][pair] = term if held is None else held + term
            for ref, value in zip(out_refs, grad):
                ref[part, at] = value.astype(ref.dtype)
        for bit in range(bits):
            for pair in range(count // 2):
                term_ref[bit, pair : pair + 1, at] = jnp.sum(
                    totals[bit][pair], axis=0, keepdims=True
                )


def cross_sections(grads, fields, cos_table, sin_table):
    count = len(grads)
    bits = cos_table.shape[0]
    rows, width = grads[0].shape
    block = min(width, 256)
    piece = pl.BlockSpec((rows, block), lambda i: (0, i))
    table = pl.BlockSpec((bits, count // 2, block), lambda i: (0, 0, i))
    outs = pl.pallas_call(
        functools.partial(cross_kernel, count, bits),
        grid=(width // block,),
        in_specs=[piece] * (2 * count) + [table] * 2,
        out_specs=[piece] * count + [table],
        out_shape=[jax.ShapeDtypeStruct((rows, width), jnp.float32)] * count
        + [jax.ShapeDtypeStruct(cos_table.shape, jnp.float32)],
        cost_estimate=pl.CostEstimate(
            flops=12 * bits * count * rows * width,
            bytes_accessed=12 * count * rows * width,
            transcendentals=0,
        ),
        name="cross_sections",
    )(*grads, *fields, cos_table, sin_table)
    return outs[:count], outs[count]


def unpack_mask(words, rows, width):
    shifts = jnp.arange(16, dtype=jnp.int32)
    bits = jnp.bitwise_and(jnp.right_shift(words[:, None, :], shifts[None, :, None]), 1)
    return bits.reshape(rows, width).astype(jnp.float32)


def exchange(pieces, axis):
    return [pieces[0]] + [swap(pieces[m], axis, m) for m in range(1, len(pieces))]


def tree_sum(parts):
    while len(parts) > 1:
        parts = [parts[k] + parts[k + 1] for k in range(0, len(parts), 2)]
    return parts[0]


def body(activations, angles, clip_bits, codes, exponents, cotangent):
    rows, width = activations.shape
    sections, share = angles.shape
    groups = lax.axis_size("dp")
    count = lax.axis_size("tensor")
    ways = count // groups
    columns = codes.shape[1]
    part = columns // ways
    local = width.bit_length() - 1
    cross = sections - local
    me = lax.axis_index("tensor")
    mine = lax.axis_index("dp")
    level = me // ways
    core = me % ways

    blocks = jnp.stack(
        [cotangent] + [swap(cotangent, "tensor", m * ways) for m in range(1, groups)]
    )
    chosen = [pick(blocks, level ^ mine ^ m) for m in range(groups)]
    arrived = [chosen[0]] + [swap(chosen[m], "dp", m) for m in range(1, groups)]
    full = [
        jnp.concatenate([x] + [swap(x, "tensor", m) for m in range(1, ways)], axis=1)
        for x in arrived
    ]

    scale = jnp.exp2(exponents.astype(jnp.float32))
    weights = []
    for m in range(ways):
        at = (core ^ m) * part
        piece = lax.dynamic_slice_in_dim(codes, at, part, 1).astype(jnp.float32)
        factor = lax.dynamic_slice_in_dim(scale, mine * columns + at, part, 0)
        weights.append((piece * factor[None, :]).astype(jnp.bfloat16))
    weight = lax.optimization_barrier(jnp.concatenate(weights, axis=1))

    cosine = jnp.cos(angles)
    sine = jnp.sin(angles)
    cos_table, sin_table = local_tables(cosine[:local], sine[:local], width)
    states, last = forward_local(activations, cos_table, sin_table)

    order = me ^ jnp.arange(count, dtype=jnp.int32)
    trig = jnp.stack([cosine[local:], sine[local:]])
    around = jnp.stack([trig] + [swap(trig, "tensor", m) for m in range(1, count)])
    around = jnp.take(around, order, axis=0)
    around = jnp.moveaxis(around, 0, 2).reshape(2, cross, count // 2, width)
    jj = jnp.arange(count // 2, dtype=jnp.int32)
    cross_cos, cross_sin, flips = [], [], []
    for bit in range(cross):
        pair = drop_bit(me, bit) ^ jj
        flip = (1 - 2 * ((me >> bit) & 1)).astype(jnp.float32)
        flips.append(flip)
        cross_cos.append(jnp.take(around[0, bit], pair, axis=0))
        cross_sin.append(jnp.take(around[1, bit], pair, axis=0) * flip)
    cross_cos = jnp.stack(cross_cos)
    cross_sin = jnp.stack(cross_sin)

    last = last.reshape(count, rows // count, width)
    fields = exchange([pick(last, me ^ m) for m in range(count)], "tensor")

    products = [
        lax.dot_general(
            x, weight, (((1,), (1,)), ((), ())), preferred_element_type=jnp.float32
        )
        for x in full
    ]
    sent = [swap(products[m].astype(jnp.bfloat16), "dp", m) for m in range(1, groups)]
    total = products[0]
    for x in sent:
        total = total + x.astype(jnp.float32)
    grad = total * unpack_mask(clip_bits, rows, width)

    grad = grad.reshape(count, rows // count, width)
    grads = exchange([pick(grad, me ^ m) for m in range(count)], "tensor")
    grads, cross_terms = cross_sections(grads, fields, cross_cos, cross_sin)
    grads = jnp.stack(exchange(list(grads), "tensor"))

    natural = []
    for bit in range(cross):
        pair = drop_bit(me, bit) ^ jj
        natural.append(jnp.take(cross_terms[bit], pair, axis=0) * flips[bit])
    natural = jnp.stack(natural).reshape(cross, count, share)
    natural = jnp.moveaxis(natural, 1, 0)
    owned = tree_sum(exchange([pick(natural, me ^ m) for m in range(count)], "tensor"))

    input_grad, lane_terms, tile_terms = backward_local(
        me.reshape(1), grads, states, cos_table, sin_table
    )
    terms = jnp.concatenate(
        [
            lane_terms.reshape(LANE_BITS, share),
            tile_terms.reshape(local - LANE_BITS, share),
            owned,
        ],
        axis=0,
    )
    angle_grad = tree_sum([terms] + [swap(terms, "dp", m) for m in range(1, groups)])
    return (input_grad, angle_grad)


def solution(mesh):
    placed = (
        P("dp", "tensor"),
        P(None, "tensor"),
        P("dp", "tensor"),
        P("tensor", "dp"),
        P(),
        P("dp", "tensor"),
    )
    return jax.shard_map(
        body,
        mesh=mesh,
        in_specs=placed,
        out_specs=(P("dp", "tensor"), P(None, "tensor")),
        check_vma=False,
    )
```

```python
import functools

import jax
import jax.numpy as jnp
from jax import lax
from jax.experimental import pallas as pl
from jax.experimental.pallas import tpu as pltpu
from jax.sharding import PartitionSpec as P

LANES = 128
LANE_BITS = 7
HIGH = lax.Precision.HIGHEST


CHUNKS = 2
STEP = 16
FRACTION = 14.0


def swap(value, axis, mask):
    pairs = [(source, source ^ mask) for source in range(lax.axis_size(axis))]
    return lax.ppermute(value, axis, pairs)


def pick(stacked, index):
    return lax.dynamic_index_in_dim(stacked, index, 0, keepdims=False)


def drop_bit(index, bit):
    return ((index >> (bit + 1)) << bit) | (index & ((1 << bit) - 1))


def lane_selectors(sections):
    lane = jnp.arange(LANES, dtype=jnp.int32)
    rows = []
    signs = []
    for section in range(sections):
        pair = drop_bit(lane, section)
        hot = pair[None, :] == jnp.arange(LANES // 2, dtype=jnp.int32)[:, None]
        rows.append(hot.astype(jnp.float32))
        signs.append(jnp.where((lane >> section) & 1 == 0, -1.0, 1.0).astype(jnp.float32))
    return jnp.stack(rows), jnp.stack(signs)


def local_tables(cosine, sine, width):
    local = cosine.shape[0]
    tiles = width // LANES
    hot, signs = lane_selectors(LANE_BITS)

    def lanes(values):
        shaped = values[:LANE_BITS].reshape(LANE_BITS, tiles, LANES // 2)
        return jnp.einsum("stk,skl->stl", shaped, hot, precision=HIGH)

    def whole(section, values, sign):
        step = 1 << (section - LANE_BITS)
        shaped = values.reshape(tiles // (2 * step), 1, step, LANES)
        return jnp.concatenate([sign * shaped, shaped], axis=1).reshape(1, tiles, LANES)

    cos_rows = [lanes(cosine)]
    sin_rows = [lanes(sine) * signs[:, None, :]]
    for section in range(LANE_BITS, local):
        cos_rows.append(whole(section, cosine[section], 1.0))
        sin_rows.append(whole(section, sine[section], -1.0))
    cos_table = jnp.concatenate(cos_rows, axis=0).reshape(local, width)
    sin_table = jnp.concatenate(sin_rows, axis=0).reshape(local, width)
    return cos_table, sin_table


def lane_partner(value, section):
    half = 1 << section
    lane = lax.broadcasted_iota(jnp.int32, value.shape, 1)
    up = pltpu.roll(value, half, 1)
    if 2 * half == LANES:
        return up
    down = pltpu.roll(value, LANES - half, 1)
    return jnp.where((lane & half) == 0, down, up)


def tile_at(tile):
    return pl.ds(tile * LANES, LANES)


def encode(values, store):
    most = functools.reduce(jnp.maximum, [jnp.abs(value) for value in values])
    most = jnp.max(most, axis=1, keepdims=True)
    power = jnp.ceil(jnp.log2(jnp.maximum(most, 1e-30)))
    factor = jnp.exp2(FRACTION - power)
    for tile, value in enumerate(values):
        store(tile, jnp.round(value * factor).astype(jnp.int32).astype(jnp.int16))
    power = jnp.broadcast_to(power, values[0].shape)
    store(len(values), power.astype(jnp.int32).astype(jnp.int16))


def widen(codes):
    return codes.astype(jnp.int32).astype(jnp.float32)


def scale_of(ref, at, width):
    return jnp.exp2(widen(ref[at, pl.ds(width, LANES)]) - FRACTION)


def weight_kernel(place_ref, codes_ref, scale_ref, out_ref):
    out_ref[...] = (codes_ref[...].astype(jnp.float32) * scale_ref[0]).astype(out_ref.dtype)


def scaled_weight(place, codes, scale, ways):
    width, columns = codes.shape
    part = columns // ways
    block = min(width, 512)
    return pl.pallas_call(
        weight_kernel,
        grid_spec=pltpu.PrefetchScalarGridSpec(
            num_scalar_prefetch=1,
            grid=(width // block, ways),
            in_specs=[
                pl.BlockSpec((block, part), lambda i, j, p: (i, p[0] ^ j)),
                pl.BlockSpec((1, 1, part), lambda i, j, p: (p[1] + (p[0] ^ j), 0, 0)),
            ],
            out_specs=pl.BlockSpec((block, part), lambda i, j, p: (i, j)),
        ),
        out_shape=jax.ShapeDtypeStruct((width, columns), jnp.bfloat16),
        cost_estimate=pl.CostEstimate(
            flops=width * columns, bytes_accessed=4 * width * columns, transcendentals=0
        ),
        name="scaled_weight",
    )(place, codes, scale.reshape(-1, 1, part))


def forward_kernel(local, act_ref, cos_ref, sin_ref, states_ref, code_ref):
    rows, width = act_ref.shape
    tiles = width // LANES

    def block(index, carry):
        at = pl.ds(pl.multiple_of(index * STEP, STEP), STEP)
        field = []
        for tile in range(tiles):
            value = act_ref[at, tile_at(tile)].astype(jnp.float32)
            for section in range(LANE_BITS):
                other = lane_partner(value, section)
                cosine = cos_ref[section : section + 1, tile_at(tile)]
                signed = sin_ref[section : section + 1, tile_at(tile)]
                value = cosine * value + signed * other
                states_ref[section, at, tile_at(tile)] = value
            field.append(value)
        for section in range(LANE_BITS, local):
            gap = 1 << (section - LANE_BITS)
            for tile in range(tiles):
                if tile & gap:
                    continue
                cosine = cos_ref[section : section + 1, tile_at(tile)]
                signed = sin_ref[section : section + 1, tile_at(tile)]
                low, high = field[tile], field[tile + gap]
                field[tile] = cosine * low + signed * high
                field[tile + gap] = cosine * high - signed * low
            for tile in range(tiles):
                states_ref[section, at, tile_at(tile)] = field[tile]

        def store(tile, codes):
            code_ref[at, tile_at(tile)] = codes

        encode(field, store)
        return carry

    lax.fori_loop(0, rows // STEP, block, 0)


def forward_local(acts, cos_table, sin_table):
    rows, width = acts.shape
    local = cos_table.shape[0]
    block = min(rows, 32)
    table = pl.BlockSpec((local, width), lambda i: (0, 0))
    return pl.pallas_call(
        functools.partial(forward_kernel, local),
        grid=(rows // block,),
        in_specs=[pl.BlockSpec((block, width), lambda i: (i, 0)), table, table],
        out_specs=[
            pl.BlockSpec((local, block, width), lambda i: (0, i, 0)),
            pl.BlockSpec((block, width + LANES), lambda i: (i, 0)),
        ],
        out_shape=[
            jax.ShapeDtypeStruct((local, rows, width), jnp.float32),
            jax.ShapeDtypeStruct((rows, width + LANES), jnp.int16),
        ],
        cost_estimate=pl.CostEstimate(
            flops=6 * local * rows * width,
            bytes_accessed=4 * (local + 1) * rows * width,
            transcendentals=0,
        ),
        name="forward_local",
    )(acts, cos_table, sin_table)


def core_kernel(place_ref, state_ref, other_ref, trig_ref, pair_ref, *code_refs):
    rows, width = other_ref.shape[0], state_ref.shape[2]
    count = len(code_refs)
    pieces, depth = state_ref.shape[0], state_ref.shape[1]
    tiles = width // LANES
    half = width // 2
    place = place_ref[0]
    start = place_ref[1] * half
    cosine_at = lambda at: trig_ref[0:1, at]
    signed_at = lambda at: trig_ref[1:2, at]
    scales = []
    for piece in range(count):
        source = place ^ piece
        mine = state_ref.at[source]
        other = other_ref.at[source]
        at = pl.ds(0, depth)
        scale = scale_of(other, at, width)
        field = []
        for tile in range(tiles):
            lanes = tile_at(tile)
            value = mine[at, lanes]
            partner = widen(other[at, lanes]) * scale
            field.append(cosine_at(lanes) * value + signed_at(lanes) * partner)

        def store(tile, codes):
            code_refs[piece][at, tile_at(tile)] = codes

        encode(field, store)
        for tile in range(tiles // 2):
            lanes = pl.ds(pl.multiple_of(start + tile * LANES, LANES), LANES)
            value = mine[at, lanes]
            partner = widen(other[at, lanes]) * scale
            cosine, signed = cosine_at(lanes), signed_at(lanes)
            pair_ref[0, source, at, tile_at(tile)] = cosine * value + signed * partner
            pair_ref[1, source, at, tile_at(tile)] = cosine * partner - signed * value


def core_forward(place, state, other, trig, count, chunks):
    rows, width = state.shape
    depth = rows // (chunks * count)
    view = state.reshape(chunks, count, depth, width)
    codes = other.reshape(chunks, count, depth, width + LANES)
    per = depth // STEP
    outs = pl.pallas_call(
        core_kernel,
        grid_spec=pltpu.PrefetchScalarGridSpec(
            num_scalar_prefetch=1,
            grid=(chunks, per),
            in_specs=[
                pl.BlockSpec((None, count, STEP, width), lambda i, j, p: (i, 0, j, 0)),
                pl.BlockSpec((None, count, STEP, width + LANES), lambda i, j, p: (i, 0, j, 0)),
                pl.BlockSpec((2, width), lambda i, j, p: (0, 0)),
            ],
            out_specs=[
                pl.BlockSpec((2, None, count, STEP, width // 2), lambda i, j, p: (0, i, 0, j, 0))
            ]
            + [pl.BlockSpec((STEP, width + LANES), lambda i, j, p: (i * per + j, 0))] * count,
        ),
        out_shape=[jax.ShapeDtypeStruct((2, chunks, count, depth, width // 2), jnp.float32)]
        + [jax.ShapeDtypeStruct((chunks * depth, width + LANES), jnp.int16)] * count,
        cost_estimate=pl.CostEstimate(
            flops=10 * rows * width, bytes_accessed=12 * rows * width, transcendentals=0
        ),
        name="core_forward",
    )(place, view, codes, trig)
    return outs[0].reshape(2, rows, width // 2), outs[1:]


def gather_kernel(count, place_ref, *refs):
    code_refs = refs[-count:]
    first_ref = refs[0]
    part_refs = refs[1 : -count - 1]
    words_ref = refs[-count - 1]
    width = first_ref.shape[2]
    place = place_ref[0]
    token = lax.broadcasted_iota(jnp.int32, (STEP, LANES), 0)
    for piece in range(count):
        source = place ^ piece
        values = []
        for tile in range(width // LANES):
            lanes = tile_at(tile)
            value = first_ref[source, :, lanes]
            for ref in part_refs:
                value = value + ref[source, :, lanes].astype(jnp.float32)
            words = words_ref[source, 0, :, lanes]
            bits = jnp.bitwise_and(jnp.right_shift(jnp.broadcast_to(words, token.shape), token), 1)
            values.append(value * bits.astype(jnp.float32))

        def store(tile, codes):
            code_refs[piece][:, tile_at(tile)] = codes

        encode(values, store)


def gather_parts(place, parts, words, count):
    rows, width = parts[0].shape
    depth = rows // count
    piece = pl.BlockSpec((count, STEP, width), lambda i, p: (0, i, 0))
    return pl.pallas_call(
        functools.partial(gather_kernel, count),
        grid_spec=pltpu.PrefetchScalarGridSpec(
            num_scalar_prefetch=1,
            grid=(depth // STEP,),
            in_specs=[piece] * len(parts)
            + [pl.BlockSpec((count, 1, 1, width), lambda i, p: (0, i, 0, 0))],
            out_specs=[pl.BlockSpec((STEP, width + LANES), lambda i, p: (i, 0))] * count,
        ),
        out_shape=[jax.ShapeDtypeStruct((depth, width + LANES), jnp.int16)] * count,
        cost_estimate=pl.CostEstimate(
            flops=12 * rows * width, bytes_accessed=12 * rows * width, transcendentals=0
        ),
        name="gather_parts",
    )(
        place,
        *[part.reshape(count, depth, width) for part in parts],
        words.reshape(count, depth // STEP, 1, width),
    )


def cross_kernel(count, bits, *refs):
    grad_refs = refs[:count]
    field_refs = refs[count : 2 * count]
    cos_ref, sin_ref = refs[2 * count : 2 * count + 2]
    out_refs = refs[2 * count + 2 : 3 * count + 2]
    term_ref, held_ref, sum_ref = refs[3 * count + 2 :]
    width = cos_ref.shape[2]
    tiles = width // LANES
    rows = pl.ds(0, STEP)
    index = pl.program_id(0)

    @pl.when(index == 0)
    def _():
        sum_ref[...] = jnp.zeros_like(sum_ref)

    grad_scales = [scale_of(ref, rows, width) for ref in grad_refs]
    field_scales = [scale_of(ref, rows, width) for ref in field_refs]
    for tile in range(tiles):
        lanes = tile_at(tile)
        levels = [[widen(r[rows, lanes]) * s for r, s in zip(field_refs, field_scales)]]
        for bit in range(bits - 1):
            field = list(levels[-1])
            for low in range(count):
                if low & (1 << bit):
                    continue
                high = low | (1 << bit)
                pair = drop_bit(low, bit)
                cosine = cos_ref[bit, pair : pair + 1, lanes]
                sine = sin_ref[bit, pair : pair + 1, lanes]
                v_low, v_high = field[low], field[high]
                field[low] = cosine * v_low - sine * v_high
                field[high] = sine * v_low + cosine * v_high
            levels.append(field)
        grad = [widen(r[rows, lanes]) * s for r, s in zip(grad_refs, grad_scales)]
        for bit in reversed(range(bits)):
            before = levels[bit]
            for low in range(count):
                if low & (1 << bit):
                    continue
                high = low | (1 << bit)
                pair = drop_bit(low, bit)
                cosine = cos_ref[bit, pair : pair + 1, lanes]
                sine = sin_ref[bit, pair : pair + 1, lanes]
                g_low, g_high = grad[low], grad[high]
                grad[low] = cosine * g_low + sine * g_high
                grad[high] = cosine * g_high - sine * g_low
                term = grad[high] * before[low] - grad[low] * before[high]
                sum_ref[bit, pair, :, lanes] += jnp.sum(term.reshape(STEP // 8, 8, LANES), axis=0)
        for piece in range(count):
            held_ref[piece, :, lanes] = grad[piece]

    for piece in range(count):

        def store(tile, codes):
            out_refs[piece][:, tile_at(tile)] = codes

        encode([held_ref[piece, :, tile_at(tile)] for tile in range(tiles)], store)

    @pl.when(index == pl.num_programs(0) - 1)
    def _():
        term_ref[...] = jnp.sum(sum_ref[...], axis=2)


def cross_sections(grads, fields, cos_table, sin_table, offset):
    count = len(grads)
    bits, pairs, width = cos_table.shape
    rows, wide = grads[0].shape
    piece = pl.BlockSpec((STEP, wide), lambda i: (i, 0))
    moved = pl.BlockSpec((STEP, wide), lambda i: (i + offset * (rows // STEP), 0))
    table = pl.BlockSpec(cos_table.shape, lambda i: (0, 0, 0))
    outs = pl.pallas_call(
        functools.partial(cross_kernel, count, bits),
        grid=(rows // STEP,),
        in_specs=[piece] * count + [moved] * count + [table] * 2,
        out_specs=[piece] * count + [table],
        out_shape=[jax.ShapeDtypeStruct((rows, wide), jnp.int16)] * count
        + [jax.ShapeDtypeStruct(cos_table.shape, jnp.float32)],
        scratch_shapes=[
            pltpu.VMEM((count, STEP, width), jnp.float32),
            pltpu.VMEM((bits, pairs, 8, width), jnp.float32),
        ],
        cost_estimate=pl.CostEstimate(
            flops=20 * bits * count * rows * width,
            bytes_accessed=6 * count * rows * width,
            transcendentals=0,
        ),
        name="cross_sections",
    )(*grads, *fields, cos_table, sin_table)
    return outs[:count], outs[count]


def backward_kernel(
    local, place_ref, grad_ref, other_ref, states_ref, pair_ref, trig_ref, cos_ref, sin_ref,
    hot_ref, lane_in, tile_in, core_in, whole_ref,
    out_ref, lane_out, tile_out, core_out, lane_sum, tile_sum, core_sum,
):
    rows, width = out_ref.shape
    tiles = width // LANES
    half = width // 2
    index = pl.program_id(0)
    start = place_ref[1] * half

    @pl.when(index == 0)
    def _():
        lane_sum[...] = jnp.zeros_like(lane_sum)
        tile_sum[...] = jnp.zeros_like(tile_sum)
        core_sum[...] = jnp.zeros_like(core_sum)

    def folded(value):
        return jnp.sum(value.reshape(STEP // 8, 8, LANES), axis=0)

    def block(number, carry):
        at = pl.ds(pl.multiple_of(number * STEP, STEP), STEP)
        scale = scale_of(grad_ref, at, width)
        other_scale = scale_of(other_ref, at, width)
        for tile in range(tiles // 2):
            lanes = pl.ds(pl.multiple_of(start + tile * LANES, LANES), LANES)
            mine = widen(grad_ref[at, lanes]) * scale
            partner = widen(other_ref[at, lanes]) * other_scale
            term = partner * pair_ref[0, at, tile_at(tile)] - mine * pair_ref[1, at, tile_at(tile)]
            core_sum[tile] += folded(term)
        grad = []
        for tile in range(tiles):
            lanes = tile_at(tile)
            mine = widen(grad_ref[at, lanes]) * scale
            partner = widen(other_ref[at, lanes]) * other_scale
            grad.append(trig_ref[0:1, lanes] * mine - trig_ref[1:2, lanes] * partner)
        for section in reversed(range(LANE_BITS, local)):
            gap = 1 << (section - LANE_BITS)
            for tile in range(tiles):
                if tile & gap:
                    continue
                cosine = cos_ref[section : section + 1, tile_at(tile)]
                signed = sin_ref[section : section + 1, tile_at(tile)]
                low, high = grad[tile], grad[tile + gap]
                before_low = states_ref[section, at, tile_at(tile)]
                before_high = states_ref[section, at, tile_at(tile + gap)]
                term = folded(high * before_low - low * before_high)
                place = drop_bit(tile, section - LANE_BITS)
                tile_sum[section - LANE_BITS, place] += term
                grad[tile] = cosine * low - signed * high
                grad[tile + gap] = cosine * high + signed * low
        for tile in range(tiles):
            value = grad[tile]
            for section in reversed(range(LANE_BITS)):
                cosine = cos_ref[section : section + 1, tile_at(tile)]
                signed = sin_ref[section : section + 1, tile_at(tile)]
                other = lane_partner(value, section)
                state = states_ref[section, at, tile_at(tile)]
                lane_sum[section, tile] += folded(other * state)
                value = cosine * value - signed * other
            out_ref[at, tile_at(tile)] = value.astype(out_ref.dtype)
        return carry

    lax.fori_loop(0, rows // STEP, block, 0)

    @pl.when(index == pl.num_programs(0) - 1)
    def _():
        for section in range(LANE_BITS):
            summed = jnp.sum(lane_sum[section], axis=1)
            lane_out[section] = lane_in[section] + lax.dot_general(
                summed,
                hot_ref[section],
                (((1,), (1,)), ((), ())),
                precision=HIGH,
                preferred_element_type=jnp.float32,
            )
        for section in range(local - LANE_BITS):
            tile_out[section] = tile_in[section] + jnp.sum(tile_sum[section], axis=1)
        core_out[...] = core_in[...] + jnp.sum(core_sum[...], axis=1)


def backward_local(
    place, grad, other, states, pair, trig, cos_table, sin_table, hot, sums, whole, chunk, piece,
    count,
):
    depth = grad.shape[0]
    local, rows, width = states.shape
    tiles = width // LANES
    high = local - LANE_BITS
    base = chunk * count
    block = min(depth, 32)
    per = depth // block
    fixed = lambda shape: pl.BlockSpec(shape, lambda i, p: (0,) * len(shape))
    row_of = lambda i, p: (base + (p[0] ^ piece)) * per + i
    shapes = [(LANE_BITS, tiles, LANES // 2), (high, tiles // 2, LANES), (tiles // 2, LANES)]
    return pl.pallas_call(
        functools.partial(backward_kernel, local),
        grid_spec=pltpu.PrefetchScalarGridSpec(
            num_scalar_prefetch=1,
            grid=(per,),
            in_specs=[
                pl.BlockSpec((block, width + LANES), lambda i, p: (i, 0)),
                pl.BlockSpec((block, width + LANES), lambda i, p: (i, 0)),
                pl.BlockSpec((local, block, width), lambda i, p: (0, row_of(i, p), 0)),
                pl.BlockSpec((2, block, width // 2), lambda i, p: (0, row_of(i, p), 0)),
                fixed((2, width)),
                fixed((local, width)),
                fixed((local, width)),
                fixed(hot.shape),
            ]
            + [fixed(shape) for shape in shapes]
            + [pl.BlockSpec(memory_space=pl.ANY)],
            out_specs=[pl.BlockSpec((block, width), lambda i, p: (row_of(i, p), 0))]
            + [fixed(shape) for shape in shapes],
            scratch_shapes=[
                pltpu.VMEM((LANE_BITS, tiles, 8, LANES), jnp.float32),
                pltpu.VMEM((high, tiles // 2, 8, LANES), jnp.float32),
                pltpu.VMEM((tiles // 2, 8, LANES), jnp.float32),
            ],
        ),
        out_shape=[jax.ShapeDtypeStruct((rows, width), jnp.bfloat16)]
        + [jax.ShapeDtypeStruct(shape, jnp.float32) for shape in shapes],
        input_output_aliases={12: 0},
        cost_estimate=pl.CostEstimate(
            flops=8 * local * depth * width,
            bytes_accessed=4 * (local + 2) * depth * width,
            transcendentals=0,
        ),
        name="backward_local",
    )(place, grad, other, states, pair, trig, cos_table, sin_table, hot, *sums, whole)


def tree_sum(parts):
    while len(parts) > 1:
        parts = [parts[k] + parts[k + 1] for k in range(0, len(parts), 2)]
    return parts[0]


def gather_shares(value, me, bits):
    for bit in range(bits):
        other = swap(value, "tensor", 1 << bit)
        first = ((me >> bit) & 1) == 0
        value = jnp.concatenate(
            [jnp.where(first, value, other), jnp.where(first, other, value)], axis=0
        )
    return value


def scatter_shares(value, me, bits):
    for bit in reversed(range(bits)):
        halves = value.reshape((2, -1) + value.shape[1:])
        own = (me >> bit) & 1
        value = pick(halves, own) + swap(pick(halves, 1 - own), "tensor", 1 << bit)
    return value[0]


def body(activations, angles, clip_bits, codes, exponents, cotangent):
    rows, width = activations.shape
    sections, share = angles.shape
    groups = lax.axis_size("dp")
    devices = lax.axis_size("tensor")
    ways = devices // groups
    columns = codes.shape[1]
    local = width.bit_length() - 1
    cross = sections - local
    count = devices // 2
    me = lax.axis_index("tensor")
    mine = lax.axis_index("dp")
    level = me // ways
    core = me & 1
    line = me >> 1
    chunks = CHUNKS
    while rows // (chunks * count) < STEP:
        chunks //= 2
    chunk_rows = rows // chunks
    place = jnp.stack([line, core])

    full = []
    for q in range(chunks):
        own = cotangent[q * chunk_rows : (q + 1) * chunk_rows]
        blocks = jnp.stack([own] + [swap(own, "tensor", m * ways) for m in range(1, groups)])
        arrived = [
            swap(pick(blocks, level ^ mine ^ m), "dp", m) for m in range(1, groups)
        ]
        arrived = [pick(blocks, level ^ mine)] + arrived
        full.append(
            [
                jnp.concatenate([x] + [swap(x, "tensor", m) for m in range(1, ways)], axis=1)
                for x in arrived
            ]
        )

    scale = jnp.exp2(exponents.astype(jnp.float32))
    weight = scaled_weight(
        jnp.stack([me % ways, mine * ways]), codes, scale, ways
    )

    cosine = jnp.cos(angles)
    sine = jnp.sin(angles)
    cos_table, sin_table = local_tables(cosine[:local], sine[:local], width)
    states, last_codes = forward_local(activations, cos_table, sin_table)

    trig = jnp.stack([cosine[local:], sine[local:]])[None]
    trig = gather_shares(trig, me, cross)
    trig = jnp.moveaxis(trig, 0, 2).reshape(2, cross, devices // 2, width)
    flip = (1 - 2 * core).astype(jnp.float32)
    core_trig = pick(jnp.moveaxis(trig[:, 0], 1, 0), line)
    core_trig = core_trig * jnp.stack([jnp.float32(1), -flip])[:, None]
    jj = jnp.arange(count // 2, dtype=jnp.int32)
    cross_cos, cross_sin, flips = [], [], []
    for bit in range(cross - 1):
        pair = (drop_bit(line, bit) ^ jj) * 2 + core
        flips.append((1 - 2 * ((line >> bit) & 1)).astype(jnp.float32))
        cross_cos.append(jnp.take(trig[0, bit + 1], pair, axis=0))
        cross_sin.append(jnp.take(trig[1, bit + 1], pair, axis=0) * flips[-1])
    cross_cos = jnp.stack(cross_cos)
    cross_sin = jnp.stack(cross_sin)

    pair_states, fields = core_forward(
        place, states[local - 1], swap(last_codes, "tensor", 1), core_trig, count, chunks
    )
    fields = [fields[0]] + [swap(fields[m], "tensor", 2 * m) for m in range(1, count)]

    hot, signs = lane_selectors(LANE_BITS)
    hot = -hot * signs[:, None, :]
    tiles = width // LANES
    sums = [
        jnp.zeros((LANE_BITS, tiles, LANES // 2), jnp.float32),
        jnp.zeros((local - LANE_BITS, tiles // 2, LANES), jnp.float32),
        jnp.zeros((tiles // 2, LANES), jnp.float32),
    ]
    whole = jnp.zeros((rows, width), jnp.bfloat16)
    cross_terms = []
    backs = []
    word_rows = chunk_rows // 16
    for q in range(chunks):
        products = [
            lax.dot_general(
                x, weight, (((1,), (1,)), ((), ())), preferred_element_type=jnp.float32
            )
            for x in full[q]
        ]
        parts = [products[0]] + [
            swap(products[m].astype(jnp.bfloat16), "dp", m) for m in range(1, groups)
        ]
        words = clip_bits[q * word_rows : (q + 1) * word_rows]
        grads = gather_parts(place, parts, words, count)
        grads = [grads[0]] + [swap(grads[m], "tensor", 2 * m) for m in range(1, count)]
        grads, terms = cross_sections(grads, fields, cross_cos, cross_sin, q)
        cross_terms.append(terms)
        backs.append([grads[0]] + [swap(grads[m], "tensor", 2 * m) for m in range(1, count)])

    for q in range(chunks):
        for m in range(count):
            grad = backs[q][m]
            outs = backward_local(
                place, grad, swap(grad, "tensor", 1), states, pair_states, core_trig,
                cos_table, sin_table, hot, sums, whole, q, m, count,
            )
            whole, sums = outs[0], outs[1:]

    terms = functools.reduce(jnp.add, cross_terms)
    natural = jnp.stack(
        [
            jnp.take(terms[bit], drop_bit(line, bit) ^ jj, axis=0) * flips[bit]
            for bit in range(cross - 1)
        ]
    )
    natural = natural.reshape(cross - 1, count // 2, 1, 2, share)
    natural = jnp.where(
        jnp.arange(2, dtype=jnp.int32)[None, None, :, None, None] == core, natural, 0.0
    )
    natural = jnp.moveaxis(natural.reshape(cross - 1, devices, share), 1, 0)
    owned = scatter_shares(natural, me, cross)

    final = jnp.concatenate(
        [
            sums[0].reshape(LANE_BITS, share),
            sums[1].reshape(local - LANE_BITS, share),
            sums[2].reshape(1, share) * flip,
            owned,
        ],
        axis=0,
    )
    angle_grad = tree_sum([final] + [swap(final, "dp", m) for m in range(1, groups)])
    return (whole, angle_grad)


def solution(mesh):
    placed = (
        P("dp", "tensor"),
        P(None, "tensor"),
        P("dp", "tensor"),
        P("tensor", "dp"),
        P(),
        P("dp", "tensor"),
    )
    return jax.shard_map(
        body,
        mesh=mesh,
        in_specs=placed,
        out_specs=(P("dp", "tensor"), P(None, "tensor")),
        check_vma=False,
    )
```

```python
import functools

import jax
import jax.numpy as jnp
from jax import lax
from jax.experimental import pallas as pl
from jax.experimental.pallas import tpu as pltpu
from jax.sharding import PartitionSpec as P


LANES = 128
LANE_BITS = 7
HIGH = lax.Precision.HIGHEST


CHUNKS = 2
STEP = 16
FRACTION = 14.0


def swap(value, axis, mask):
    pairs = [(source, source ^ mask) for source in range(lax.axis_size(axis))]
    return lax.ppermute(value, axis, pairs)


def pick(stacked, index):
    return lax.dynamic_index_in_dim(stacked, index, 0, keepdims=False)


def drop_bit(index, bit):
    return ((index >> (bit + 1)) << bit) | (index & ((1 << bit) - 1))


def lane_selectors(sections):
    lane = jnp.arange(LANES, dtype=jnp.int32)
    rows = []
    signs = []
    for section in range(sections):
        pair = drop_bit(lane, section)
        hot = pair[None, :] == jnp.arange(LANES // 2, dtype=jnp.int32)[:, None]
        rows.append(hot.astype(jnp.float32))
        signs.append(jnp.where((lane >> section) & 1 == 0, -1.0, 1.0).astype(jnp.float32))
    return jnp.stack(rows), jnp.stack(signs)


def local_tables(cosine, sine, width):
    local = cosine.shape[0]
    tiles = width // LANES
    hot, signs = lane_selectors(LANE_BITS)

    def lanes(values):
        shaped = values[:LANE_BITS].reshape(LANE_BITS, tiles, LANES // 2)
        return jnp.einsum("stk,skl->stl", shaped, hot, precision=HIGH)

    def whole(section, values, sign):
        step = 1 << (section - LANE_BITS)
        shaped = values.reshape(tiles // (2 * step), 1, step, LANES)
        return jnp.concatenate([sign * shaped, shaped], axis=1).reshape(1, tiles, LANES)

    cos_rows = [lanes(cosine)]
    sin_rows = [lanes(sine) * signs[:, None, :]]
    for section in range(LANE_BITS, local):
        cos_rows.append(whole(section, cosine[section], 1.0))
        sin_rows.append(whole(section, sine[section], -1.0))
    cos_table = jnp.concatenate(cos_rows, axis=0).reshape(local, width)
    sin_table = jnp.concatenate(sin_rows, axis=0).reshape(local, width)
    return cos_table, sin_table


def lane_partner(value, section):
    half = 1 << section
    lane = lax.broadcasted_iota(jnp.int32, value.shape, 1)
    up = pltpu.roll(value, half, 1)
    if 2 * half == LANES:
        return up
    down = pltpu.roll(value, LANES - half, 1)
    return jnp.where((lane & half) == 0, down, up)


def tile_at(tile):
    return pl.ds(tile * LANES, LANES)


def encode(values, store):
    most = functools.reduce(jnp.maximum, [jnp.abs(value) for value in values])
    most = jnp.max(most, axis=1, keepdims=True)
    power = jnp.ceil(jnp.log2(jnp.maximum(most, 1e-30)))
    factor = jnp.exp2(FRACTION - power)
    for tile, value in enumerate(values):
        store(tile, jnp.round(value * factor).astype(jnp.int32).astype(jnp.int16))
    power = jnp.broadcast_to(power, values[0].shape)
    store(len(values), power.astype(jnp.int32).astype(jnp.int16))


def widen(codes):
    return codes.astype(jnp.int32).astype(jnp.float32)


def scale_of(ref, at, width):
    return jnp.exp2(widen(ref[at, pl.ds(width, LANES)]) - FRACTION)


def product_kernel(ways, place_ref, *refs):
    token_refs = refs[:ways]
    code_refs = refs[ways : 2 * ways]
    scale_refs = refs[2 * ways : 3 * ways]
    out_refs = refs[3 * ways :]
    total = None
    for tokens, codes, scale in zip(token_refs, code_refs, scale_refs):
        weight = codes[...] * scale[0]
        part = lax.dot_general(
            tokens[...],
            weight,
            (((1,), (1,)), ((), ())),
            preferred_element_type=jnp.float32,
        )
        total = part if total is None else total + part
    rows = out_refs[0].shape[0]
    for index, ref in enumerate(out_refs):
        ref[...] = total[index * rows : (index + 1) * rows].astype(ref.dtype)


def product(place, tokens, codes, scale, outs, dtype):
    ways = len(tokens)
    width = codes.shape[0]
    rows, part = tokens[0].shape
    block = min(width, 256)
    code_spec = lambda j: pl.BlockSpec((block, part), lambda i, p: (i, p[0] ^ j))
    scale_spec = lambda j: pl.BlockSpec((1, 1, part), lambda i, p: (p[1] + (p[0] ^ j), 0, 0))
    return pl.pallas_call(
        functools.partial(product_kernel, ways),
        grid_spec=pltpu.PrefetchScalarGridSpec(
            num_scalar_prefetch=1,
            grid=(width // block,),
            in_specs=[pl.BlockSpec((rows, part), lambda i, p: (0, 0))] * ways
            + [code_spec(j) for j in range(ways)]
            + [scale_spec(j) for j in range(ways)],
            out_specs=[pl.BlockSpec((rows // outs, block), lambda i, p: (0, i))] * outs,
        ),
        out_shape=[jax.ShapeDtypeStruct((rows // outs, width), dtype)] * outs,
        cost_estimate=pl.CostEstimate(
            flops=2 * rows * part * ways * width,
            bytes_accessed=2 * part * ways * width,
            transcendentals=0,
        ),
        name="product",
    )(place, *tokens, *[codes] * ways, *[scale] * ways)


def forward_kernel(local, act_ref, cos_ref, sin_ref, states_ref, code_ref):
    rows, width = act_ref.shape
    tiles = width // LANES

    def block(index, carry):
        at = pl.ds(pl.multiple_of(index * STEP, STEP), STEP)
        field = []
        for tile in range(tiles):
            value = act_ref[at, tile_at(tile)].astype(jnp.float32)
            for section in range(LANE_BITS):
                other = lane_partner(value, section)
                cosine = cos_ref[section : section + 1, tile_at(tile)]
                signed = sin_ref[section : section + 1, tile_at(tile)]
                value = cosine * value + signed * other
                states_ref[section, at, tile_at(tile)] = value
            field.append(value)
        for section in range(LANE_BITS, local):
            gap = 1 << (section - LANE_BITS)
            for tile in range(tiles):
                if tile & gap:
                    continue
                cosine = cos_ref[section : section + 1, tile_at(tile)]
                signed = sin_ref[section : section + 1, tile_at(tile)]
                low, high = field[tile], field[tile + gap]
                field[tile] = cosine * low + signed * high
                field[tile + gap] = cosine * high - signed * low
            for tile in range(tiles):
                states_ref[section, at, tile_at(tile)] = field[tile]

        def store(tile, codes):
            code_ref[at, tile_at(tile)] = codes

        encode(field, store)
        return carry

    lax.fori_loop(0, rows // STEP, block, 0)


def forward_local(acts, cos_table, sin_table):
    rows, width = acts.shape
    local = cos_table.shape[0]
    block = min(rows, 32)
    table = pl.BlockSpec((local, width), lambda i: (0, 0))
    return pl.pallas_call(
        functools.partial(forward_kernel, local),
        grid=(rows // block,),
        in_specs=[pl.BlockSpec((block, width), lambda i: (i, 0)), table, table],
        out_specs=[
            pl.BlockSpec((local, block, width), lambda i: (0, i, 0)),
            pl.BlockSpec((block, width + LANES), lambda i: (i, 0)),
        ],
        out_shape=[
            jax.ShapeDtypeStruct((local, rows, width), jnp.float32),
            jax.ShapeDtypeStruct((rows, width + LANES), jnp.int16),
        ],
        cost_estimate=pl.CostEstimate(
            flops=6 * local * rows * width,
            bytes_accessed=4 * (local + 1) * rows * width,
            transcendentals=0,
        ),
        name="forward_local",
    )(acts, cos_table, sin_table)


def core_kernel(place_ref, state_ref, other_ref, trig_ref, pair_ref, *code_refs):
    width = state_ref.shape[2]
    count = len(code_refs)
    depth = state_ref.shape[1]
    tiles = width // LANES
    half = width // 2
    place = place_ref[0]
    start = place_ref[1] * half
    cosine_at = lambda at: trig_ref[0:1, at]
    signed_at = lambda at: trig_ref[1:2, at]
    for piece in range(count):
        source = place ^ piece
        mine = state_ref.at[source]
        other = other_ref.at[source]
        at = pl.ds(0, depth)
        scale = scale_of(other, at, width)
        field = []
        for tile in range(tiles):
            lanes = tile_at(tile)
            value = mine[at, lanes]
            partner = widen(other[at, lanes]) * scale
            field.append(cosine_at(lanes) * value + signed_at(lanes) * partner)

        def store(tile, codes):
            code_refs[piece][at, tile_at(tile)] = codes

        encode(field, store)
        for tile in range(tiles // 2):
            lanes = pl.ds(pl.multiple_of(start + tile * LANES, LANES), LANES)
            value = mine[at, lanes]
            partner = widen(other[at, lanes]) * scale
            cosine, signed = cosine_at(lanes), signed_at(lanes)
            pair_ref[0, source, at, tile_at(tile)] = cosine * value + signed * partner
            pair_ref[1, source, at, tile_at(tile)] = cosine * partner - signed * value


def core_forward(place, states, other, trig, count, chunks):
    local, rows, width = states.shape
    depth = rows // (chunks * count)
    view = states.reshape(local, chunks, count, depth, width)
    codes = other.reshape(chunks, count, depth, width + LANES)
    per = depth // STEP
    outs = pl.pallas_call(
        core_kernel,
        grid_spec=pltpu.PrefetchScalarGridSpec(
            num_scalar_prefetch=1,
            grid=(chunks, per),
            in_specs=[
                pl.BlockSpec(
                    (None, None, count, STEP, width), lambda i, j, p: (local - 1, i, 0, j, 0)
                ),
                pl.BlockSpec((None, count, STEP, width + LANES), lambda i, j, p: (i, 0, j, 0)),
                pl.BlockSpec((2, width), lambda i, j, p: (0, 0)),
            ],
            out_specs=[
                pl.BlockSpec((2, None, count, STEP, width // 2), lambda i, j, p: (0, i, 0, j, 0))
            ]
            + [pl.BlockSpec((STEP, width + LANES), lambda i, j, p: (i * per + j, 0))] * count,
        ),
        out_shape=[jax.ShapeDtypeStruct((2, chunks, count, depth, width // 2), jnp.float32)]
        + [jax.ShapeDtypeStruct((chunks * depth, width + LANES), jnp.int16)] * count,
        cost_estimate=pl.CostEstimate(
            flops=10 * rows * width, bytes_accessed=12 * rows * width, transcendentals=0
        ),
        name="core_forward",
    )(place, view, codes, trig)
    return outs[0].reshape(2, rows, width // 2), outs[1:]


def gather_kernel(count, place_ref, *refs):
    code_refs = refs[-count:]
    first_ref = refs[0]
    part_refs = refs[1 : -count - 1]
    words_ref = refs[-count - 1]
    width = first_ref.shape[2]
    place = place_ref[0]
    token = lax.broadcasted_iota(jnp.int32, (STEP, LANES), 0)
    for piece in range(count):
        source = place ^ piece
        values = []
        for tile in range(width // LANES):
            lanes = tile_at(tile)
            value = first_ref[source, :, lanes]
            for ref in part_refs:
                value = value + ref[source, :, lanes].astype(jnp.float32)
            words = words_ref[source, 0, :, lanes]
            bits = jnp.bitwise_and(jnp.right_shift(jnp.broadcast_to(words, token.shape), token), 1)
            values.append(value * bits.astype(jnp.float32))

        def store(tile, codes):
            code_refs[piece][:, tile_at(tile)] = codes

        encode(values, store)


def gather_parts(place, parts, words, count):
    rows, width = parts[0].shape
    depth = rows // count
    piece = pl.BlockSpec((count, STEP, width), lambda i, p: (0, i, 0))
    return pl.pallas_call(
        functools.partial(gather_kernel, count),
        grid_spec=pltpu.PrefetchScalarGridSpec(
            num_scalar_prefetch=1,
            grid=(depth // STEP,),
            in_specs=[piece] * len(parts)
            + [pl.BlockSpec((count, 1, 1, width), lambda i, p: (0, i, 0, 0))],
            out_specs=[pl.BlockSpec((STEP, width + LANES), lambda i, p: (i, 0))] * count,
        ),
        out_shape=[jax.ShapeDtypeStruct((depth, width + LANES), jnp.int16)] * count,
        cost_estimate=pl.CostEstimate(
            flops=12 * rows * width, bytes_accessed=12 * rows * width, transcendentals=0
        ),
        name="gather_parts",
    )(
        place,
        *[part.reshape(count, depth, width) for part in parts],
        words.reshape(count, depth // STEP, 1, width),
    )


def cross_kernel(count, bits, *refs):
    grad_refs = refs[:count]
    field_refs = refs[count : 2 * count]
    cos_ref, sin_ref = refs[2 * count : 2 * count + 2]
    out_refs = refs[2 * count + 2 : 3 * count + 2]
    term_ref, held_ref, sum_ref = refs[3 * count + 2 :]
    width = cos_ref.shape[2]
    tiles = width // LANES
    rows = pl.ds(0, STEP)
    index = pl.program_id(0)

    @pl.when(index == 0)
    def _():
        sum_ref[...] = jnp.zeros_like(sum_ref)

    grad_scales = [scale_of(ref, rows, width) for ref in grad_refs]
    field_scales = [scale_of(ref, rows, width) for ref in field_refs]
    for tile in range(tiles):
        lanes = tile_at(tile)
        levels = [[widen(r[rows, lanes]) * s for r, s in zip(field_refs, field_scales)]]
        for bit in range(bits - 1):
            field = list(levels[-1])
            for low in range(count):
                if low & (1 << bit):
                    continue
                high = low | (1 << bit)
                pair = drop_bit(low, bit)
                cosine = cos_ref[bit, pair : pair + 1, lanes]
                sine = sin_ref[bit, pair : pair + 1, lanes]
                v_low, v_high = field[low], field[high]
                field[low] = cosine * v_low - sine * v_high
                field[high] = sine * v_low + cosine * v_high
            levels.append(field)
        grad = [widen(r[rows, lanes]) * s for r, s in zip(grad_refs, grad_scales)]
        for bit in reversed(range(bits)):
            before = levels[bit]
            for low in range(count):
                if low & (1 << bit):
                    continue
                high = low | (1 << bit)
                pair = drop_bit(low, bit)
                cosine = cos_ref[bit, pair : pair + 1, lanes]
                sine = sin_ref[bit, pair : pair + 1, lanes]
                g_low, g_high = grad[low], grad[high]
                grad[low] = cosine * g_low + sine * g_high
                grad[high] = cosine * g_high - sine * g_low
                term = grad[high] * before[low] - grad[low] * before[high]
                sum_ref[bit, pair, :, lanes] += jnp.sum(term.reshape(STEP // 8, 8, LANES), axis=0)
        for piece in range(count):
            held_ref[piece, :, lanes] = grad[piece]

    for piece in range(count):

        def store(tile, codes):
            out_refs[piece][:, tile_at(tile)] = codes

        encode([held_ref[piece, :, tile_at(tile)] for tile in range(tiles)], store)

    @pl.when(index == pl.num_programs(0) - 1)
    def _():
        term_ref[...] = jnp.sum(sum_ref[...], axis=2)


def cross_sections(grads, fields, cos_table, sin_table, offset):
    count = len(grads)
    bits, pairs, width = cos_table.shape
    rows, wide = grads[0].shape
    piece = pl.BlockSpec((STEP, wide), lambda i: (i, 0))
    moved = pl.BlockSpec((STEP, wide), lambda i: (i + offset * (rows // STEP), 0))
    table = pl.BlockSpec(cos_table.shape, lambda i: (0, 0, 0))
    outs = pl.pallas_call(
        functools.partial(cross_kernel, count, bits),
        grid=(rows // STEP,),
        in_specs=[piece] * count + [moved] * count + [table] * 2,
        out_specs=[piece] * count + [table],
        out_shape=[jax.ShapeDtypeStruct((rows, wide), jnp.int16)] * count
        + [jax.ShapeDtypeStruct(cos_table.shape, jnp.float32)],
        scratch_shapes=[
            pltpu.VMEM((count, STEP, width), jnp.float32),
            pltpu.VMEM((bits, pairs, 8, width), jnp.float32),
        ],
        cost_estimate=pl.CostEstimate(
            flops=20 * bits * count * rows * width,
            bytes_accessed=6 * count * rows * width,
            transcendentals=0,
        ),
        name="cross_sections",
    )(*grads, *fields, cos_table, sin_table)
    return outs[:count], outs[count]


def backward_kernel(
    local, place_ref, grad_ref, other_ref, states_ref, pair_ref, trig_ref, cos_ref, sin_ref,
    hot_ref, lane_in, tile_in, core_in, whole_ref,
    out_ref, lane_out, tile_out, core_out, lane_sum, tile_sum, core_sum,
):
    rows, width = out_ref.shape
    tiles = width // LANES
    half = width // 2
    index = pl.program_id(0)
    start = place_ref[1] * half

    @pl.when(index == 0)
    def _():
        lane_sum[...] = jnp.zeros_like(lane_sum)
        tile_sum[...] = jnp.zeros_like(tile_sum)
        core_sum[...] = jnp.zeros_like(core_sum)

    def folded(value):
        return jnp.sum(value.reshape(STEP // 8, 8, LANES), axis=0)

    def block(number, carry):
        at = pl.ds(pl.multiple_of(number * STEP, STEP), STEP)
        scale = scale_of(grad_ref, at, width)
        other_scale = scale_of(other_ref, at, width)
        for tile in range(tiles // 2):
            lanes = pl.ds(pl.multiple_of(start + tile * LANES, LANES), LANES)
            mine = widen(grad_ref[at, lanes]) * scale
            partner = widen(other_ref[at, lanes]) * other_scale
            term = partner * pair_ref[0, at, tile_at(tile)] - mine * pair_ref[1, at, tile_at(tile)]
            core_sum[tile] += folded(term)
        grad = []
        for tile in range(tiles):
            lanes = tile_at(tile)
            mine = widen(grad_ref[at, lanes]) * scale
            partner = widen(other_ref[at, lanes]) * other_scale
            grad.append(trig_ref[0:1, lanes] * mine - trig_ref[1:2, lanes] * partner)
        for section in reversed(range(LANE_BITS, local)):
            gap = 1 << (section - LANE_BITS)
            for tile in range(tiles):
                if tile & gap:
                    continue
                cosine = cos_ref[section : section + 1, tile_at(tile)]
                signed = sin_ref[section : section + 1, tile_at(tile)]
                low, high = grad[tile], grad[tile + gap]
                before_low = states_ref[section, at, tile_at(tile)]
                before_high = states_ref[section, at, tile_at(tile + gap)]
                term = folded(high * before_low - low * before_high)
                place = drop_bit(tile, section - LANE_BITS)
                tile_sum[section - LANE_BITS, place] += term
                grad[tile] = cosine * low - signed * high
                grad[tile + gap] = cosine * high + signed * low
        for tile in range(tiles):
            value = grad[tile]
            for section in reversed(range(LANE_BITS)):
                cosine = cos_ref[section : section + 1, tile_at(tile)]
                signed = sin_ref[section : section + 1, tile_at(tile)]
                other = lane_partner(value, section)
                state = states_ref[section, at, tile_at(tile)]
                lane_sum[section, tile] += folded(other * state)
                value = cosine * value - signed * other
            out_ref[at, tile_at(tile)] = value.astype(out_ref.dtype)
        return carry

    lax.fori_loop(0, rows // STEP, block, 0)

    @pl.when(index == pl.num_programs(0) - 1)
    def _():
        for section in range(LANE_BITS):
            summed = jnp.sum(lane_sum[section], axis=1)
            lane_out[section] = lane_in[section] + lax.dot_general(
                summed,
                hot_ref[section],
                (((1,), (1,)), ((), ())),
                precision=HIGH,
                preferred_element_type=jnp.float32,
            )
        for section in range(local - LANE_BITS):
            tile_out[section] = tile_in[section] + jnp.sum(tile_sum[section], axis=1)
        core_out[...] = core_in[...] + jnp.sum(core_sum[...], axis=1)


def backward_local(
    place, grad, other, states, pair, trig, cos_table, sin_table, hot, sums, whole, chunk, count,
):
    depth = grad.shape[0] // count
    local, rows, width = states.shape
    tiles = width // LANES
    high = local - LANE_BITS
    base = chunk * count
    block = min(depth, 32)
    per = depth // block
    fixed = lambda shape: pl.BlockSpec(shape, lambda i, p: (0,) * len(shape))
    row_of = lambda i, p: (base + (p[0] ^ (i // per))) * per + i % per
    shapes = [(LANE_BITS, tiles, LANES // 2), (high, tiles // 2, LANES), (tiles // 2, LANES)]
    return pl.pallas_call(
        functools.partial(backward_kernel, local),
        grid_spec=pltpu.PrefetchScalarGridSpec(
            num_scalar_prefetch=1,
            grid=(count * per,),
            in_specs=[
                pl.BlockSpec((block, width + LANES), lambda i, p: (i, 0)),
                pl.BlockSpec((block, width + LANES), lambda i, p: (i, 0)),
                pl.BlockSpec((local, block, width), lambda i, p: (0, row_of(i, p), 0)),
                pl.BlockSpec((2, block, width // 2), lambda i, p: (0, row_of(i, p), 0)),
                fixed((2, width)),
                fixed((local, width)),
                fixed((local, width)),
                fixed(hot.shape),
            ]
            + [fixed(shape) for shape in shapes]
            + [pl.BlockSpec(memory_space=pl.ANY)],
            out_specs=[pl.BlockSpec((block, width), lambda i, p: (row_of(i, p), 0))]
            + [fixed(shape) for shape in shapes],
            scratch_shapes=[
                pltpu.VMEM((LANE_BITS, tiles, 8, LANES), jnp.float32),
                pltpu.VMEM((high, tiles // 2, 8, LANES), jnp.float32),
                pltpu.VMEM((tiles // 2, 8, LANES), jnp.float32),
            ],
        ),
        out_shape=[jax.ShapeDtypeStruct((rows, width), jnp.bfloat16)]
        + [jax.ShapeDtypeStruct(shape, jnp.float32) for shape in shapes],
        input_output_aliases={12: 0},
        cost_estimate=pl.CostEstimate(
            flops=8 * local * depth * count * width,
            bytes_accessed=4 * (local + 2) * depth * count * width,
            transcendentals=0,
        ),
        name="backward_local",
    )(place, grad, other, states, pair, trig, cos_table, sin_table, hot, *sums, whole)


def tree_sum(parts):
    while len(parts) > 1:
        parts = [parts[k] + parts[k + 1] for k in range(0, len(parts), 2)]
    return parts[0]


def gather_shares(value, me, bits):
    for bit in range(bits):
        other = swap(value, "tensor", 1 << bit)
        first = ((me >> bit) & 1) == 0
        value = jnp.concatenate(
            [jnp.where(first, value, other), jnp.where(first, other, value)], axis=0
        )
        if bit == 0:
            pair = value
    return value, pair


def scatter_shares(value, me, bits):
    for bit in reversed(range(bits)):
        halves = value.reshape((2, -1) + value.shape[1:])
        own = (me >> bit) & 1
        value = pick(halves, own) + swap(pick(halves, 1 - own), "tensor", 1 << bit)
    return value[0]


def body(activations, angles, clip_bits, codes, exponents, cotangent):
    rows, width = activations.shape
    sections, share = angles.shape
    groups = lax.axis_size("dp")
    devices = lax.axis_size("tensor")
    ways = devices // groups
    columns = codes.shape[1]
    part = columns // ways
    local = width.bit_length() - 1
    cross = sections - local
    count = devices // 2
    me = lax.axis_index("tensor")
    mine = lax.axis_index("dp")
    level = me // ways
    core = me & 1
    line = me >> 1
    chunks = chunks_of(rows, count)
    chunk_rows = rows // chunks
    place = jnp.stack([line, core])

    remote = []
    near = []
    for q in range(chunks):
        own = cotangent[q * chunk_rows : (q + 1) * chunk_rows]
        blocks = jnp.stack([own] + [swap(own, "tensor", m * ways) for m in range(1, groups)])
        arrived = jnp.concatenate(
            [swap(pick(blocks, level ^ mine ^ m), "dp", m) for m in range(1, groups)],
            axis=0,
        )
        close = pick(blocks, level ^ mine)
        remote.append([arrived] + [swap(arrived, "tensor", m) for m in range(1, ways)])
        near.append([close] + [swap(close, "tensor", m) for m in range(1, ways)])

    scale = jnp.exp2(exponents.astype(jnp.float32)).astype(jnp.bfloat16)
    scale = scale.reshape(-1, 1, part)
    column_place = jnp.stack([me % ways, mine * ways])

    cosine = jnp.cos(angles)
    sine = jnp.sin(angles)
    cos_table, sin_table = local_tables(cosine[:local], sine[:local], width)
    states, last_codes = forward_local(activations, cos_table, sin_table)

    trig = jnp.stack([cosine[local:], sine[local:]])[None]
    trig, first_trig = gather_shares(trig, me, cross)
    flip = (1 - 2 * core).astype(jnp.float32)
    core_trig = jnp.moveaxis(first_trig[:, :, 0], 0, 1).reshape(2, width)
    core_trig = core_trig * jnp.stack([jnp.float32(1), -flip])[:, None]
    trig = jnp.moveaxis(trig, 0, 2).reshape(2, cross, devices // 2, width)
    jj = jnp.arange(count // 2, dtype=jnp.int32)
    cross_cos, cross_sin, flips = [], [], []
    for bit in range(cross - 1):
        pair = (drop_bit(line, bit) ^ jj) * 2 + core
        flips.append((1 - 2 * ((line >> bit) & 1)).astype(jnp.float32))
        cross_cos.append(jnp.take(trig[0, bit + 1], pair, axis=0))
        cross_sin.append(jnp.take(trig[1, bit + 1], pair, axis=0) * flips[-1])
    cross_cos = jnp.stack(cross_cos)
    cross_sin = jnp.stack(cross_sin)

    partner_codes = swap(last_codes, "tensor", 1)
    pair_states, fields = core_forward(place, states, partner_codes, core_trig, count, chunks)
    fields = [fields[0]] + [swap(fields[m], "tensor", 2 * m) for m in range(1, count)]

    hot, signs = lane_selectors(LANE_BITS)
    hot = -hot * signs[:, None, :]
    tiles = width // LANES
    sums = [
        jnp.zeros((LANE_BITS, tiles, LANES // 2), jnp.float32),
        jnp.zeros((local - LANE_BITS, tiles // 2, LANES), jnp.float32),
        jnp.zeros((tiles // 2, LANES), jnp.float32),
    ]
    whole = jnp.zeros((rows, width), jnp.bfloat16)
    cross_terms = []
    backs = []
    word_rows = chunk_rows // 16
    for q in range(chunks):
        sent = product(column_place, remote[q], codes, scale, groups - 1, jnp.bfloat16)
        kept = product(column_place, near[q], codes, scale, 1, jnp.float32)
        parts = list(kept) + [swap(sent[m - 1], "dp", m) for m in range(1, groups)]
        words = clip_bits[q * word_rows : (q + 1) * word_rows]
        grads = gather_parts(place, parts, words, count)
        grads = [grads[0]] + [swap(grads[m], "tensor", 2 * m) for m in range(1, count)]
        grads, terms = cross_sections(grads, fields, cross_cos, cross_sin, q)
        cross_terms.append(terms)
        backs.append([grads[0]] + [swap(grads[m], "tensor", 2 * m) for m in range(1, count)])

    for q in range(chunks):
        grad = jnp.concatenate(backs[q], axis=0)
        outs = backward_local(
            place, grad, swap(grad, "tensor", 1), states,
            pair_states, core_trig, cos_table, sin_table, hot, sums, whole, q, count,
        )
        whole, sums = outs[0], outs[1:]

    terms = functools.reduce(jnp.add, cross_terms)
    natural = jnp.stack(
        [
            jnp.take(terms[bit], drop_bit(line, bit) ^ jj, axis=0) * flips[bit]
            for bit in range(cross - 1)
        ]
    )
    natural = natural.reshape(cross - 1, count // 2, 1, 2, share)
    natural = jnp.where(
        jnp.arange(2, dtype=jnp.int32)[None, None, :, None, None] == core, natural, 0.0
    )
    natural = jnp.moveaxis(natural.reshape(cross - 1, devices, share), 1, 0)
    owned = scatter_shares(natural, me, cross)

    final = jnp.concatenate(
        [
            sums[0].reshape(LANE_BITS, share),
            sums[1].reshape(local - LANE_BITS, share),
            sums[2].reshape(1, share) * flip,
            owned,
        ],
        axis=0,
    )
    angle_grad = tree_sum([final] + [swap(final, "dp", m) for m in range(1, groups)])
    return (whole, angle_grad)


def chunks_of(rows, count):
    chunks = CHUNKS
    while rows // (chunks * count) < STEP:
        chunks //= 2
    return chunks


def solution(mesh):
    placed = (
        P("dp", "tensor"),
        P(None, "tensor"),
        P("dp", "tensor"),
        P("tensor", "dp"),
        P(),
        P("dp", "tensor"),
    )

    return jax.shard_map(
        body,
        mesh=mesh,
        in_specs=placed,
        out_specs=(P("dp", "tensor"), P(None, "tensor")),
        check_vma=False,
    )
```

```python
import functools

import jax
import jax.numpy as jnp
from jax import lax
from jax.experimental import pallas as pl
from jax.experimental.pallas import tpu as pltpu
from jax.sharding import PartitionSpec as P


LANES = 128
LANE_BITS = 7
HIGH = lax.Precision.HIGHEST


CHUNKS = 2
STEP = 16
FRACTION = 14.0


def swap(value, axis, mask):
    pairs = [(source, source ^ mask) for source in range(lax.axis_size(axis))]
    return lax.ppermute(value, axis, pairs)


def pick(stacked, index):
    return lax.dynamic_index_in_dim(stacked, index, 0, keepdims=False)


def drop_bit(index, bit):
    return ((index >> (bit + 1)) << bit) | (index & ((1 << bit) - 1))


def lane_selectors(sections):
    lane = jnp.arange(LANES, dtype=jnp.int32)
    rows = []
    signs = []
    for section in range(sections):
        pair = drop_bit(lane, section)
        hot = pair[None, :] == jnp.arange(LANES // 2, dtype=jnp.int32)[:, None]
        rows.append(hot.astype(jnp.float32))
        signs.append(jnp.where((lane >> section) & 1 == 0, -1.0, 1.0).astype(jnp.float32))
    return jnp.stack(rows), jnp.stack(signs)


def local_tables(cosine, sine, width):
    local = cosine.shape[0]
    tiles = width // LANES
    hot, signs = lane_selectors(LANE_BITS)

    def lanes(values):
        shaped = values[:LANE_BITS].reshape(LANE_BITS, tiles, LANES // 2)
        return jnp.einsum("stk,skl->stl", shaped, hot, precision=HIGH)

    def whole(section, values, sign):
        step = 1 << (section - LANE_BITS)
        shaped = values.reshape(tiles // (2 * step), 1, step, LANES)
        return jnp.concatenate([sign * shaped, shaped], axis=1).reshape(1, tiles, LANES)

    cos_rows = [lanes(cosine)]
    sin_rows = [lanes(sine) * signs[:, None, :]]
    for section in range(LANE_BITS, local):
        cos_rows.append(whole(section, cosine[section], 1.0))
        sin_rows.append(whole(section, sine[section], -1.0))
    cos_table = jnp.concatenate(cos_rows, axis=0).reshape(local, width)
    sin_table = jnp.concatenate(sin_rows, axis=0).reshape(local, width)
    return cos_table, sin_table


def lane_partner(value, section):
    half = 1 << section
    lane = lax.broadcasted_iota(jnp.int32, value.shape, 1)
    up = pltpu.roll(value, half, 1)
    if 2 * half == LANES:
        return up
    down = pltpu.roll(value, LANES - half, 1)
    return jnp.where((lane & half) == 0, down, up)


def tile_at(tile):
    return pl.ds(tile * LANES, LANES)


def encode(values, store):
    most = functools.reduce(jnp.maximum, [jnp.abs(value) for value in values])
    most = jnp.max(most, axis=1, keepdims=True)
    power = jnp.ceil(jnp.log2(jnp.maximum(most, 1e-30)))
    factor = jnp.exp2(FRACTION - power)
    for tile, value in enumerate(values):
        store(tile, jnp.round(value * factor).astype(jnp.int32).astype(jnp.int16))
    power = jnp.broadcast_to(power, values[0].shape)
    store(len(values), power.astype(jnp.int32).astype(jnp.int16))


def widen(codes):
    return codes.astype(jnp.int32).astype(jnp.float32)


def scale_of(ref, at, width):
    return jnp.exp2(widen(ref[at, pl.ds(width, LANES)]) - FRACTION)


def product_kernel(ways, place_ref, *refs):
    token_refs = refs[:ways]
    code_refs = refs[ways : 2 * ways]
    scale_refs = refs[2 * ways : 3 * ways]
    out_refs = refs[3 * ways :]
    total = None
    for tokens, codes, scale in zip(token_refs, code_refs, scale_refs):
        weight = codes[...] * scale[0]
        part = lax.dot_general(
            tokens[...],
            weight,
            (((1,), (1,)), ((), ())),
            preferred_element_type=jnp.float32,
        )
        total = part if total is None else total + part
    rows = out_refs[0].shape[0]
    for index, ref in enumerate(out_refs):
        ref[...] = total[index * rows : (index + 1) * rows].astype(ref.dtype)


def product(place, tokens, codes, scale, outs, dtype):
    ways = len(tokens)
    width = codes.shape[0]
    rows, part = tokens[0].shape
    block = min(width, 512)
    code_spec = lambda j: pl.BlockSpec((block, part), lambda i, p: (i, p[0] ^ j))
    scale_spec = lambda j: pl.BlockSpec((1, 1, part), lambda i, p: (p[1] + (p[0] ^ j), 0, 0))
    return pl.pallas_call(
        functools.partial(product_kernel, ways),
        grid_spec=pltpu.PrefetchScalarGridSpec(
            num_scalar_prefetch=1,
            grid=(width // block,),
            in_specs=[pl.BlockSpec((rows, part), lambda i, p: (0, 0))] * ways
            + [code_spec(j) for j in range(ways)]
            + [scale_spec(j) for j in range(ways)],
            out_specs=[pl.BlockSpec((rows // outs, block), lambda i, p: (0, i))] * outs,
        ),
        out_shape=[jax.ShapeDtypeStruct((rows // outs, width), dtype)] * outs,
        cost_estimate=pl.CostEstimate(
            flops=2 * rows * part * ways * width,
            bytes_accessed=2 * part * ways * width,
            transcendentals=0,
        ),
        name="product",
    )(place, *tokens, *[codes] * ways, *[scale] * ways)


def forward_kernel(local, act_ref, cos_ref, sin_ref, states_ref, code_ref):
    rows, width = act_ref.shape
    tiles = width // LANES

    def block(index, carry):
        at = pl.ds(pl.multiple_of(index * STEP, STEP), STEP)
        field = []
        for tile in range(tiles):
            value = act_ref[at, tile_at(tile)].astype(jnp.float32)
            for section in range(LANE_BITS):
                other = lane_partner(value, section)
                cosine = cos_ref[section : section + 1, tile_at(tile)]
                signed = sin_ref[section : section + 1, tile_at(tile)]
                value = cosine * value + signed * other
                states_ref[section, at, tile_at(tile)] = value
            field.append(value)
        for section in range(LANE_BITS, local):
            gap = 1 << (section - LANE_BITS)
            for tile in range(tiles):
                if tile & gap:
                    continue
                cosine = cos_ref[section : section + 1, tile_at(tile)]
                signed = sin_ref[section : section + 1, tile_at(tile)]
                low, high = field[tile], field[tile + gap]
                field[tile] = cosine * low + signed * high
                field[tile + gap] = cosine * high - signed * low
            for tile in range(tiles):
                states_ref[section, at, tile_at(tile)] = field[tile]

        def store(tile, codes):
            code_ref[at, tile_at(tile)] = codes

        encode(field, store)
        return carry

    lax.fori_loop(0, rows // STEP, block, 0)


def forward_local(acts, cos_table, sin_table):
    rows, width = acts.shape
    local = cos_table.shape[0]
    block = min(rows, 32)
    table = pl.BlockSpec((local, width), lambda i: (0, 0))
    return pl.pallas_call(
        functools.partial(forward_kernel, local),
        grid=(rows // block,),
        in_specs=[pl.BlockSpec((block, width), lambda i: (i, 0)), table, table],
        out_specs=[
            pl.BlockSpec((local, block, width), lambda i: (0, i, 0)),
            pl.BlockSpec((block, width + LANES), lambda i: (i, 0)),
        ],
        out_shape=[
            jax.ShapeDtypeStruct((local, rows, width), jnp.float32),
            jax.ShapeDtypeStruct((rows, width + LANES), jnp.int16),
        ],
        cost_estimate=pl.CostEstimate(
            flops=6 * local * rows * width,
            bytes_accessed=4 * (local + 1) * rows * width,
            transcendentals=0,
        ),
        name="forward_local",
    )(acts, cos_table, sin_table)


def core_kernel(place_ref, state_ref, other_ref, trig_ref, pair_ref, *code_refs):
    width = state_ref.shape[2]
    count = len(code_refs)
    depth = state_ref.shape[1]
    tiles = width // LANES
    half = width // 2
    place = place_ref[0]
    start = place_ref[1] * half
    cosine_at = lambda at: trig_ref[0:1, at]
    signed_at = lambda at: trig_ref[1:2, at]
    for piece in range(count):
        source = place ^ piece
        mine = state_ref.at[source]
        other = other_ref.at[source]
        at = pl.ds(0, depth)
        scale = scale_of(other, at, width)
        field = []
        for tile in range(tiles):
            lanes = tile_at(tile)
            value = mine[at, lanes]
            partner = widen(other[at, lanes]) * scale
            field.append(cosine_at(lanes) * value + signed_at(lanes) * partner)

        def store(tile, codes):
            code_refs[piece][at, tile_at(tile)] = codes

        encode(field, store)
        for tile in range(tiles // 2):
            lanes = pl.ds(pl.multiple_of(start + tile * LANES, LANES), LANES)
            value = mine[at, lanes]
            partner = widen(other[at, lanes]) * scale
            cosine, signed = cosine_at(lanes), signed_at(lanes)
            pair_ref[0, source, at, tile_at(tile)] = cosine * value + signed * partner
            pair_ref[1, source, at, tile_at(tile)] = cosine * partner - signed * value


def core_forward(place, states, other, trig, count, chunks):
    local, rows, width = states.shape
    depth = rows // (chunks * count)
    view = states.reshape(local, chunks, count, depth, width)
    codes = other.reshape(chunks, count, depth, width + LANES)
    per = depth // STEP
    outs = pl.pallas_call(
        core_kernel,
        grid_spec=pltpu.PrefetchScalarGridSpec(
            num_scalar_prefetch=1,
            grid=(chunks, per),
            in_specs=[
                pl.BlockSpec(
                    (None, None, count, STEP, width), lambda i, j, p: (local - 1, i, 0, j, 0)
                ),
                pl.BlockSpec((None, count, STEP, width + LANES), lambda i, j, p: (i, 0, j, 0)),
                pl.BlockSpec((2, width), lambda i, j, p: (0, 0)),
            ],
            out_specs=[
                pl.BlockSpec((2, None, count, STEP, width // 2), lambda i, j, p: (0, i, 0, j, 0))
            ]
            + [pl.BlockSpec((STEP, width + LANES), lambda i, j, p: (i * per + j, 0))] * count,
        ),
        out_shape=[jax.ShapeDtypeStruct((2, chunks, count, depth, width // 2), jnp.float32)]
        + [jax.ShapeDtypeStruct((chunks * depth, width + LANES), jnp.int16)] * count,
        cost_estimate=pl.CostEstimate(
            flops=10 * rows * width, bytes_accessed=12 * rows * width, transcendentals=0
        ),
        name="core_forward",
    )(place, view, codes, trig)
    return outs[0].reshape(2, rows, width // 2), outs[1:]


def gather_kernel(count, place_ref, *refs):
    code_refs = refs[-count:]
    first_ref = refs[0]
    part_refs = refs[1 : -count - 1]
    words_ref = refs[-count - 1]
    width = first_ref.shape[2]
    place = place_ref[0]
    token = lax.broadcasted_iota(jnp.int32, (STEP, LANES), 0)
    for piece in range(count):
        source = place ^ piece
        values = []
        for tile in range(width // LANES):
            lanes = tile_at(tile)
            value = first_ref[source, :, lanes]
            for ref in part_refs:
                value = value + ref[source, :, lanes].astype(jnp.float32)
            words = words_ref[source, 0, :, lanes]
            bits = jnp.bitwise_and(jnp.right_shift(jnp.broadcast_to(words, token.shape), token), 1)
            values.append(value * bits.astype(jnp.float32))

        def store(tile, codes):
            code_refs[piece][:, tile_at(tile)] = codes

        encode(values, store)


def gather_parts(place, parts, words, count):
    rows, width = parts[0].shape
    depth = rows // count
    piece = pl.BlockSpec((count, STEP, width), lambda i, p: (0, i, 0))
    return pl.pallas_call(
        functools.partial(gather_kernel, count),
        grid_spec=pltpu.PrefetchScalarGridSpec(
            num_scalar_prefetch=1,
            grid=(depth // STEP,),
            in_specs=[piece] * len(parts)
            + [pl.BlockSpec((count, 1, 1, width), lambda i, p: (0, i, 0, 0))],
            out_specs=[pl.BlockSpec((STEP, width + LANES), lambda i, p: (i, 0))] * count,
        ),
        out_shape=[jax.ShapeDtypeStruct((depth, width + LANES), jnp.int16)] * count,
        cost_estimate=pl.CostEstimate(
            flops=12 * rows * width, bytes_accessed=12 * rows * width, transcendentals=0
        ),
        name="gather_parts",
    )(
        place,
        *[part.reshape(count, depth, width) for part in parts],
        words.reshape(count, depth // STEP, 1, width),
    )


def cross_kernel(count, bits, *refs):
    grad_refs = refs[:count]
    field_refs = refs[count : 2 * count]
    cos_ref, sin_ref = refs[2 * count : 2 * count + 2]
    out_refs = refs[2 * count + 2 : 3 * count + 2]
    term_ref, held_ref, sum_ref = refs[3 * count + 2 :]
    width = cos_ref.shape[2]
    tiles = width // LANES
    rows = pl.ds(0, STEP)
    index = pl.program_id(0)

    @pl.when(index == 0)
    def _():
        sum_ref[...] = jnp.zeros_like(sum_ref)

    grad_scales = [scale_of(ref, rows, width) for ref in grad_refs]
    field_scales = [scale_of(ref, rows, width) for ref in field_refs]
    for tile in range(tiles):
        lanes = tile_at(tile)
        levels = [[widen(r[rows, lanes]) * s for r, s in zip(field_refs, field_scales)]]
        for bit in range(bits - 1):
            field = list(levels[-1])
            for low in range(count):
                if low & (1 << bit):
                    continue
                high = low | (1 << bit)
                pair = drop_bit(low, bit)
                cosine = cos_ref[bit, pair : pair + 1, lanes]
                sine = sin_ref[bit, pair : pair + 1, lanes]
                v_low, v_high = field[low], field[high]
                field[low] = cosine * v_low - sine * v_high
                field[high] = sine * v_low + cosine * v_high
            levels.append(field)
        grad = [widen(r[rows, lanes]) * s for r, s in zip(grad_refs, grad_scales)]
        for bit in reversed(range(bits)):
            before = levels[bit]
            for low in range(count):
                if low & (1 << bit):
                    continue
                high = low | (1 << bit)
                pair = drop_bit(low, bit)
                cosine = cos_ref[bit, pair : pair + 1, lanes]
                sine = sin_ref[bit, pair : pair + 1, lanes]
                g_low, g_high = grad[low], grad[high]
                grad[low] = cosine * g_low + sine * g_high
                grad[high] = cosine * g_high - sine * g_low
                term = grad[high] * before[low] - grad[low] * before[high]
                sum_ref[bit, pair, :, lanes] += jnp.sum(term.reshape(STEP // 8, 8, LANES), axis=0)
        for piece in range(count):
            held_ref[piece, :, lanes] = grad[piece]

    for piece in range(count):

        def store(tile, codes):
            out_refs[piece][:, tile_at(tile)] = codes

        encode([held_ref[piece, :, tile_at(tile)] for tile in range(tiles)], store)

    @pl.when(index == pl.num_programs(0) - 1)
    def _():
        term_ref[...] = jnp.sum(sum_ref[...], axis=2)


def cross_sections(grads, fields, cos_table, sin_table, offset):
    count = len(grads)
    bits, pairs, width = cos_table.shape
    rows, wide = grads[0].shape
    piece = pl.BlockSpec((STEP, wide), lambda i: (i, 0))
    moved = pl.BlockSpec((STEP, wide), lambda i: (i + offset * (rows // STEP), 0))
    table = pl.BlockSpec(cos_table.shape, lambda i: (0, 0, 0))
    outs = pl.pallas_call(
        functools.partial(cross_kernel, count, bits),
        grid=(rows // STEP,),
        in_specs=[piece] * count + [moved] * count + [table] * 2,
        out_specs=[piece] * count + [table],
        out_shape=[jax.ShapeDtypeStruct((rows, wide), jnp.int16)] * count
        + [jax.ShapeDtypeStruct(cos_table.shape, jnp.float32)],
        scratch_shapes=[
            pltpu.VMEM((count, STEP, width), jnp.float32),
            pltpu.VMEM((bits, pairs, 8, width), jnp.float32),
        ],
        cost_estimate=pl.CostEstimate(
            flops=20 * bits * count * rows * width,
            bytes_accessed=6 * count * rows * width,
            transcendentals=0,
        ),
        name="cross_sections",
    )(*grads, *fields, cos_table, sin_table)
    return outs[:count], outs[count]


def backward_kernel(
    local, place_ref, grad_ref, other_ref, states_ref, pair_ref, trig_ref, cos_ref, sin_ref,
    hot_ref, lane_in, tile_in, core_in, whole_ref,
    out_ref, lane_out, tile_out, core_out, lane_sum, tile_sum, core_sum,
):
    rows, width = out_ref.shape
    tiles = width // LANES
    half = width // 2
    index = pl.program_id(0)
    start = place_ref[1] * half

    @pl.when(index == 0)
    def _():
        lane_sum[...] = jnp.zeros_like(lane_sum)
        tile_sum[...] = jnp.zeros_like(tile_sum)
        core_sum[...] = jnp.zeros_like(core_sum)

    def folded(value):
        return jnp.sum(value.reshape(STEP // 8, 8, LANES), axis=0)

    def block(number, carry):
        at = pl.ds(pl.multiple_of(number * STEP, STEP), STEP)
        scale = scale_of(grad_ref, at, width)
        other_scale = scale_of(other_ref, at, width)
        for tile in range(tiles // 2):
            lanes = pl.ds(pl.multiple_of(start + tile * LANES, LANES), LANES)
            mine = widen(grad_ref[at, lanes]) * scale
            partner = widen(other_ref[at, lanes]) * other_scale
            term = partner * pair_ref[0, at, tile_at(tile)] - mine * pair_ref[1, at, tile_at(tile)]
            core_sum[tile] += folded(term)
        grad = []
        for tile in range(tiles):
            lanes = tile_at(tile)
            mine = widen(grad_ref[at, lanes]) * scale
            partner = widen(other_ref[at, lanes]) * other_scale
            grad.append(trig_ref[0:1, lanes] * mine - trig_ref[1:2, lanes] * partner)
        for section in reversed(range(LANE_BITS, local)):
            gap = 1 << (section - LANE_BITS)
            for tile in range(tiles):
                if tile & gap:
                    continue
                cosine = cos_ref[section : section + 1, tile_at(tile)]
                signed = sin_ref[section : section + 1, tile_at(tile)]
                low, high = grad[tile], grad[tile + gap]
                before_low = states_ref[section, at, tile_at(tile)]
                before_high = states_ref[section, at, tile_at(tile + gap)]
                term = folded(high * before_low - low * before_high)
                place = drop_bit(tile, section - LANE_BITS)
                tile_sum[section - LANE_BITS, place] += term
                grad[tile] = cosine * low - signed * high
                grad[tile + gap] = cosine * high + signed * low
        for tile in range(tiles):
            value = grad[tile]
            for section in reversed(range(LANE_BITS)):
                cosine = cos_ref[section : section + 1, tile_at(tile)]
                signed = sin_ref[section : section + 1, tile_at(tile)]
                other = lane_partner(value, section)
                state = states_ref[section, at, tile_at(tile)]
                lane_sum[section, tile] += folded(other * state)
                value = cosine * value - signed * other
            out_ref[at, tile_at(tile)] = value.astype(out_ref.dtype)
        return carry

    lax.fori_loop(0, rows // STEP, block, 0)

    @pl.when(index == pl.num_programs(0) - 1)
    def _():
        for section in range(LANE_BITS):
            summed = jnp.sum(lane_sum[section], axis=1)
            lane_out[section] = lane_in[section] + lax.dot_general(
                summed,
                hot_ref[section],
                (((1,), (1,)), ((), ())),
                precision=HIGH,
                preferred_element_type=jnp.float32,
            )
        for section in range(local - LANE_BITS):
            tile_out[section] = tile_in[section] + jnp.sum(tile_sum[section], axis=1)
        core_out[...] = core_in[...] + jnp.sum(core_sum[...], axis=1)


def backward_local(
    place, grad, other, states, pair, trig, cos_table, sin_table, hot, sums, whole, chunk, count,
):
    depth = grad.shape[0] // count
    local, rows, width = states.shape
    tiles = width // LANES
    high = local - LANE_BITS
    base = chunk * count
    block = min(depth, 32)
    per = depth // block
    fixed = lambda shape: pl.BlockSpec(shape, lambda i, p: (0,) * len(shape))
    row_of = lambda i, p: (base + (p[0] ^ (i // per))) * per + i % per
    shapes = [(LANE_BITS, tiles, LANES // 2), (high, tiles // 2, LANES), (tiles // 2, LANES)]
    return pl.pallas_call(
        functools.partial(backward_kernel, local),
        grid_spec=pltpu.PrefetchScalarGridSpec(
            num_scalar_prefetch=1,
            grid=(count * per,),
            in_specs=[
                pl.BlockSpec((block, width + LANES), lambda i, p: (i, 0)),
                pl.BlockSpec((block, width + LANES), lambda i, p: (i, 0)),
                pl.BlockSpec((local, block, width), lambda i, p: (0, row_of(i, p), 0)),
                pl.BlockSpec((2, block, width // 2), lambda i, p: (0, row_of(i, p), 0)),
                fixed((2, width)),
                fixed((local, width)),
                fixed((local, width)),
                fixed(hot.shape),
            ]
            + [fixed(shape) for shape in shapes]
            + [pl.BlockSpec(memory_space=pl.ANY)],
            out_specs=[pl.BlockSpec((block, width), lambda i, p: (row_of(i, p), 0))]
            + [fixed(shape) for shape in shapes],
            scratch_shapes=[
                pltpu.VMEM((LANE_BITS, tiles, 8, LANES), jnp.float32),
                pltpu.VMEM((high, tiles // 2, 8, LANES), jnp.float32),
                pltpu.VMEM((tiles // 2, 8, LANES), jnp.float32),
            ],
        ),
        out_shape=[jax.ShapeDtypeStruct((rows, width), jnp.bfloat16)]
        + [jax.ShapeDtypeStruct(shape, jnp.float32) for shape in shapes],
        input_output_aliases={12: 0},
        cost_estimate=pl.CostEstimate(
            flops=8 * local * depth * count * width,
            bytes_accessed=4 * (local + 2) * depth * count * width,
            transcendentals=0,
        ),
        name="backward_local",
    )(place, grad, other, states, pair, trig, cos_table, sin_table, hot, *sums, whole)


def tree_sum(parts):
    while len(parts) > 1:
        parts = [parts[k] + parts[k + 1] for k in range(0, len(parts), 2)]
    return parts[0]


def gather_shares(value, line, core, count):
    near = jnp.stack([value] + [swap(value, "tensor", 2 * m) for m in range(1, count)])
    near = jnp.take(near, line ^ jnp.arange(count, dtype=jnp.int32), axis=0)
    other = swap(near, "tensor", 1)
    first = core == 0
    return jnp.stack([jnp.where(first, near, other), jnp.where(first, other, near)], axis=1)


def scatter_shares(value, me, bits):
    for bit in reversed(range(bits)):
        halves = value.reshape((2, -1) + value.shape[1:])
        own = (me >> bit) & 1
        value = pick(halves, own) + swap(pick(halves, 1 - own), "tensor", 1 << bit)
    return value[0]


def body(activations, angles, clip_bits, codes, exponents, cotangent):
    rows, width = activations.shape
    sections, share = angles.shape
    groups = lax.axis_size("dp")
    devices = lax.axis_size("tensor")
    ways = devices // groups
    columns = codes.shape[1]
    part = columns // ways
    local = width.bit_length() - 1
    cross = sections - local
    count = devices // 2
    me = lax.axis_index("tensor")
    mine = lax.axis_index("dp")
    level = me // ways
    core = me & 1
    line = me >> 1
    chunks = chunks_of(rows, count)
    chunk_rows = rows // chunks
    place = jnp.stack([line, core])

    remote = []
    near = []
    for q in range(chunks):
        own = cotangent[q * chunk_rows : (q + 1) * chunk_rows]
        blocks = jnp.stack([own] + [swap(own, "tensor", m * ways) for m in range(1, groups)])
        arrived = jnp.concatenate(
            [swap(pick(blocks, level ^ mine ^ m), "dp", m) for m in range(1, groups)],
            axis=0,
        )
        near.append(pick(blocks, level ^ mine))
        remote.append([arrived] + [swap(arrived, "tensor", m) for m in range(1, ways)])
    near = jnp.concatenate(near, axis=0)
    near = [near] + [swap(near, "tensor", m) for m in range(1, ways)]

    scale = jnp.exp2(exponents.astype(jnp.float32)).astype(jnp.bfloat16)
    scale = scale.reshape(-1, 1, part)
    column_place = jnp.stack([me % ways, mine * ways])

    cosine = jnp.cos(angles)
    sine = jnp.sin(angles)
    cos_table, sin_table = local_tables(cosine[:local], sine[:local], width)
    states, last_codes = forward_local(activations, cos_table, sin_table)

    trig = jnp.stack([cosine[local:], sine[local:]])
    trig = gather_shares(trig, line, core, count)
    trig = jnp.moveaxis(trig.reshape(devices, 2, cross, share), 0, 2)
    trig = trig.reshape(2, cross, devices // 2, width)
    flip = (1 - 2 * core).astype(jnp.float32)
    core_trig = lax.dynamic_index_in_dim(trig[:, 0], line, 1, keepdims=False)
    core_trig = core_trig * jnp.stack([jnp.float32(1), -flip])[:, None]
    jj = jnp.arange(count // 2, dtype=jnp.int32)
    cross_cos, cross_sin, flips = [], [], []
    for bit in range(cross - 1):
        pair = (drop_bit(line, bit) ^ jj) * 2 + core
        flips.append((1 - 2 * ((line >> bit) & 1)).astype(jnp.float32))
        cross_cos.append(jnp.take(trig[0, bit + 1], pair, axis=0))
        cross_sin.append(jnp.take(trig[1, bit + 1], pair, axis=0) * flips[-1])
    cross_cos = jnp.stack(cross_cos)
    cross_sin = jnp.stack(cross_sin)

    partner_codes = swap(last_codes, "tensor", 1)
    pair_states, fields = core_forward(place, states, partner_codes, core_trig, count, chunks)
    fields = [fields[0]] + [swap(fields[m], "tensor", 2 * m) for m in range(1, count)]

    hot, signs = lane_selectors(LANE_BITS)
    hot = -hot * signs[:, None, :]
    tiles = width // LANES
    sums = [
        jnp.zeros((LANE_BITS, tiles, LANES // 2), jnp.float32),
        jnp.zeros((local - LANE_BITS, tiles // 2, LANES), jnp.float32),
        jnp.zeros((tiles // 2, LANES), jnp.float32),
    ]
    whole = jnp.zeros((rows, width), jnp.bfloat16)
    cross_terms = []
    backs = []
    word_rows = chunk_rows // 16
    kept = product(column_place, near, codes, scale, chunks, jnp.float32)
    for q in range(chunks):
        sent = product(column_place, remote[q], codes, scale, groups - 1, jnp.bfloat16)
        parts = [kept[q]] + [swap(sent[m - 1], "dp", m) for m in range(1, groups)]
        words = clip_bits[q * word_rows : (q + 1) * word_rows]
        grads = gather_parts(place, parts, words, count)
        grads = [grads[0]] + [swap(grads[m], "tensor", 2 * m) for m in range(1, count)]
        grads, terms = cross_sections(grads, fields, cross_cos, cross_sin, q)
        cross_terms.append(terms)
        backs.append([grads[0]] + [swap(grads[m], "tensor", 2 * m) for m in range(1, count)])

    for q in range(chunks):
        grad = jnp.concatenate(backs[q], axis=0)
        outs = backward_local(
            place, grad, swap(grad, "tensor", 1), states,
            pair_states, core_trig, cos_table, sin_table, hot, sums, whole, q, count,
        )
        whole, sums = outs[0], outs[1:]

    terms = functools.reduce(jnp.add, cross_terms)
    natural = jnp.stack(
        [
            jnp.take(terms[bit], drop_bit(line, bit) ^ jj, axis=0) * flips[bit]
            for bit in range(cross - 1)
        ]
    )
    natural = natural.reshape(cross - 1, count // 2, 1, 2, share)
    natural = jnp.where(
        jnp.arange(2, dtype=jnp.int32)[None, None, :, None, None] == core, natural, 0.0
    )
    natural = jnp.moveaxis(natural.reshape(cross - 1, devices, share), 1, 0)
    owned = scatter_shares(natural, me, cross)

    final = jnp.concatenate(
        [
            sums[0].reshape(LANE_BITS, share),
            sums[1].reshape(local - LANE_BITS, share),
            sums[2].reshape(1, share) * flip,
            owned,
        ],
        axis=0,
    )
    angle_grad = tree_sum([final] + [swap(final, "dp", m) for m in range(1, groups)])
    return (whole, angle_grad)


def chunks_of(rows, count):
    chunks = CHUNKS
    while rows // (chunks * count) < STEP:
        chunks //= 2
    return chunks


def solution(mesh):
    placed = (
        P("dp", "tensor"),
        P(None, "tensor"),
        P("dp", "tensor"),
        P("tensor", "dp"),
        P(),
        P("dp", "tensor"),
    )

    return jax.shard_map(
        body,
        mesh=mesh,
        in_specs=placed,
        out_specs=(P("dp", "tensor"), P(None, "tensor")),
        check_vma=False,
    )
```

```python
import functools

import jax
import jax.numpy as jnp
from jax import lax
from jax.experimental import pallas as pl
from jax.experimental.pallas import tpu as pltpu
from jax.sharding import PartitionSpec as P


LANES = 128
LANE_BITS = 7
HIGH = lax.Precision.HIGHEST


CHUNKS = 2
STEP = 16
FRACTION = 14.0


def swap(value, axis, mask):
    pairs = [(source, source ^ mask) for source in range(lax.axis_size(axis))]
    return lax.ppermute(value, axis, pairs)


def pick(stacked, index):
    return lax.dynamic_index_in_dim(stacked, index, 0, keepdims=False)


def drop_bit(index, bit):
    return ((index >> (bit + 1)) << bit) | (index & ((1 << bit) - 1))


def lane_selectors(sections):
    lane = jnp.arange(LANES, dtype=jnp.int32)
    rows = []
    signs = []
    for section in range(sections):
        pair = drop_bit(lane, section)
        hot = pair[None, :] == jnp.arange(LANES // 2, dtype=jnp.int32)[:, None]
        rows.append(hot.astype(jnp.float32))
        signs.append(jnp.where((lane >> section) & 1 == 0, -1.0, 1.0).astype(jnp.float32))
    return jnp.stack(rows), jnp.stack(signs)


def local_tables(cosine, sine, width):
    local = cosine.shape[0]
    tiles = width // LANES
    hot, signs = lane_selectors(LANE_BITS)

    def lanes(values):
        shaped = values[:LANE_BITS].reshape(LANE_BITS, tiles, LANES // 2)
        return jnp.einsum("stk,skl->stl", shaped, hot, precision=HIGH)

    def whole(section, values, sign):
        step = 1 << (section - LANE_BITS)
        shaped = values.reshape(tiles // (2 * step), 1, step, LANES)
        return jnp.concatenate([sign * shaped, shaped], axis=1).reshape(1, tiles, LANES)

    cos_rows = [lanes(cosine)]
    sin_rows = [lanes(sine) * signs[:, None, :]]
    for section in range(LANE_BITS, local):
        cos_rows.append(whole(section, cosine[section], 1.0))
        sin_rows.append(whole(section, sine[section], -1.0))
    cos_table = jnp.concatenate(cos_rows, axis=0).reshape(local, width)
    sin_table = jnp.concatenate(sin_rows, axis=0).reshape(local, width)
    return cos_table, sin_table


def lane_partner(value, section):
    half = 1 << section
    lane = lax.broadcasted_iota(jnp.int32, value.shape, 1)
    up = pltpu.roll(value, half, 1)
    if 2 * half == LANES:
        return up
    down = pltpu.roll(value, LANES - half, 1)
    return jnp.where((lane & half) == 0, down, up)


def tile_at(tile):
    return pl.ds(tile * LANES, LANES)


def encode(values, store):
    most = functools.reduce(jnp.maximum, [jnp.abs(value) for value in values])
    most = jnp.max(most, axis=1, keepdims=True)
    power = jnp.ceil(jnp.log2(jnp.maximum(most, 1e-30)))
    factor = jnp.exp2(FRACTION - power)
    for tile, value in enumerate(values):
        store(tile, jnp.round(value * factor).astype(jnp.int32).astype(jnp.int16))
    power = jnp.broadcast_to(power, values[0].shape)
    store(len(values), power.astype(jnp.int32).astype(jnp.int16))


def widen(codes):
    return codes.astype(jnp.int32).astype(jnp.float32)


def scale_of(ref, at, width):
    return jnp.exp2(widen(ref[at, pl.ds(width, LANES)]) - FRACTION)


def product_kernel(ways, place_ref, *refs):
    token_refs = refs[:ways]
    code_refs = refs[ways : 2 * ways]
    scale_refs = refs[2 * ways : 3 * ways]
    out_refs = refs[3 * ways :]
    total = None
    for tokens, codes, scale in zip(token_refs, code_refs, scale_refs):
        weight = codes[...] * scale[0]
        part = lax.dot_general(
            tokens[...],
            weight,
            (((1,), (1,)), ((), ())),
            preferred_element_type=jnp.float32,
        )
        total = part if total is None else total + part
    rows = out_refs[0].shape[0]
    for index, ref in enumerate(out_refs):
        ref[...] = total[index * rows : (index + 1) * rows].astype(ref.dtype)


def product(place, tokens, codes, scale, outs):
    ways = len(tokens)
    width = codes.shape[0]
    rows, part = tokens[0].shape
    block = min(width, 512)
    code_spec = lambda j: pl.BlockSpec((block, part), lambda i, p: (i, p[0] ^ j))
    scale_spec = lambda j: pl.BlockSpec((1, 1, part), lambda i, p: (p[1] + (p[0] ^ j), 0, 0))
    return pl.pallas_call(
        functools.partial(product_kernel, ways),
        grid_spec=pltpu.PrefetchScalarGridSpec(
            num_scalar_prefetch=1,
            grid=(width // block,),
            in_specs=[pl.BlockSpec((rows, part), lambda i, p: (0, 0))] * ways
            + [code_spec(j) for j in range(ways)]
            + [scale_spec(j) for j in range(ways)],
            out_specs=[pl.BlockSpec((rows // outs, block), lambda i, p: (0, i))] * outs,
        ),
        out_shape=[jax.ShapeDtypeStruct((rows // outs, width), jnp.float32)]
        + [jax.ShapeDtypeStruct((rows // outs, width), jnp.bfloat16)] * (outs - 1),
        cost_estimate=pl.CostEstimate(
            flops=2 * rows * part * ways * width,
            bytes_accessed=2 * part * ways * width,
            transcendentals=0,
        ),
        name="product",
    )(place, *tokens, *[codes] * ways, *[scale] * ways)


def forward_kernel(local, act_ref, cos_ref, sin_ref, states_ref, code_ref):
    rows, width = act_ref.shape
    tiles = width // LANES

    def block(index, carry):
        at = pl.ds(pl.multiple_of(index * STEP, STEP), STEP)
        field = []
        for tile in range(tiles):
            value = act_ref[at, tile_at(tile)].astype(jnp.float32)
            for section in range(LANE_BITS):
                other = lane_partner(value, section)
                cosine = cos_ref[section : section + 1, tile_at(tile)]
                signed = sin_ref[section : section + 1, tile_at(tile)]
                value = cosine * value + signed * other
                states_ref[section, at, tile_at(tile)] = value
            field.append(value)
        for section in range(LANE_BITS, local):
            gap = 1 << (section - LANE_BITS)
            for tile in range(tiles):
                if tile & gap:
                    continue
                cosine = cos_ref[section : section + 1, tile_at(tile)]
                signed = sin_ref[section : section + 1, tile_at(tile)]
                low, high = field[tile], field[tile + gap]
                field[tile] = cosine * low + signed * high
                field[tile + gap] = cosine * high - signed * low
            for tile in range(tiles):
                states_ref[section, at, tile_at(tile)] = field[tile]

        def store(tile, codes):
            code_ref[at, tile_at(tile)] = codes

        encode(field, store)
        return carry

    lax.fori_loop(0, rows // STEP, block, 0)


def forward_local(acts, cos_table, sin_table):
    rows, width = acts.shape
    local = cos_table.shape[0]
    block = min(rows, 32)
    table = pl.BlockSpec((local, width), lambda i: (0, 0))
    return pl.pallas_call(
        functools.partial(forward_kernel, local),
        grid=(rows // block,),
        in_specs=[pl.BlockSpec((block, width), lambda i: (i, 0)), table, table],
        out_specs=[
            pl.BlockSpec((local, block, width), lambda i: (0, i, 0)),
            pl.BlockSpec((block, width + LANES), lambda i: (i, 0)),
        ],
        out_shape=[
            jax.ShapeDtypeStruct((local, rows, width), jnp.float32),
            jax.ShapeDtypeStruct((rows, width + LANES), jnp.int16),
        ],
        cost_estimate=pl.CostEstimate(
            flops=6 * local * rows * width,
            bytes_accessed=4 * (local + 1) * rows * width,
            transcendentals=0,
        ),
        name="forward_local",
    )(acts, cos_table, sin_table)


def core_kernel(place_ref, state_ref, other_ref, trig_ref, pair_ref, *code_refs):
    width = state_ref.shape[2]
    count = len(code_refs)
    depth = state_ref.shape[1]
    tiles = width // LANES
    half = width // 2
    place = place_ref[0]
    start = place_ref[1] * half
    cosine_at = lambda at: trig_ref[0:1, at]
    signed_at = lambda at: trig_ref[1:2, at]
    for piece in range(count):
        source = place ^ piece
        mine = state_ref.at[source]
        other = other_ref.at[source]
        at = pl.ds(0, depth)
        scale = scale_of(other, at, width)
        field = []
        for tile in range(tiles):
            lanes = tile_at(tile)
            value = mine[at, lanes]
            partner = widen(other[at, lanes]) * scale
            field.append(cosine_at(lanes) * value + signed_at(lanes) * partner)

        def store(tile, codes):
            code_refs[piece][at, tile_at(tile)] = codes

        encode(field, store)
        for tile in range(tiles // 2):
            lanes = pl.ds(pl.multiple_of(start + tile * LANES, LANES), LANES)
            value = mine[at, lanes]
            partner = widen(other[at, lanes]) * scale
            cosine, signed = cosine_at(lanes), signed_at(lanes)
            pair_ref[0, source, at, tile_at(tile)] = cosine * value + signed * partner
            pair_ref[1, source, at, tile_at(tile)] = cosine * partner - signed * value


def core_forward(place, states, other, trig, count, chunks):
    local, rows, width = states.shape
    depth = rows // (chunks * count)
    view = states.reshape(local, chunks, count, depth, width)
    codes = other.reshape(chunks, count, depth, width + LANES)
    per = depth // STEP
    outs = pl.pallas_call(
        core_kernel,
        grid_spec=pltpu.PrefetchScalarGridSpec(
            num_scalar_prefetch=1,
            grid=(chunks, per),
            in_specs=[
                pl.BlockSpec(
                    (None, None, count, STEP, width), lambda i, j, p: (local - 1, i, 0, j, 0)
                ),
                pl.BlockSpec((None, count, STEP, width + LANES), lambda i, j, p: (i, 0, j, 0)),
                pl.BlockSpec((2, width), lambda i, j, p: (0, 0)),
            ],
            out_specs=[
                pl.BlockSpec((2, None, count, STEP, width // 2), lambda i, j, p: (0, i, 0, j, 0))
            ]
            + [pl.BlockSpec((STEP, width + LANES), lambda i, j, p: (i * per + j, 0))] * count,
        ),
        out_shape=[jax.ShapeDtypeStruct((2, chunks, count, depth, width // 2), jnp.float32)]
        + [jax.ShapeDtypeStruct((chunks * depth, width + LANES), jnp.int16)] * count,
        cost_estimate=pl.CostEstimate(
            flops=10 * rows * width, bytes_accessed=12 * rows * width, transcendentals=0
        ),
        name="core_forward",
    )(place, view, codes, trig)
    return outs[0].reshape(2, rows, width // 2), outs[1:]


def gather_kernel(count, place_ref, *refs):
    code_refs = refs[-count:]
    first_ref = refs[0]
    part_refs = refs[1 : -count - 1]
    words_ref = refs[-count - 1]
    width = first_ref.shape[2]
    place = place_ref[0]
    token = lax.broadcasted_iota(jnp.int32, (STEP, LANES), 0)
    for piece in range(count):
        source = place ^ piece
        values = []
        for tile in range(width // LANES):
            lanes = tile_at(tile)
            value = first_ref[source, :, lanes]
            for ref in part_refs:
                value = value + ref[source, :, lanes].astype(jnp.float32)
            words = words_ref[source, 0, :, lanes]
            bits = jnp.bitwise_and(jnp.right_shift(jnp.broadcast_to(words, token.shape), token), 1)
            values.append(value * bits.astype(jnp.float32))

        def store(tile, codes):
            code_refs[piece][:, tile_at(tile)] = codes

        encode(values, store)


def gather_parts(place, parts, words, count):
    rows, width = parts[0].shape
    depth = rows // count
    piece = pl.BlockSpec((count, STEP, width), lambda i, p: (0, i, 0))
    return pl.pallas_call(
        functools.partial(gather_kernel, count),
        grid_spec=pltpu.PrefetchScalarGridSpec(
            num_scalar_prefetch=1,
            grid=(depth // STEP,),
            in_specs=[piece] * len(parts)
            + [pl.BlockSpec((count, 1, 1, width), lambda i, p: (0, i, 0, 0))],
            out_specs=[pl.BlockSpec((STEP, width + LANES), lambda i, p: (i, 0))] * count,
        ),
        out_shape=[jax.ShapeDtypeStruct((depth, width + LANES), jnp.int16)] * count,
        cost_estimate=pl.CostEstimate(
            flops=12 * rows * width, bytes_accessed=12 * rows * width, transcendentals=0
        ),
        name="gather_parts",
    )(
        place,
        *[part.reshape(count, depth, width) for part in parts],
        words.reshape(count, depth // STEP, 1, width),
    )


def cross_kernel(count, bits, *refs):
    grad_refs = refs[:count]
    field_refs = refs[count : 2 * count]
    cos_ref, sin_ref = refs[2 * count : 2 * count + 2]
    out_refs = refs[2 * count + 2 : 3 * count + 2]
    term_ref, held_ref, sum_ref = refs[3 * count + 2 :]
    width = cos_ref.shape[2]
    tiles = width // LANES
    rows = pl.ds(0, STEP)
    index = pl.program_id(0)

    @pl.when(index == 0)
    def _():
        sum_ref[...] = jnp.zeros_like(sum_ref)

    grad_scales = [scale_of(ref, rows, width) for ref in grad_refs]
    field_scales = [scale_of(ref, rows, width) for ref in field_refs]
    for tile in range(tiles):
        lanes = tile_at(tile)
        levels = [[widen(r[rows, lanes]) * s for r, s in zip(field_refs, field_scales)]]
        for bit in range(bits - 1):
            field = list(levels[-1])
            for low in range(count):
                if low & (1 << bit):
                    continue
                high = low | (1 << bit)
                pair = drop_bit(low, bit)
                cosine = cos_ref[bit, pair : pair + 1, lanes]
                sine = sin_ref[bit, pair : pair + 1, lanes]
                v_low, v_high = field[low], field[high]
                field[low] = cosine * v_low - sine * v_high
                field[high] = sine * v_low + cosine * v_high
            levels.append(field)
        grad = [widen(r[rows, lanes]) * s for r, s in zip(grad_refs, grad_scales)]
        for bit in reversed(range(bits)):
            before = levels[bit]
            for low in range(count):
                if low & (1 << bit):
                    continue
                high = low | (1 << bit)
                pair = drop_bit(low, bit)
                cosine = cos_ref[bit, pair : pair + 1, lanes]
                sine = sin_ref[bit, pair : pair + 1, lanes]
                g_low, g_high = grad[low], grad[high]
                grad[low] = cosine * g_low + sine * g_high
                grad[high] = cosine * g_high - sine * g_low
                term = grad[high] * before[low] - grad[low] * before[high]
                sum_ref[bit, pair, :, lanes] += jnp.sum(term.reshape(STEP // 8, 8, LANES), axis=0)
        for piece in range(count):
            held_ref[piece, :, lanes] = grad[piece]

    for piece in range(count):

        def store(tile, codes):
            out_refs[piece][:, tile_at(tile)] = codes

        encode([held_ref[piece, :, tile_at(tile)] for tile in range(tiles)], store)

    @pl.when(index == pl.num_programs(0) - 1)
    def _():
        term_ref[...] = jnp.sum(sum_ref[...], axis=2)


def cross_sections(grads, fields, cos_table, sin_table, offset):
    count = len(grads)
    bits, pairs, width = cos_table.shape
    rows, wide = grads[0].shape
    piece = pl.BlockSpec((STEP, wide), lambda i: (i, 0))
    moved = pl.BlockSpec((STEP, wide), lambda i: (i + offset * (rows // STEP), 0))
    table = pl.BlockSpec(cos_table.shape, lambda i: (0, 0, 0))
    outs = pl.pallas_call(
        functools.partial(cross_kernel, count, bits),
        grid=(rows // STEP,),
        in_specs=[piece] * count + [moved] * count + [table] * 2,
        out_specs=[piece] * count + [table],
        out_shape=[jax.ShapeDtypeStruct((rows, wide), jnp.int16)] * count
        + [jax.ShapeDtypeStruct(cos_table.shape, jnp.float32)],
        scratch_shapes=[
            pltpu.VMEM((count, STEP, width), jnp.float32),
            pltpu.VMEM((bits, pairs, 8, width), jnp.float32),
        ],
        cost_estimate=pl.CostEstimate(
            flops=20 * bits * count * rows * width,
            bytes_accessed=6 * count * rows * width,
            transcendentals=0,
        ),
        name="cross_sections",
    )(*grads, *fields, cos_table, sin_table)
    return outs[:count], outs[count]


def backward_kernel(
    local, place_ref, grad_ref, other_ref, states_ref, pair_ref, trig_ref, cos_ref, sin_ref,
    hot_ref, lane_in, tile_in, core_in, whole_ref,
    out_ref, lane_out, tile_out, core_out, lane_sum, tile_sum, core_sum,
):
    rows, width = out_ref.shape
    tiles = width // LANES
    half = width // 2
    index = pl.program_id(0)
    start = place_ref[1] * half

    @pl.when(index == 0)
    def _():
        lane_sum[...] = jnp.zeros_like(lane_sum)
        tile_sum[...] = jnp.zeros_like(tile_sum)
        core_sum[...] = jnp.zeros_like(core_sum)

    def folded(value):
        return jnp.sum(value.reshape(STEP // 8, 8, LANES), axis=0)

    def block(number, carry):
        at = pl.ds(pl.multiple_of(number * STEP, STEP), STEP)
        scale = scale_of(grad_ref, at, width)
        other_scale = scale_of(other_ref, at, width)
        for tile in range(tiles // 2):
            lanes = pl.ds(pl.multiple_of(start + tile * LANES, LANES), LANES)
            mine = widen(grad_ref[at, lanes]) * scale
            partner = widen(other_ref[at, lanes]) * other_scale
            term = partner * pair_ref[0, at, tile_at(tile)] - mine * pair_ref[1, at, tile_at(tile)]
            core_sum[tile] += folded(term)
        grad = []
        for tile in range(tiles):
            lanes = tile_at(tile)
            mine = widen(grad_ref[at, lanes]) * scale
            partner = widen(other_ref[at, lanes]) * other_scale
            grad.append(trig_ref[0:1, lanes] * mine - trig_ref[1:2, lanes] * partner)
        for section in reversed(range(LANE_BITS, local)):
            gap = 1 << (section - LANE_BITS)
            for tile in range(tiles):
                if tile & gap:
                    continue
                cosine = cos_ref[section : section + 1, tile_at(tile)]
                signed = sin_ref[section : section + 1, tile_at(tile)]
                low, high = grad[tile], grad[tile + gap]
                before_low = states_ref[section, at, tile_at(tile)]
                before_high = states_ref[section, at, tile_at(tile + gap)]
                term = folded(high * before_low - low * before_high)
                place = drop_bit(tile, section - LANE_BITS)
                tile_sum[section - LANE_BITS, place] += term
                grad[tile] = cosine * low - signed * high
                grad[tile + gap] = cosine * high + signed * low
        for tile in range(tiles):
            value = grad[tile]
            for section in reversed(range(LANE_BITS)):
                cosine = cos_ref[section : section + 1, tile_at(tile)]
                signed = sin_ref[section : section + 1, tile_at(tile)]
                other = lane_partner(value, section)
                state = states_ref[section, at, tile_at(tile)]
                lane_sum[section, tile] += folded(other * state)
                value = cosine * value - signed * other
            out_ref[at, tile_at(tile)] = value.astype(out_ref.dtype)
        return carry

    lax.fori_loop(0, rows // STEP, block, 0)

    @pl.when(index == pl.num_programs(0) - 1)
    def _():
        for section in range(LANE_BITS):
            summed = jnp.sum(lane_sum[section], axis=1)
            lane_out[section] = lane_in[section] + lax.dot_general(
                summed,
                hot_ref[section],
                (((1,), (1,)), ((), ())),
                precision=HIGH,
                preferred_element_type=jnp.float32,
            )
        for section in range(local - LANE_BITS):
            tile_out[section] = tile_in[section] + jnp.sum(tile_sum[section], axis=1)
        core_out[...] = core_in[...] + jnp.sum(core_sum[...], axis=1)


def backward_local(
    place, grad, other, states, pair, trig, cos_table, sin_table, hot, sums, whole, chunk, count,
):
    depth = grad.shape[0] // count
    local, rows, width = states.shape
    tiles = width // LANES
    high = local - LANE_BITS
    base = chunk * count
    block = min(depth, 32)
    per = depth // block
    fixed = lambda shape: pl.BlockSpec(shape, lambda i, p: (0,) * len(shape))
    row_of = lambda i, p: (base + (p[0] ^ (i // per))) * per + i % per
    shapes = [(LANE_BITS, tiles, LANES // 2), (high, tiles // 2, LANES), (tiles // 2, LANES)]
    return pl.pallas_call(
        functools.partial(backward_kernel, local),
        grid_spec=pltpu.PrefetchScalarGridSpec(
            num_scalar_prefetch=1,
            grid=(count * per,),
            in_specs=[
                pl.BlockSpec((block, width + LANES), lambda i, p: (i, 0)),
                pl.BlockSpec((block, width + LANES), lambda i, p: (i, 0)),
                pl.BlockSpec((local, block, width), lambda i, p: (0, row_of(i, p), 0)),
                pl.BlockSpec((2, block, width // 2), lambda i, p: (0, row_of(i, p), 0)),
                fixed((2, width)),
                fixed((local, width)),
                fixed((local, width)),
                fixed(hot.shape),
            ]
            + [fixed(shape) for shape in shapes]
            + [pl.BlockSpec(memory_space=pl.ANY)],
            out_specs=[pl.BlockSpec((block, width), lambda i, p: (row_of(i, p), 0))]
            + [fixed(shape) for shape in shapes],
            scratch_shapes=[
                pltpu.VMEM((LANE_BITS, tiles, 8, LANES), jnp.float32),
                pltpu.VMEM((high, tiles // 2, 8, LANES), jnp.float32),
                pltpu.VMEM((tiles // 2, 8, LANES), jnp.float32),
            ],
        ),
        out_shape=[jax.ShapeDtypeStruct((rows, width), jnp.bfloat16)]
        + [jax.ShapeDtypeStruct(shape, jnp.float32) for shape in shapes],
        input_output_aliases={12: 0},
        cost_estimate=pl.CostEstimate(
            flops=8 * local * depth * count * width,
            bytes_accessed=4 * (local + 2) * depth * count * width,
            transcendentals=0,
        ),
        name="backward_local",
    )(place, grad, other, states, pair, trig, cos_table, sin_table, hot, *sums, whole)


def tree_sum(parts):
    while len(parts) > 1:
        parts = [parts[k] + parts[k + 1] for k in range(0, len(parts), 2)]
    return parts[0]


def gather_shares(value, line, core, count):
    near = jnp.stack([value] + [swap(value, "tensor", 2 * m) for m in range(1, count)])
    near = jnp.take(near, line ^ jnp.arange(count, dtype=jnp.int32), axis=0)
    other = swap(near, "tensor", 1)
    first = core == 0
    return jnp.stack([jnp.where(first, near, other), jnp.where(first, other, near)], axis=1)


def scatter_shares(value, me, bits):
    for bit in reversed(range(bits)):
        halves = value.reshape((2, -1) + value.shape[1:])
        own = (me >> bit) & 1
        value = pick(halves, own) + swap(pick(halves, 1 - own), "tensor", 1 << bit)
    return value[0]


def body(activations, angles, clip_bits, codes, exponents, cotangent):
    rows, width = activations.shape
    sections, share = angles.shape
    groups = lax.axis_size("dp")
    devices = lax.axis_size("tensor")
    ways = devices // groups
    columns = codes.shape[1]
    part = columns // ways
    local = width.bit_length() - 1
    cross = sections - local
    count = devices // 2
    me = lax.axis_index("tensor")
    mine = lax.axis_index("dp")
    level = me // ways
    core = me & 1
    line = me >> 1
    chunks = chunks_of(rows, count)
    chunk_rows = rows // chunks
    place = jnp.stack([line, core])

    gathered = []
    for q in range(chunks):
        own = cotangent[q * chunk_rows : (q + 1) * chunk_rows]
        blocks = jnp.stack([own] + [swap(own, "tensor", m * ways) for m in range(1, groups)])
        arrived = jnp.concatenate(
            [pick(blocks, level ^ mine)]
            + [swap(pick(blocks, level ^ mine ^ m), "dp", m) for m in range(1, groups)],
            axis=0,
        )
        gathered.append([arrived] + [swap(arrived, "tensor", m) for m in range(1, ways)])

    scale = jnp.exp2(exponents.astype(jnp.float32)).astype(jnp.bfloat16)
    scale = scale.reshape(-1, 1, part)
    column_place = jnp.stack([me % ways, mine * ways])

    cosine = jnp.cos(angles)
    sine = jnp.sin(angles)
    cos_table, sin_table = local_tables(cosine[:local], sine[:local], width)
    states, last_codes = forward_local(activations, cos_table, sin_table)

    trig = jnp.stack([cosine[local:], sine[local:]])
    trig = gather_shares(trig, line, core, count)
    trig = jnp.moveaxis(trig.reshape(devices, 2, cross, share), 0, 2)
    trig = trig.reshape(2, cross, devices // 2, width)
    flip = (1 - 2 * core).astype(jnp.float32)
    core_trig = lax.dynamic_index_in_dim(trig[:, 0], line, 1, keepdims=False)
    core_trig = core_trig * jnp.stack([jnp.float32(1), -flip])[:, None]
    jj = jnp.arange(count // 2, dtype=jnp.int32)
    cross_cos, cross_sin, flips = [], [], []
    for bit in range(cross - 1):
        pair = (drop_bit(line, bit) ^ jj) * 2 + core
        flips.append((1 - 2 * ((line >> bit) & 1)).astype(jnp.float32))
        cross_cos.append(jnp.take(trig[0, bit + 1], pair, axis=0))
        cross_sin.append(jnp.take(trig[1, bit + 1], pair, axis=0) * flips[-1])
    cross_cos = jnp.stack(cross_cos)
    cross_sin = jnp.stack(cross_sin)

    partner_codes = swap(last_codes, "tensor", 1)
    pair_states, fields = core_forward(place, states, partner_codes, core_trig, count, chunks)
    fields = [fields[0]] + [swap(fields[m], "tensor", 2 * m) for m in range(1, count)]

    hot, signs = lane_selectors(LANE_BITS)
    hot = -hot * signs[:, None, :]
    tiles = width // LANES
    sums = [
        jnp.zeros((LANE_BITS, tiles, LANES // 2), jnp.float32),
        jnp.zeros((local - LANE_BITS, tiles // 2, LANES), jnp.float32),
        jnp.zeros((tiles // 2, LANES), jnp.float32),
    ]
    whole = jnp.zeros((rows, width), jnp.bfloat16)
    cross_terms = []
    backs = []
    word_rows = chunk_rows // 16
    for q in range(chunks):
        sent = product(column_place, gathered[q], codes, scale, groups)
        parts = [sent[0]] + [swap(sent[m], "dp", m) for m in range(1, groups)]
        words = clip_bits[q * word_rows : (q + 1) * word_rows]
        grads = gather_parts(place, parts, words, count)
        grads = [grads[0]] + [swap(grads[m], "tensor", 2 * m) for m in range(1, count)]
        grads, terms = cross_sections(grads, fields, cross_cos, cross_sin, q)
        cross_terms.append(terms)
        backs.append([grads[0]] + [swap(grads[m], "tensor", 2 * m) for m in range(1, count)])

    for q in range(chunks):
        grad = jnp.concatenate(backs[q], axis=0)
        outs = backward_local(
            place, grad, swap(grad, "tensor", 1), states,
            pair_states, core_trig, cos_table, sin_table, hot, sums, whole, q, count,
        )
        whole, sums = outs[0], outs[1:]

    terms = functools.reduce(jnp.add, cross_terms)
    natural = jnp.stack(
        [
            jnp.take(terms[bit], drop_bit(line, bit) ^ jj, axis=0) * flips[bit]
            for bit in range(cross - 1)
        ]
    )
    natural = natural.reshape(cross - 1, count // 2, 1, 2, share)
    natural = jnp.where(
        jnp.arange(2, dtype=jnp.int32)[None, None, :, None, None] == core, natural, 0.0
    )
    natural = jnp.moveaxis(natural.reshape(cross - 1, devices, share), 1, 0)
    owned = scatter_shares(natural, me, cross)

    final = jnp.concatenate(
        [
            sums[0].reshape(LANE_BITS, share),
            sums[1].reshape(local - LANE_BITS, share),
            sums[2].reshape(1, share) * flip,
            owned,
        ],
        axis=0,
    )
    angle_grad = tree_sum([final] + [swap(final, "dp", m) for m in range(1, groups)])
    return (whole, angle_grad)


def chunks_of(rows, count):
    chunks = CHUNKS
    while rows // (chunks * count) < STEP:
        chunks //= 2
    return chunks


def solution(mesh):
    placed = (
        P("dp", "tensor"),
        P(None, "tensor"),
        P("dp", "tensor"),
        P("tensor", "dp"),
        P(),
        P("dp", "tensor"),
    )

    return jax.shard_map(
        body,
        mesh=mesh,
        in_specs=placed,
        out_specs=(P("dp", "tensor"), P(None, "tensor")),
        check_vma=False,
    )
```

```python
import functools

import jax
import jax.numpy as jnp
from jax import lax
from jax.experimental import pallas as pl
from jax.experimental.pallas import tpu as pltpu
from jax.sharding import PartitionSpec as P


LANES = 128
LANE_BITS = 7
HIGH = lax.Precision.HIGHEST


CHUNKS = 2
STEP = 16
FRACTION = 14.0


def swap(value, axis, mask):
    pairs = [(source, source ^ mask) for source in range(lax.axis_size(axis))]
    return lax.ppermute(value, axis, pairs)


def pick(stacked, index):
    return lax.dynamic_index_in_dim(stacked, index, 0, keepdims=False)


def drop_bit(index, bit):
    return ((index >> (bit + 1)) << bit) | (index & ((1 << bit) - 1))


def lane_selectors(sections):
    lane = jnp.arange(LANES, dtype=jnp.int32)
    rows = []
    signs = []
    for section in range(sections):
        pair = drop_bit(lane, section)
        hot = pair[None, :] == jnp.arange(LANES // 2, dtype=jnp.int32)[:, None]
        rows.append(hot.astype(jnp.float32))
        signs.append(jnp.where((lane >> section) & 1 == 0, -1.0, 1.0).astype(jnp.float32))
    return jnp.stack(rows), jnp.stack(signs)


def local_tables(cosine, sine, width):
    local = cosine.shape[0]
    tiles = width // LANES
    hot, signs = lane_selectors(LANE_BITS)

    def lanes(values):
        shaped = values[:LANE_BITS].reshape(LANE_BITS, tiles, LANES // 2)
        return jnp.einsum("stk,skl->stl", shaped, hot, precision=HIGH)

    def whole(section, values, sign):
        step = 1 << (section - LANE_BITS)
        shaped = values.reshape(tiles // (2 * step), 1, step, LANES)
        return jnp.concatenate([sign * shaped, shaped], axis=1).reshape(1, tiles, LANES)

    cos_rows = [lanes(cosine)]
    sin_rows = [lanes(sine) * signs[:, None, :]]
    for section in range(LANE_BITS, local):
        cos_rows.append(whole(section, cosine[section], 1.0))
        sin_rows.append(whole(section, sine[section], -1.0))
    cos_table = jnp.concatenate(cos_rows, axis=0).reshape(local, width)
    sin_table = jnp.concatenate(sin_rows, axis=0).reshape(local, width)
    return cos_table, sin_table


def lane_partner(value, section):
    half = 1 << section
    lane = lax.broadcasted_iota(jnp.int32, value.shape, 1)
    up = pltpu.roll(value, half, 1)
    if 2 * half == LANES:
        return up
    down = pltpu.roll(value, LANES - half, 1)
    return jnp.where((lane & half) == 0, down, up)


def tile_at(tile):
    return pl.ds(tile * LANES, LANES)


def encode(values, store):
    most = functools.reduce(jnp.maximum, [jnp.abs(value) for value in values])
    most = jnp.max(most, axis=1, keepdims=True)
    power = jnp.ceil(jnp.log2(jnp.maximum(most, 1e-30)))
    factor = jnp.exp2(FRACTION - power)
    for tile, value in enumerate(values):
        store(tile, jnp.round(value * factor).astype(jnp.int32).astype(jnp.int16))
    power = jnp.broadcast_to(power, values[0].shape)
    store(len(values), power.astype(jnp.int32).astype(jnp.int16))


def widen(codes):
    return codes.astype(jnp.int32).astype(jnp.float32)


def scale_of(ref, at, width):
    return jnp.exp2(widen(ref[at, pl.ds(width, LANES)]) - FRACTION)


def product_kernel(ways, place_ref, *refs):
    outs = (len(refs) - 3 * ways) // (ways + 1)
    token_refs = refs[: ways * outs]
    code_refs = refs[ways * outs : ways * (outs + 1)]
    scale_refs = refs[ways * (outs + 1) : ways * (outs + 2)]
    out_refs = refs[ways * (outs + 2) : -ways]
    joined_refs = refs[-ways:]
    rows = out_refs[0].shape[0]

    @pl.when(pl.program_id(0) == 0)
    def _():
        for way, joined in enumerate(joined_refs):
            for index in range(outs):
                joined[pl.ds(index * rows, rows), :] = token_refs[way * outs + index][...]

    total = None
    for joined, codes, scale in zip(joined_refs, code_refs, scale_refs):
        part = lax.dot_general(
            joined[...],
            codes[...] * scale[0],
            (((1,), (1,)), ((), ())),
            preferred_element_type=jnp.float32,
        )
        total = part if total is None else total + part
    for index, ref in enumerate(out_refs):
        ref[...] = total[index * rows : (index + 1) * rows].astype(ref.dtype)


def product(place, tokens, codes, scale):
    ways, outs = len(tokens), len(tokens[0])
    width = codes.shape[0]
    rows, part = tokens[0][0].shape
    block = min(width, 512)
    code_spec = lambda j: pl.BlockSpec((block, part), lambda i, p: (i, p[0] ^ j))
    scale_spec = lambda j: pl.BlockSpec((1, 1, part), lambda i, p: (p[1] + (p[0] ^ j), 0, 0))
    return pl.pallas_call(
        functools.partial(product_kernel, ways),
        grid_spec=pltpu.PrefetchScalarGridSpec(
            num_scalar_prefetch=1,
            grid=(width // block,),
            in_specs=[pl.BlockSpec((rows, part), lambda i, p: (0, 0))] * (ways * outs)
            + [code_spec(j) for j in range(ways)]
            + [scale_spec(j) for j in range(ways)],
            out_specs=[pl.BlockSpec((rows, block), lambda i, p: (0, i))] * outs,
            scratch_shapes=[pltpu.VMEM((rows * outs, part), jnp.bfloat16)] * ways,
        ),
        out_shape=[jax.ShapeDtypeStruct((rows, width), jnp.float32)]
        + [jax.ShapeDtypeStruct((rows, width), jnp.bfloat16)] * (outs - 1),
        cost_estimate=pl.CostEstimate(
            flops=2 * rows * outs * part * ways * width,
            bytes_accessed=2 * part * ways * width,
            transcendentals=0,
        ),
        name="product",
    )(place, *[x for way in tokens for x in way], *[codes] * ways, *[scale] * ways)


def forward_kernel(local, act_ref, cos_ref, sin_ref, states_ref, code_ref):
    rows, width = act_ref.shape
    tiles = width // LANES

    def block(index, carry):
        at = pl.ds(pl.multiple_of(index * STEP, STEP), STEP)
        field = []
        for tile in range(tiles):
            value = act_ref[at, tile_at(tile)].astype(jnp.float32)
            for section in range(LANE_BITS):
                other = lane_partner(value, section)
                cosine = cos_ref[section : section + 1, tile_at(tile)]
                signed = sin_ref[section : section + 1, tile_at(tile)]
                value = cosine * value + signed * other
                states_ref[section, at, tile_at(tile)] = value
            field.append(value)
        for section in range(LANE_BITS, local):
            gap = 1 << (section - LANE_BITS)
            for tile in range(tiles):
                if tile & gap:
                    continue
                cosine = cos_ref[section : section + 1, tile_at(tile)]
                signed = sin_ref[section : section + 1, tile_at(tile)]
                low, high = field[tile], field[tile + gap]
                field[tile] = cosine * low + signed * high
                field[tile + gap] = cosine * high - signed * low
            for tile in range(tiles):
                states_ref[section, at, tile_at(tile)] = field[tile]

        def store(tile, codes):
            code_ref[at, tile_at(tile)] = codes

        encode(field, store)
        return carry

    lax.fori_loop(0, rows // STEP, block, 0)


def forward_local(acts, cos_table, sin_table):
    rows, width = acts.shape
    local = cos_table.shape[0]
    block = min(rows, 32)
    table = pl.BlockSpec((local, width), lambda i: (0, 0))
    return pl.pallas_call(
        functools.partial(forward_kernel, local),
        grid=(rows // block,),
        in_specs=[pl.BlockSpec((block, width), lambda i: (i, 0)), table, table],
        out_specs=[
            pl.BlockSpec((local, block, width), lambda i: (0, i, 0)),
            pl.BlockSpec((block, width + LANES), lambda i: (i, 0)),
        ],
        out_shape=[
            jax.ShapeDtypeStruct((local, rows, width), jnp.float32),
            jax.ShapeDtypeStruct((rows, width + LANES), jnp.int16),
        ],
        cost_estimate=pl.CostEstimate(
            flops=6 * local * rows * width,
            bytes_accessed=4 * (local + 1) * rows * width,
            transcendentals=0,
        ),
        name="forward_local",
    )(acts, cos_table, sin_table)


def core_kernel(place_ref, state_ref, other_ref, trig_ref, pair_ref, *code_refs):
    width = state_ref.shape[2]
    count = len(code_refs)
    depth = state_ref.shape[1]
    tiles = width // LANES
    half = width // 2
    place = place_ref[0]
    start = place_ref[1] * half
    cosine_at = lambda at: trig_ref[0:1, at]
    signed_at = lambda at: trig_ref[1:2, at]
    for piece in range(count):
        source = place ^ piece
        mine = state_ref.at[source]
        other = other_ref.at[source]
        at = pl.ds(0, depth)
        scale = scale_of(other, at, width)
        field = []
        for tile in range(tiles):
            lanes = tile_at(tile)
            value = mine[at, lanes]
            partner = widen(other[at, lanes]) * scale
            field.append(cosine_at(lanes) * value + signed_at(lanes) * partner)

        def store(tile, codes):
            code_refs[piece][at, tile_at(tile)] = codes

        encode(field, store)
        for tile in range(tiles // 2):
            lanes = pl.ds(pl.multiple_of(start + tile * LANES, LANES), LANES)
            value = mine[at, lanes]
            partner = widen(other[at, lanes]) * scale
            cosine, signed = cosine_at(lanes), signed_at(lanes)
            pair_ref[0, source, at, tile_at(tile)] = cosine * value + signed * partner
            pair_ref[1, source, at, tile_at(tile)] = cosine * partner - signed * value


def core_forward(place, states, other, trig, count, chunks):
    local, rows, width = states.shape
    depth = rows // (chunks * count)
    view = states.reshape(local, chunks, count, depth, width)
    codes = other.reshape(chunks, count, depth, width + LANES)
    per = depth // STEP
    outs = pl.pallas_call(
        core_kernel,
        grid_spec=pltpu.PrefetchScalarGridSpec(
            num_scalar_prefetch=1,
            grid=(chunks, per),
            in_specs=[
                pl.BlockSpec(
                    (None, None, count, STEP, width), lambda i, j, p: (local - 1, i, 0, j, 0)
                ),
                pl.BlockSpec((None, count, STEP, width + LANES), lambda i, j, p: (i, 0, j, 0)),
                pl.BlockSpec((2, width), lambda i, j, p: (0, 0)),
            ],
            out_specs=[
                pl.BlockSpec((2, None, count, STEP, width // 2), lambda i, j, p: (0, i, 0, j, 0))
            ]
            + [pl.BlockSpec((STEP, width + LANES), lambda i, j, p: (i * per + j, 0))] * count,
        ),
        out_shape=[jax.ShapeDtypeStruct((2, chunks, count, depth, width // 2), jnp.float32)]
        + [jax.ShapeDtypeStruct((chunks * depth, width + LANES), jnp.int16)] * count,
        cost_estimate=pl.CostEstimate(
            flops=10 * rows * width, bytes_accessed=12 * rows * width, transcendentals=0
        ),
        name="core_forward",
    )(place, view, codes, trig)
    return outs[0].reshape(2, rows, width // 2), outs[1:]


def gather_kernel(count, place_ref, *refs):
    code_refs = refs[-count:]
    first_ref = refs[0]
    part_refs = refs[1 : -count - 1]
    words_ref = refs[-count - 1]
    width = first_ref.shape[2]
    place = place_ref[0]
    token = lax.broadcasted_iota(jnp.int32, (STEP, LANES), 0)
    for piece in range(count):
        source = place ^ piece
        values = []
        for tile in range(width // LANES):
            lanes = tile_at(tile)
            value = first_ref[source, :, lanes]
            for ref in part_refs:
                value = value + ref[source, :, lanes].astype(jnp.float32)
            words = words_ref[source, 0, :, lanes]
            bits = jnp.bitwise_and(jnp.right_shift(jnp.broadcast_to(words, token.shape), token), 1)
            values.append(value * bits.astype(jnp.float32))

        def store(tile, codes):
            code_refs[piece][:, tile_at(tile)] = codes

        encode(values, store)


def gather_parts(place, parts, words, count):
    rows, width = parts[0].shape
    depth = rows // count
    piece = pl.BlockSpec((count, STEP, width), lambda i, p: (0, i, 0))
    return pl.pallas_call(
        functools.partial(gather_kernel, count),
        grid_spec=pltpu.PrefetchScalarGridSpec(
            num_scalar_prefetch=1,
            grid=(depth // STEP,),
            in_specs=[piece] * len(parts)
            + [pl.BlockSpec((count, 1, 1, width), lambda i, p: (0, i, 0, 0))],
            out_specs=[pl.BlockSpec((STEP, width + LANES), lambda i, p: (i, 0))] * count,
        ),
        out_shape=[jax.ShapeDtypeStruct((depth, width + LANES), jnp.int16)] * count,
        cost_estimate=pl.CostEstimate(
            flops=12 * rows * width, bytes_accessed=12 * rows * width, transcendentals=0
        ),
        name="gather_parts",
    )(
        place,
        *[part.reshape(count, depth, width) for part in parts],
        words.reshape(count, depth // STEP, 1, width),
    )


def cross_kernel(count, bits, *refs):
    grad_refs = refs[:count]
    field_refs = refs[count : 2 * count]
    cos_ref, sin_ref = refs[2 * count : 2 * count + 2]
    out_refs = refs[2 * count + 2 : 3 * count + 2]
    term_ref, held_ref, sum_ref = refs[3 * count + 2 :]
    width = cos_ref.shape[2]
    tiles = width // LANES
    rows = pl.ds(0, STEP)
    index = pl.program_id(0)

    @pl.when(index == 0)
    def _():
        sum_ref[...] = jnp.zeros_like(sum_ref)

    grad_scales = [scale_of(ref, rows, width) for ref in grad_refs]
    field_scales = [scale_of(ref, rows, width) for ref in field_refs]
    for tile in range(tiles):
        lanes = tile_at(tile)
        levels = [[widen(r[rows, lanes]) * s for r, s in zip(field_refs, field_scales)]]
        for bit in range(bits - 1):
            field = list(levels[-1])
            for low in range(count):
                if low & (1 << bit):
                    continue
                high = low | (1 << bit)
                pair = drop_bit(low, bit)
                cosine = cos_ref[bit, pair : pair + 1, lanes]
                sine = sin_ref[bit, pair : pair + 1, lanes]
                v_low, v_high = field[low], field[high]
                field[low] = cosine * v_low - sine * v_high
                field[high] = sine * v_low + cosine * v_high
            levels.append(field)
        grad = [widen(r[rows, lanes]) * s for r, s in zip(grad_refs, grad_scales)]
        for bit in reversed(range(bits)):
            before = levels[bit]
            for low in range(count):
                if low & (1 << bit):
                    continue
                high = low | (1 << bit)
                pair = drop_bit(low, bit)
                cosine = cos_ref[bit, pair : pair + 1, lanes]
                sine = sin_ref[bit, pair : pair + 1, lanes]
                g_low, g_high = grad[low], grad[high]
                grad[low] = cosine * g_low + sine * g_high
                grad[high] = cosine * g_high - sine * g_low
                term = grad[high] * before[low] - grad[low] * before[high]
                sum_ref[bit, pair, :, lanes] += jnp.sum(term.reshape(STEP // 8, 8, LANES), axis=0)
        for piece in range(count):
            held_ref[piece, :, lanes] = grad[piece]

    for piece in range(count):

        def store(tile, codes):
            out_refs[piece][:, tile_at(tile)] = codes

        encode([held_ref[piece, :, tile_at(tile)] for tile in range(tiles)], store)

    @pl.when(index == pl.num_programs(0) - 1)
    def _():
        term_ref[...] = jnp.sum(sum_ref[...], axis=2)


def cross_sections(grads, fields, cos_table, sin_table, offset):
    count = len(grads)
    bits, pairs, width = cos_table.shape
    rows, wide = grads[0].shape
    piece = pl.BlockSpec((STEP, wide), lambda i: (i, 0))
    moved = pl.BlockSpec((STEP, wide), lambda i: (i + offset * (rows // STEP), 0))
    table = pl.BlockSpec(cos_table.shape, lambda i: (0, 0, 0))
    outs = pl.pallas_call(
        functools.partial(cross_kernel, count, bits),
        grid=(rows // STEP,),
        in_specs=[piece] * count + [moved] * count + [table] * 2,
        out_specs=[piece] * count + [table],
        out_shape=[jax.ShapeDtypeStruct((rows, wide), jnp.int16)] * count
        + [jax.ShapeDtypeStruct(cos_table.shape, jnp.float32)],
        scratch_shapes=[
            pltpu.VMEM((count, STEP, width), jnp.float32),
            pltpu.VMEM((bits, pairs, 8, width), jnp.float32),
        ],
        cost_estimate=pl.CostEstimate(
            flops=20 * bits * count * rows * width,
            bytes_accessed=6 * count * rows * width,
            transcendentals=0,
        ),
        name="cross_sections",
    )(*grads, *fields, cos_table, sin_table)
    return outs[:count], outs[count]


def backward_kernel(local, count, per, place_ref, *refs):
    grad_refs = refs[:count]
    other_refs = refs[count : 2 * count]
    states_ref, pair_ref, trig_ref, cos_ref, sin_ref, hot_ref, term_in, _ = refs[
        2 * count : 2 * count + 8
    ]
    out_ref, term_out, grad_ref, other_ref, lane_sum, tile_sum, core_sum = refs[2 * count + 8 :]
    rows, width = out_ref.shape
    tiles = width // LANES
    half = width // 2
    index = pl.program_id(0)
    start = place_ref[1] * half

    @pl.when(index == 0)
    def _():
        lane_sum[...] = jnp.zeros_like(lane_sum)
        tile_sum[...] = jnp.zeros_like(tile_sum)
        core_sum[...] = jnp.zeros_like(core_sum)

    for piece in range(count):

        @pl.when(index // per == piece)
        def _():
            at = pl.ds(pl.multiple_of((index % per) * rows, rows), rows)
            grad_ref[...] = grad_refs[piece][at, :]
            other_ref[...] = other_refs[piece][at, :]

    def folded(value):
        return jnp.sum(value.reshape(STEP // 8, 8, LANES), axis=0)

    def block(number, carry):
        at = pl.ds(pl.multiple_of(number * STEP, STEP), STEP)
        scale = scale_of(grad_ref, at, width)
        other_scale = scale_of(other_ref, at, width)
        for tile in range(tiles // 2):
            lanes = pl.ds(pl.multiple_of(start + tile * LANES, LANES), LANES)
            mine = widen(grad_ref[at, lanes]) * scale
            partner = widen(other_ref[at, lanes]) * other_scale
            term = partner * pair_ref[0, at, tile_at(tile)] - mine * pair_ref[1, at, tile_at(tile)]
            core_sum[tile] += folded(term)
        grad = []
        for tile in range(tiles):
            lanes = tile_at(tile)
            mine = widen(grad_ref[at, lanes]) * scale
            partner = widen(other_ref[at, lanes]) * other_scale
            grad.append(trig_ref[0:1, lanes] * mine - trig_ref[1:2, lanes] * partner)
        for section in reversed(range(LANE_BITS, local)):
            gap = 1 << (section - LANE_BITS)
            for tile in range(tiles):
                if tile & gap:
                    continue
                cosine = cos_ref[section : section + 1, tile_at(tile)]
                signed = sin_ref[section : section + 1, tile_at(tile)]
                low, high = grad[tile], grad[tile + gap]
                before_low = states_ref[section, at, tile_at(tile)]
                before_high = states_ref[section, at, tile_at(tile + gap)]
                term = folded(high * before_low - low * before_high)
                place = drop_bit(tile, section - LANE_BITS)
                tile_sum[section - LANE_BITS, place] += term
                grad[tile] = cosine * low - signed * high
                grad[tile + gap] = cosine * high + signed * low
        for tile in range(tiles):
            value = grad[tile]
            for section in reversed(range(LANE_BITS)):
                cosine = cos_ref[section : section + 1, tile_at(tile)]
                signed = sin_ref[section : section + 1, tile_at(tile)]
                other = lane_partner(value, section)
                state = states_ref[section, at, tile_at(tile)]
                lane_sum[section, tile % 2, tile // 2] += folded(other * state)
                value = cosine * value - signed * other
            out_ref[at, tile_at(tile)] = value.astype(out_ref.dtype)
        return carry

    lax.fori_loop(0, rows // STEP, block, 0)

    @pl.when(index == pl.num_programs(0) - 1)
    def _():
        for section in range(LANE_BITS):
            terms = term_in[section]
            for parity in range(2):
                terms += lax.dot_general(
                    jnp.sum(lane_sum[section, parity], axis=1),
                    hot_ref[section, parity],
                    (((1,), (1,)), ((), ())),
                    precision=HIGH,
                    preferred_element_type=jnp.float32,
                )
            term_out[section] = terms
        for section in range(LANE_BITS, local):
            term_out[section] = term_in[section] + jnp.sum(tile_sum[section - LANE_BITS], axis=1)
        flip = (1 - 2 * place_ref[1]).astype(jnp.float32)
        term_out[local] = term_in[local] + flip * jnp.sum(core_sum[...], axis=1)


def backward_local(
    place, grads, others, states, pair, trig, cos_table, sin_table, hot, terms, whole, chunk
):
    count = len(grads)
    depth = grads[0].shape[0]
    local, rows, width = states.shape
    tiles = width // LANES
    high = local - LANE_BITS
    base = chunk * count
    block = min(depth, 32)
    per = depth // block
    fixed = lambda shape: pl.BlockSpec(shape, lambda i, p: (0,) * len(shape))
    row_of = lambda i, p: (base + (p[0] ^ (i // per))) * per + i % per
    return pl.pallas_call(
        functools.partial(backward_kernel, local, count, per),
        grid_spec=pltpu.PrefetchScalarGridSpec(
            num_scalar_prefetch=1,
            grid=(count * per,),
            in_specs=[fixed((depth, width + LANES))] * (2 * count)
            + [
                pl.BlockSpec((local, block, width), lambda i, p: (0, row_of(i, p), 0)),
                pl.BlockSpec((2, block, width // 2), lambda i, p: (0, row_of(i, p), 0)),
                fixed((2, width)),
                fixed((local, width)),
                fixed((local, width)),
                fixed(hot.shape),
                fixed(terms.shape),
                pl.BlockSpec(memory_space=pl.ANY),
            ],
            out_specs=[
                pl.BlockSpec((block, width), lambda i, p: (row_of(i, p), 0)),
                fixed(terms.shape),
            ],
            scratch_shapes=[
                pltpu.VMEM((block, width + LANES), jnp.int16),
                pltpu.VMEM((block, width + LANES), jnp.int16),
                pltpu.VMEM((LANE_BITS, 2, tiles // 2, 8, LANES), jnp.float32),
                pltpu.VMEM((high, tiles // 2, 8, LANES), jnp.float32),
                pltpu.VMEM((tiles // 2, 8, LANES), jnp.float32),
            ],
        ),
        out_shape=[
            jax.ShapeDtypeStruct((rows, width), jnp.bfloat16),
            jax.ShapeDtypeStruct(terms.shape, jnp.float32),
        ],
        input_output_aliases={2 * count + 8: 0},
        cost_estimate=pl.CostEstimate(
            flops=8 * local * depth * count * width,
            bytes_accessed=4 * (local + 2) * depth * count * width,
            transcendentals=0,
        ),
        name="backward_local",
    )(place, *grads, *others, states, pair, trig, cos_table, sin_table, hot, terms, whole)


def tree_sum(parts):
    while len(parts) > 1:
        parts = [parts[k] + parts[k + 1] for k in range(0, len(parts), 2)]
    return parts[0]


def gather_shares(value, line, core, count):
    near = jnp.stack([value] + [swap(value, "tensor", 2 * m) for m in range(1, count)])
    near = jnp.take(near, line ^ jnp.arange(count, dtype=jnp.int32), axis=0)
    other = swap(near, "tensor", 1)
    first = core == 0
    return jnp.stack([jnp.where(first, near, other), jnp.where(first, other, near)], axis=1)


def scatter_shares(value, me, bits):
    for bit in reversed(range(bits)):
        halves = value.reshape((2, -1) + value.shape[1:])
        own = (me >> bit) & 1
        value = pick(halves, own) + swap(pick(halves, 1 - own), "tensor", 1 << bit)
    return value[0]


def body(activations, angles, clip_bits, codes, exponents, cotangent):
    rows, width = activations.shape
    sections, share = angles.shape
    groups = lax.axis_size("dp")
    devices = lax.axis_size("tensor")
    ways = devices // groups
    columns = codes.shape[1]
    part = columns // ways
    local = width.bit_length() - 1
    cross = sections - local
    count = devices // 2
    me = lax.axis_index("tensor")
    mine = lax.axis_index("dp")
    level = me // ways
    core = me & 1
    line = me >> 1
    chunks = chunks_of(rows, count)
    chunk_rows = rows // chunks
    place = jnp.stack([line, core])

    gathered = []
    for q in range(chunks):
        own = cotangent[q * chunk_rows : (q + 1) * chunk_rows]
        blocks = jnp.stack([own] + [swap(own, "tensor", m * ways) for m in range(1, groups)])
        arrived = [pick(blocks, level ^ mine)] + [
            swap(pick(blocks, level ^ mine ^ m), "dp", m) for m in range(1, groups)
        ]
        gathered.append(
            [arrived]
            + [[swap(x, "tensor", m) for x in arrived] for m in range(1, ways)]
        )

    scale = jnp.exp2(exponents.astype(jnp.float32)).astype(jnp.bfloat16)
    scale = scale.reshape(-1, 1, part)
    column_place = jnp.stack([me % ways, mine * ways])

    cosine = jnp.cos(angles)
    sine = jnp.sin(angles)
    cos_table, sin_table = local_tables(cosine[:local], sine[:local], width)
    states, last_codes = forward_local(activations, cos_table, sin_table)

    trig = jnp.stack([cosine[local:], sine[local:]])
    trig = gather_shares(trig, line, core, count)
    trig = jnp.moveaxis(trig.reshape(devices, 2, cross, share), 0, 2)
    trig = trig.reshape(2, cross, devices // 2, width)
    flip = (1 - 2 * core).astype(jnp.float32)
    core_trig = lax.dynamic_index_in_dim(trig[:, 0], line, 1, keepdims=False)
    core_trig = core_trig * jnp.stack([jnp.float32(1), -flip])[:, None]
    jj = jnp.arange(count // 2, dtype=jnp.int32)
    cross_cos, cross_sin, flips = [], [], []
    for bit in range(cross - 1):
        pair = (drop_bit(line, bit) ^ jj) * 2 + core
        flips.append((1 - 2 * ((line >> bit) & 1)).astype(jnp.float32))
        cross_cos.append(jnp.take(trig[0, bit + 1], pair, axis=0))
        cross_sin.append(jnp.take(trig[1, bit + 1], pair, axis=0) * flips[-1])
    cross_cos = jnp.stack(cross_cos)
    cross_sin = jnp.stack(cross_sin)

    partner_codes = swap(last_codes, "tensor", 1)
    pair_states, fields = core_forward(place, states, partner_codes, core_trig, count, chunks)
    fields = [fields[0]] + [swap(fields[m], "tensor", 2 * m) for m in range(1, count)]

    hot, signs = lane_selectors(LANE_BITS)
    hot = -hot * signs[:, None, :]
    empty = jnp.zeros_like(hot)
    hot = jnp.stack(
        [jnp.concatenate([hot, empty], axis=1), jnp.concatenate([empty, hot], axis=1)], axis=1
    )
    local_terms = jnp.zeros((local + 1, share // LANES, LANES), jnp.float32)
    whole = jnp.zeros((rows, width), jnp.bfloat16)
    cross_terms = []
    backs = []
    word_rows = chunk_rows // 16
    for q in range(chunks):
        sent = product(column_place, gathered[q], codes, scale)
        parts = [sent[0]] + [swap(sent[m], "dp", m) for m in range(1, groups)]
        words = clip_bits[q * word_rows : (q + 1) * word_rows]
        grads = gather_parts(place, parts, words, count)
        grads = [grads[0]] + [swap(grads[m], "tensor", 2 * m) for m in range(1, count)]
        grads, terms = cross_sections(grads, fields, cross_cos, cross_sin, q)
        cross_terms.append(terms)
        backs.append([grads[0]] + [swap(grads[m], "tensor", 2 * m) for m in range(1, count)])

    for q in range(chunks):
        others = [swap(grad, "tensor", 1) for grad in backs[q]]
        whole, local_terms = backward_local(
            place, backs[q], others, states, pair_states, core_trig,
            cos_table, sin_table, hot, local_terms, whole, q,
        )

    terms = functools.reduce(jnp.add, cross_terms)
    natural = jnp.stack(
        [
            jnp.take(terms[bit], drop_bit(line, bit) ^ jj, axis=0) * flips[bit]
            for bit in range(cross - 1)
        ]
    )
    natural = natural.reshape(cross - 1, count // 2, 1, 2, share)
    natural = jnp.where(
        jnp.arange(2, dtype=jnp.int32)[None, None, :, None, None] == core, natural, 0.0
    )
    natural = jnp.moveaxis(natural.reshape(cross - 1, devices, share), 1, 0)
    owned = scatter_shares(natural, me, cross)

    owned = owned.reshape(cross - 1, share // LANES, LANES)
    final = jnp.concatenate([local_terms, owned], axis=0)
    angle_grad = tree_sum([final] + [swap(final, "dp", m) for m in range(1, groups)])
    angle_grad = angle_grad.reshape(sections, share)
    return (whole, angle_grad)


def chunks_of(rows, count):
    chunks = CHUNKS
    while rows // (chunks * count) < STEP:
        chunks //= 2
    return chunks


def solution(mesh):
    placed = (
        P("dp", "tensor"),
        P(None, "tensor"),
        P("dp", "tensor"),
        P("tensor", "dp"),
        P(),
        P("dp", "tensor"),
    )

    return jax.shard_map(
        body,
        mesh=mesh,
        in_specs=placed,
        out_specs=(P("dp", "tensor"), P(None, "tensor")),
        check_vma=False,
    )
```

```python
import functools

import jax
import jax.numpy as jnp
from jax import lax
from jax.experimental import pallas as pl
from jax.experimental.pallas import tpu as pltpu
from jax.sharding import PartitionSpec as P


LANES = 128
LANE_BITS = 7


CHUNKS = 2
STEP = 16
FRACTION = 14.0
GROUP = 2


def swap(value, axis, mask):
    pairs = [(source, source ^ mask) for source in range(lax.axis_size(axis))]
    return lax.ppermute(value, axis, pairs)


def pick(stacked, index):
    return lax.dynamic_index_in_dim(stacked, index, 0, keepdims=False)


def drop_bit(index, bit):
    return ((index >> (bit + 1)) << bit) | (index & ((1 << bit) - 1))


def spread_matrix():
    first = jnp.arange(2 * LANES, dtype=jnp.int32)[:, None]
    second = jnp.arange(2 * LANES, dtype=jnp.int32)[None, :]
    lane, part = first % LANES, first // LANES
    feature, row = second % LANES, second // LANES
    hit = (lane == row * (LANES // 2) + feature // 2) & (part == feature % 2)
    return hit.astype(jnp.bfloat16)


def local_tables(cosine, sine, width):
    local = cosine.shape[0]
    tiles = width // LANES

    def lanes(values):
        shaped = values[:LANE_BITS].reshape(LANE_BITS, tiles, LANES // 2)
        return jnp.concatenate([shaped, shaped], axis=2)

    def whole(section, values, sign):
        step = 1 << (section - LANE_BITS)
        shaped = values.reshape(tiles // (2 * step), 1, step, LANES)
        return jnp.concatenate([sign * shaped, shaped], axis=1).reshape(1, tiles, LANES)

    cos_rows = [lanes(cosine)]
    sin_rows = [lanes(sine)]
    for section in range(LANE_BITS, local):
        cos_rows.append(whole(section, cosine[section], 1.0))
        sin_rows.append(whole(section, sine[section], -1.0))
    cos_table = jnp.concatenate(cos_rows, axis=0).reshape(local, width)
    sin_table = jnp.concatenate(sin_rows, axis=0).reshape(local, width)
    return cos_table, sin_table


def trade(first, second, section):
    half = 1 << section
    lane = lax.broadcasted_iota(jnp.int32, first.shape, 1)
    low = (lane & half) == 0
    up = pltpu.roll(second, half, 1)
    down = pltpu.roll(first, LANES - half, 1)
    return jnp.where(low, first, up), jnp.where(low, down, second)


def tile_at(tile):
    return pl.ds(tile * LANES, LANES)


def encode(values, store):
    most = functools.reduce(jnp.maximum, [jnp.abs(value) for value in values])
    most = jnp.max(most, axis=1, keepdims=True)
    power = jnp.ceil(jnp.log2(jnp.maximum(most, 1e-30)))
    factor = jnp.exp2(FRACTION - power)
    for tile, value in enumerate(values):
        store(tile, jnp.round(value * factor).astype(jnp.int32).astype(jnp.int16))
    power = jnp.broadcast_to(power, values[0].shape)
    store(len(values), power.astype(jnp.int32).astype(jnp.int16))


def widen(codes):
    return codes.astype(jnp.int32).astype(jnp.float32)


def scale_of(ref, at, width):
    return jnp.exp2(widen(ref[at, pl.ds(width, LANES)]) - FRACTION)


def product_kernel(ways, place_ref, *refs):
    outs = (len(refs) - 3 * ways) // (ways + 1)
    token_refs = refs[: ways * outs]
    code_refs = refs[ways * outs : ways * (outs + 1)]
    scale_refs = refs[ways * (outs + 1) : ways * (outs + 2)]
    out_refs = refs[ways * (outs + 2) : -ways]
    joined_refs = refs[-ways:]
    rows = out_refs[0].shape[0]

    @pl.when(pl.program_id(0) == 0)
    def _():
        for way, joined in enumerate(joined_refs):
            for index in range(outs):
                joined[pl.ds(index * rows, rows), :] = token_refs[way * outs + index][...]

    total = None
    for joined, codes, scale in zip(joined_refs, code_refs, scale_refs):
        part = lax.dot_general(
            joined[...],
            codes[...] * scale[0],
            (((1,), (1,)), ((), ())),
            preferred_element_type=jnp.float32,
        )
        total = part if total is None else total + part
    for index, ref in enumerate(out_refs):
        ref[...] = total[index * rows : (index + 1) * rows].astype(ref.dtype)


def product(place, tokens, codes, scale):
    ways, outs = len(tokens), len(tokens[0])
    width = codes.shape[0]
    rows, part = tokens[0][0].shape
    block = min(width, 512)
    code_spec = lambda j: pl.BlockSpec((block, part), lambda i, p: (i, p[0] ^ j))
    scale_spec = lambda j: pl.BlockSpec((1, 1, part), lambda i, p: (p[1] + (p[0] ^ j), 0, 0))
    return pl.pallas_call(
        functools.partial(product_kernel, ways),
        grid_spec=pltpu.PrefetchScalarGridSpec(
            num_scalar_prefetch=1,
            grid=(width // block,),
            in_specs=[pl.BlockSpec((rows, part), lambda i, p: (0, 0))] * (ways * outs)
            + [code_spec(j) for j in range(ways)]
            + [scale_spec(j) for j in range(ways)],
            out_specs=[pl.BlockSpec((rows, block), lambda i, p: (0, i))] * outs,
            scratch_shapes=[pltpu.VMEM((rows * outs, part), jnp.bfloat16)] * ways,
        ),
        out_shape=[jax.ShapeDtypeStruct((rows, width), jnp.float32)]
        + [jax.ShapeDtypeStruct((rows, width), jnp.bfloat16)] * (outs - 1),
        cost_estimate=pl.CostEstimate(
            flops=2 * rows * outs * part * ways * width,
            bytes_accessed=2 * part * ways * width,
            transcendentals=0,
        ),
        name="product",
    )(place, *[x for way in tokens for x in way], *[codes] * ways, *[scale] * ways)


def forward_kernel(local, act_ref, cos_ref, sin_ref, spread_ref, states_ref, code_ref, stage_ref):
    rows, width = act_ref.shape
    tiles = width // LANES

    def block(index, carry):
        at = pl.ds(pl.multiple_of(index * STEP, STEP), STEP)
        for tile in range(tiles):
            value = act_ref[at, tile_at(tile)].astype(jnp.float32)
            place = pl.ds(tile * 8, 8)
            stage_ref[place, tile_at(0)] = value[:8]
            stage_ref[place, tile_at(1)] = value[8:]
        spread = lax.dot_general(
            stage_ref[...].astype(jnp.bfloat16),
            spread_ref[...],
            (((1,), (1,)), ((), ())),
            preferred_element_type=jnp.float32,
        )
        start = pl.multiple_of(index * STEP, STEP)
        top, bottom = pl.ds(start, 8), pl.ds(pl.multiple_of(start + 8, 8), 8)
        field = []
        for base in range(0, tiles, GROUP):
            group = range(base, min(base + GROUP, tiles))
            lows = [spread[tile * 8 : tile * 8 + 8, :LANES] for tile in group]
            highs = [spread[tile * 8 : tile * 8 + 8, LANES:] for tile in group]
            for section in range(LANE_BITS):
                for slot, tile in enumerate(group):
                    low, high = lows[slot], highs[slot]
                    cosine = cos_ref[section : section + 1, tile_at(tile)]
                    sine = sin_ref[section : section + 1, tile_at(tile)]
                    low, high = cosine * low - sine * high, cosine * high + sine * low
                    states_ref[section, top, tile_at(tile)] = low
                    states_ref[section, bottom, tile_at(tile)] = high
                    lows[slot], highs[slot] = trade(low, high, section)
            field += [jnp.concatenate([lows[k], highs[k]], axis=0) for k in range(len(group))]
        for section in range(LANE_BITS, local):
            gap = 1 << (section - LANE_BITS)
            for tile in range(tiles):
                if tile & gap:
                    continue
                cosine = cos_ref[section : section + 1, tile_at(tile)]
                signed = sin_ref[section : section + 1, tile_at(tile)]
                low, high = field[tile], field[tile + gap]
                field[tile] = cosine * low + signed * high
                field[tile + gap] = cosine * high - signed * low
            for tile in range(tiles):
                states_ref[section, at, tile_at(tile)] = field[tile]

        def store(tile, codes):
            code_ref[at, tile_at(tile)] = codes

        encode(field, store)
        return carry

    lax.fori_loop(0, rows // STEP, block, 0, unroll=True)


def forward_local(acts, cos_table, sin_table, spread):
    rows, width = acts.shape
    local = cos_table.shape[0]
    block = min(rows, 32)
    table = pl.BlockSpec((local, width), lambda i: (0, 0))
    return pl.pallas_call(
        functools.partial(forward_kernel, local),
        grid=(rows // block,),
        in_specs=[
            pl.BlockSpec((block, width), lambda i: (i, 0)),
            table,
            table,
            pl.BlockSpec(spread.shape, lambda i: (0, 0)),
        ],
        out_specs=[
            pl.BlockSpec((local, block, width), lambda i: (0, i, 0)),
            pl.BlockSpec((block, width + LANES), lambda i: (i, 0)),
        ],
        out_shape=[
            jax.ShapeDtypeStruct((local, rows, width), jnp.float32),
            jax.ShapeDtypeStruct((rows, width + LANES), jnp.int16),
        ],
        scratch_shapes=[pltpu.VMEM((8 * (width // LANES), 2 * LANES), jnp.float32)],
        cost_estimate=pl.CostEstimate(
            flops=6 * local * rows * width,
            bytes_accessed=4 * (local + 1) * rows * width,
            transcendentals=0,
        ),
        name="forward_local",
    )(acts, cos_table, sin_table, spread)


def core_kernel(place_ref, state_ref, other_ref, trig_ref, pair_ref, *code_refs):
    width = state_ref.shape[2]
    count = len(code_refs)
    depth = state_ref.shape[1]
    tiles = width // LANES
    half = width // 2
    place = place_ref[0]
    start = place_ref[1] * half
    cosine_at = lambda at: trig_ref[0:1, at]
    signed_at = lambda at: trig_ref[1:2, at]
    for piece in range(count):
        source = place ^ piece
        mine = state_ref.at[source]
        other = other_ref.at[source]
        at = pl.ds(0, depth)
        scale = scale_of(other, at, width)
        field = []
        for tile in range(tiles):
            lanes = tile_at(tile)
            value = mine[at, lanes]
            partner = widen(other[at, lanes]) * scale
            field.append(cosine_at(lanes) * value + signed_at(lanes) * partner)

        def store(tile, codes):
            code_refs[piece][at, tile_at(tile)] = codes

        encode(field, store)
        for tile in range(tiles // 2):
            lanes = pl.ds(pl.multiple_of(start + tile * LANES, LANES), LANES)
            value = mine[at, lanes]
            partner = widen(other[at, lanes]) * scale
            cosine, signed = cosine_at(lanes), signed_at(lanes)
            pair_ref[0, source, at, tile_at(tile)] = cosine * value + signed * partner
            pair_ref[1, source, at, tile_at(tile)] = cosine * partner - signed * value


def core_forward(place, states, other, trig, count, chunks):
    local, rows, width = states.shape
    depth = rows // (chunks * count)
    view = states.reshape(local, chunks, count, depth, width)
    codes = other.reshape(chunks, count, depth, width + LANES)
    per = depth // STEP
    outs = pl.pallas_call(
        core_kernel,
        grid_spec=pltpu.PrefetchScalarGridSpec(
            num_scalar_prefetch=1,
            grid=(chunks, per),
            in_specs=[
                pl.BlockSpec(
                    (None, None, count, STEP, width), lambda i, j, p: (local - 1, i, 0, j, 0)
                ),
                pl.BlockSpec((None, count, STEP, width + LANES), lambda i, j, p: (i, 0, j, 0)),
                pl.BlockSpec((2, width), lambda i, j, p: (0, 0)),
            ],
            out_specs=[
                pl.BlockSpec((2, None, count, STEP, width // 2), lambda i, j, p: (0, i, 0, j, 0))
            ]
            + [pl.BlockSpec((STEP, width + LANES), lambda i, j, p: (i * per + j, 0))] * count,
        ),
        out_shape=[jax.ShapeDtypeStruct((2, chunks, count, depth, width // 2), jnp.float32)]
        + [jax.ShapeDtypeStruct((chunks * depth, width + LANES), jnp.int16)] * count,
        cost_estimate=pl.CostEstimate(
            flops=10 * rows * width, bytes_accessed=12 * rows * width, transcendentals=0
        ),
        name="core_forward",
    )(place, view, codes, trig)
    return outs[0].reshape(2, rows, width // 2), outs[1:]


def gather_kernel(count, place_ref, *refs):
    code_refs = refs[-count:]
    first_ref = refs[0]
    part_refs = refs[1 : -count - 1]
    words_ref = refs[-count - 1]
    width = first_ref.shape[2]
    place = place_ref[0]
    token = lax.broadcasted_iota(jnp.int32, (STEP, LANES), 0)
    for piece in range(count):
        source = place ^ piece
        values = []
        for tile in range(width // LANES):
            lanes = tile_at(tile)
            value = first_ref[source, :, lanes]
            for ref in part_refs:
                value = value + ref[source, :, lanes].astype(jnp.float32)
            words = words_ref[source, 0, :, lanes]
            bits = jnp.bitwise_and(jnp.right_shift(jnp.broadcast_to(words, token.shape), token), 1)
            values.append(value * bits.astype(jnp.float32))

        def store(tile, codes):
            code_refs[piece][:, tile_at(tile)] = codes

        encode(values, store)


def gather_parts(place, parts, words, count):
    rows, width = parts[0].shape
    depth = rows // count
    piece = pl.BlockSpec((count, STEP, width), lambda i, p: (0, i, 0))
    return pl.pallas_call(
        functools.partial(gather_kernel, count),
        grid_spec=pltpu.PrefetchScalarGridSpec(
            num_scalar_prefetch=1,
            grid=(depth // STEP,),
            in_specs=[piece] * len(parts)
            + [pl.BlockSpec((count, 1, 1, width), lambda i, p: (0, i, 0, 0))],
            out_specs=[pl.BlockSpec((STEP, width + LANES), lambda i, p: (i, 0))] * count,
        ),
        out_shape=[jax.ShapeDtypeStruct((depth, width + LANES), jnp.int16)] * count,
        cost_estimate=pl.CostEstimate(
            flops=12 * rows * width, bytes_accessed=12 * rows * width, transcendentals=0
        ),
        name="gather_parts",
    )(
        place,
        *[part.reshape(count, depth, width) for part in parts],
        words.reshape(count, depth // STEP, 1, width),
    )


def cross_kernel(count, bits, *refs):
    grad_refs = refs[:count]
    field_refs = refs[count : 2 * count]
    cos_ref, sin_ref = refs[2 * count : 2 * count + 2]
    out_refs = refs[2 * count + 2 : 3 * count + 2]
    term_ref, held_ref, sum_ref = refs[3 * count + 2 :]
    width = cos_ref.shape[2]
    tiles = width // LANES
    rows = pl.ds(0, STEP)
    index = pl.program_id(0)

    @pl.when(index == 0)
    def _():
        sum_ref[...] = jnp.zeros_like(sum_ref)

    grad_scales = [scale_of(ref, rows, width) for ref in grad_refs]
    field_scales = [scale_of(ref, rows, width) for ref in field_refs]
    for tile in range(tiles):
        lanes = tile_at(tile)
        levels = [[widen(r[rows, lanes]) * s for r, s in zip(field_refs, field_scales)]]
        for bit in range(bits - 1):
            field = list(levels[-1])
            for low in range(count):
                if low & (1 << bit):
                    continue
                high = low | (1 << bit)
                pair = drop_bit(low, bit)
                cosine = cos_ref[bit, pair : pair + 1, lanes]
                sine = sin_ref[bit, pair : pair + 1, lanes]
                v_low, v_high = field[low], field[high]
                field[low] = cosine * v_low - sine * v_high
                field[high] = sine * v_low + cosine * v_high
            levels.append(field)
        grad = [widen(r[rows, lanes]) * s for r, s in zip(grad_refs, grad_scales)]
        for bit in reversed(range(bits)):
            before = levels[bit]
            for low in range(count):
                if low & (1 << bit):
                    continue
                high = low | (1 << bit)
                pair = drop_bit(low, bit)
                cosine = cos_ref[bit, pair : pair + 1, lanes]
                sine = sin_ref[bit, pair : pair + 1, lanes]
                g_low, g_high = grad[low], grad[high]
                grad[low] = cosine * g_low + sine * g_high
                grad[high] = cosine * g_high - sine * g_low
                term = grad[high] * before[low] - grad[low] * before[high]
                sum_ref[bit, pair, :, lanes] += jnp.sum(term.reshape(STEP // 8, 8, LANES), axis=0)
        for piece in range(count):
            held_ref[piece, :, lanes] = grad[piece]

    for piece in range(count):

        def store(tile, codes):
            out_refs[piece][:, tile_at(tile)] = codes

        encode([held_ref[piece, :, tile_at(tile)] for tile in range(tiles)], store)

    @pl.when(index == pl.num_programs(0) - 1)
    def _():
        term_ref[...] = jnp.sum(sum_ref[...], axis=2)


def cross_sections(grads, fields, cos_table, sin_table, offset):
    count = len(grads)
    bits, pairs, width = cos_table.shape
    rows, wide = grads[0].shape
    piece = pl.BlockSpec((STEP, wide), lambda i: (i, 0))
    moved = pl.BlockSpec((STEP, wide), lambda i: (i + offset * (rows // STEP), 0))
    table = pl.BlockSpec(cos_table.shape, lambda i: (0, 0, 0))
    outs = pl.pallas_call(
        functools.partial(cross_kernel, count, bits),
        grid=(rows // STEP,),
        in_specs=[piece] * count + [moved] * count + [table] * 2,
        out_specs=[piece] * count + [table],
        out_shape=[jax.ShapeDtypeStruct((rows, wide), jnp.int16)] * count
        + [jax.ShapeDtypeStruct(cos_table.shape, jnp.float32)],
        scratch_shapes=[
            pltpu.VMEM((count, STEP, width), jnp.float32),
            pltpu.VMEM((bits, pairs, 8, width), jnp.float32),
        ],
        cost_estimate=pl.CostEstimate(
            flops=20 * bits * count * rows * width,
            bytes_accessed=6 * count * rows * width,
            transcendentals=0,
        ),
        name="cross_sections",
    )(*grads, *fields, cos_table, sin_table)
    return outs[:count], outs[count]


def backward_kernel(local, count, per, place_ref, *refs):
    grad_refs = refs[:count]
    other_refs = refs[count : 2 * count]
    states_ref, pair_ref, trig_ref, cos_ref, sin_ref, spread_ref = refs[
        2 * count : 2 * count + 6
    ]
    out_ref, term_out, grad_ref, other_ref, stage_ref, lane_sum, tile_sum, core_sum = refs[-8:]
    term_in = refs[2 * count + 6] if len(refs) > 2 * count + 14 else None
    rows, width = out_ref.shape
    tiles = width // LANES
    half = width // 2
    index = pl.program_id(0)
    start = place_ref[1] * half

    @pl.when(index == 0)
    def _():
        lane_sum[...] = jnp.zeros_like(lane_sum)
        tile_sum[...] = jnp.zeros_like(tile_sum)
        core_sum[...] = jnp.zeros_like(core_sum)

    for piece in range(count):

        @pl.when(index // per == piece)
        def _():
            at = pl.ds(pl.multiple_of((index % per) * rows, rows), rows)
            grad_ref[...] = grad_refs[piece][at, :]
            other_ref[...] = other_refs[piece][at, :]

    def folded(value):
        return jnp.sum(value.reshape(STEP // 8, 8, LANES), axis=0)

    def block(number, carry):
        at = pl.ds(pl.multiple_of(number * STEP, STEP), STEP)
        scale = scale_of(grad_ref, at, width)
        other_scale = scale_of(other_ref, at, width)
        for tile in range(tiles // 2):
            lanes = pl.ds(pl.multiple_of(start + tile * LANES, LANES), LANES)
            mine = widen(grad_ref[at, lanes]) * scale
            partner = widen(other_ref[at, lanes]) * other_scale
            term = partner * pair_ref[0, at, tile_at(tile)] - mine * pair_ref[1, at, tile_at(tile)]
            core_sum[tile] += folded(term)
        grad = []
        for tile in range(tiles):
            lanes = tile_at(tile)
            mine = widen(grad_ref[at, lanes]) * scale
            partner = widen(other_ref[at, lanes]) * other_scale
            grad.append(trig_ref[0:1, lanes] * mine - trig_ref[1:2, lanes] * partner)
        for section in reversed(range(LANE_BITS, local)):
            gap = 1 << (section - LANE_BITS)
            for tile in range(tiles):
                if tile & gap:
                    continue
                cosine = cos_ref[section : section + 1, tile_at(tile)]
                signed = sin_ref[section : section + 1, tile_at(tile)]
                low, high = grad[tile], grad[tile + gap]
                before_low = states_ref[section, at, tile_at(tile)]
                before_high = states_ref[section, at, tile_at(tile + gap)]
                term = folded(high * before_low - low * before_high)
                place = drop_bit(tile, section - LANE_BITS)
                tile_sum[section - LANE_BITS, place] += term
                grad[tile] = cosine * low - signed * high
                grad[tile + gap] = cosine * high + signed * low
        first_row = pl.multiple_of(number * STEP, STEP)
        top, bottom = pl.ds(first_row, 8), pl.ds(pl.multiple_of(first_row + 8, 8), 8)
        for base in range(0, tiles, GROUP):
            group = range(base, min(base + GROUP, tiles))
            lows = [grad[tile][:8] for tile in group]
            highs = [grad[tile][8:] for tile in group]
            for section in reversed(range(LANE_BITS)):
                for slot, tile in enumerate(group):
                    low, high = trade(lows[slot], highs[slot], section)
                    cosine = cos_ref[section : section + 1, tile_at(tile)]
                    sine = sin_ref[section : section + 1, tile_at(tile)]
                    before_low = states_ref[section, top, tile_at(tile)]
                    before_high = states_ref[section, bottom, tile_at(tile)]
                    term = high * before_low - low * before_high
                    lane_sum[section, tile % 2, tile // 2] += term
                    lows[slot] = cosine * low + sine * high
                    highs[slot] = cosine * high - sine * low
            for slot, tile in enumerate(group):
                place = pl.ds(tile * 8, 8)
                stage_ref[place, tile_at(0)] = lows[slot]
                stage_ref[place, tile_at(1)] = highs[slot]
        plain = lax.dot_general(
            stage_ref[...].astype(jnp.bfloat16),
            spread_ref[...],
            (((1,), (0,)), ((), ())),
            preferred_element_type=jnp.float32,
        )
        for tile in range(tiles):
            rows_of = plain[tile * 8 : tile * 8 + 8]
            value = jnp.concatenate([rows_of[:, :LANES], rows_of[:, LANES:]], axis=0)
            out_ref[at, tile_at(tile)] = value.astype(out_ref.dtype)
        return carry

    lax.fori_loop(0, rows // STEP, block, 0, unroll=True)

    @pl.when(index == pl.num_programs(0) - 1)
    def _():
        low = lax.broadcasted_iota(jnp.int32, (tiles // 2, LANES), 1) < LANES // 2
        for section in range(LANE_BITS):
            even = jnp.sum(lane_sum[section, 0], axis=1)
            odd = jnp.sum(lane_sum[section, 1], axis=1)
            even = even + pltpu.roll(even, LANES // 2, 1)
            odd = odd + pltpu.roll(odd, LANES // 2, 1)
            term_out[section] = jnp.where(low, even, odd)
        for section in range(LANE_BITS, local):
            term_out[section] = jnp.sum(tile_sum[section - LANE_BITS], axis=1)
        flip = (1 - 2 * place_ref[1]).astype(jnp.float32)
        term_out[local] = flip * jnp.sum(core_sum[...], axis=1)
        if term_in is not None:
            term_out[...] += term_in[...]


def backward_local(
    place, grads, others, states, pair, trig, cos_table, sin_table, spread, before, chunk
):
    count = len(grads)
    depth = grads[0].shape[0]
    local, rows, width = states.shape
    tiles = width // LANES
    high = local - LANE_BITS
    shape = (local + 1, tiles // 2, LANES)
    base = chunk * count
    block = min(depth, 32)
    per = depth // block
    fixed = lambda shape: pl.BlockSpec(shape, lambda i, p: (0,) * len(shape))
    row_of = lambda i, p: (base + (p[0] ^ (i // per))) * per + i % per
    return pl.pallas_call(
        functools.partial(backward_kernel, local, count, per),
        grid_spec=pltpu.PrefetchScalarGridSpec(
            num_scalar_prefetch=1,
            grid=(count * per,),
            in_specs=[fixed((depth, width + LANES))] * (2 * count)
            + [
                pl.BlockSpec((local, block, width), lambda i, p: (0, row_of(i, p), 0)),
                pl.BlockSpec((2, block, width // 2), lambda i, p: (0, row_of(i, p), 0)),
                fixed((2, width)),
                fixed((local, width)),
                fixed((local, width)),
                fixed(spread.shape),
            ]
            + [fixed(shape), pl.BlockSpec(memory_space=pl.ANY)][: len(before)],
            out_specs=[
                pl.BlockSpec((block, width), lambda i, p: (row_of(i, p), 0)),
                fixed(shape),
            ],
            scratch_shapes=[
                pltpu.VMEM((block, width + LANES), jnp.int16),
                pltpu.VMEM((block, width + LANES), jnp.int16),
                pltpu.VMEM((8 * tiles, 2 * LANES), jnp.float32),
                pltpu.VMEM((LANE_BITS, 2, tiles // 2, 8, LANES), jnp.float32),
                pltpu.VMEM((high, tiles // 2, 8, LANES), jnp.float32),
                pltpu.VMEM((tiles // 2, 8, LANES), jnp.float32),
            ],
        ),
        out_shape=[
            jax.ShapeDtypeStruct((rows, width), jnp.bfloat16),
            jax.ShapeDtypeStruct(shape, jnp.float32),
        ],
        input_output_aliases={2 * count + 8: 0} if before else {},
        cost_estimate=pl.CostEstimate(
            flops=8 * local * depth * count * width,
            bytes_accessed=4 * (local + 2) * depth * count * width,
            transcendentals=0,
        ),
        name="backward_local",
    )(place, *grads, *others, states, pair, trig, cos_table, sin_table, spread, *before)


def tree_sum(parts):
    while len(parts) > 1:
        parts = [parts[k] + parts[k + 1] for k in range(0, len(parts), 2)]
    return parts[0]


def gather_shares(value, line, core, count):
    near = jnp.stack([value] + [swap(value, "tensor", 2 * m) for m in range(1, count)])
    near = jnp.take(near, line ^ jnp.arange(count, dtype=jnp.int32), axis=0)
    other = swap(near, "tensor", 1)
    first = core == 0
    return jnp.stack([jnp.where(first, near, other), jnp.where(first, other, near)], axis=1)


def scatter_shares(value, me, bits):
    for bit in reversed(range(bits)):
        halves = value.reshape((2, -1) + value.shape[1:])
        own = (me >> bit) & 1
        value = pick(halves, own) + swap(pick(halves, 1 - own), "tensor", 1 << bit)
    return value[0]


def body(activations, angles, clip_bits, codes, exponents, cotangent):
    rows, width = activations.shape
    sections, share = angles.shape
    groups = lax.axis_size("dp")
    devices = lax.axis_size("tensor")
    ways = devices // groups
    columns = codes.shape[1]
    part = columns // ways
    local = width.bit_length() - 1
    cross = sections - local
    count = devices // 2
    me = lax.axis_index("tensor")
    mine = lax.axis_index("dp")
    level = me // ways
    core = me & 1
    line = me >> 1
    chunks = chunks_of(rows, count)
    chunk_rows = rows // chunks
    place = jnp.stack([line, core])

    gathered = []
    for q in range(chunks):
        own = cotangent[q * chunk_rows : (q + 1) * chunk_rows]
        blocks = jnp.stack([own] + [swap(own, "tensor", m * ways) for m in range(1, groups)])
        arrived = [pick(blocks, level ^ mine)] + [
            swap(pick(blocks, level ^ mine ^ m), "dp", m) for m in range(1, groups)
        ]
        gathered.append(
            [arrived]
            + [[swap(x, "tensor", m) for x in arrived] for m in range(1, ways)]
        )

    scale = jnp.exp2(exponents.astype(jnp.float32)).astype(jnp.bfloat16)
    scale = scale.reshape(-1, 1, part)
    column_place = jnp.stack([me % ways, mine * ways])

    cosine = jnp.cos(angles)
    sine = jnp.sin(angles)
    cos_table, sin_table = local_tables(cosine[:local], sine[:local], width)
    spread = spread_matrix()
    states, last_codes = forward_local(activations, cos_table, sin_table, spread)

    trig = jnp.stack([cosine[local:], sine[local:]])
    trig = gather_shares(trig, line, core, count)
    trig = jnp.moveaxis(trig.reshape(devices, 2, cross, share), 0, 2)
    trig = trig.reshape(2, cross, devices // 2, width)
    flip = (1 - 2 * core).astype(jnp.float32)
    core_trig = lax.dynamic_index_in_dim(trig[:, 0], line, 1, keepdims=False)
    core_trig = core_trig * jnp.stack([jnp.float32(1), -flip])[:, None]
    jj = jnp.arange(count // 2, dtype=jnp.int32)
    cross_cos, cross_sin, flips = [], [], []
    for bit in range(cross - 1):
        pair = (drop_bit(line, bit) ^ jj) * 2 + core
        flips.append((1 - 2 * ((line >> bit) & 1)).astype(jnp.float32))
        cross_cos.append(jnp.take(trig[0, bit + 1], pair, axis=0))
        cross_sin.append(jnp.take(trig[1, bit + 1], pair, axis=0) * flips[-1])
    cross_cos = jnp.stack(cross_cos)
    cross_sin = jnp.stack(cross_sin)

    partner_codes = swap(last_codes, "tensor", 1)
    pair_states, fields = core_forward(place, states, partner_codes, core_trig, count, chunks)
    fields = [fields[0]] + [swap(fields[m], "tensor", 2 * m) for m in range(1, count)]

    before = ()
    cross_terms = []
    backs = []
    word_rows = chunk_rows // 16
    for q in range(chunks):
        sent = product(column_place, gathered[q], codes, scale)
        parts = [sent[0]] + [swap(sent[m], "dp", m) for m in range(1, groups)]
        words = clip_bits[q * word_rows : (q + 1) * word_rows]
        grads = gather_parts(place, parts, words, count)
        grads = [grads[0]] + [swap(grads[m], "tensor", 2 * m) for m in range(1, count)]
        grads, terms = cross_sections(grads, fields, cross_cos, cross_sin, q)
        cross_terms.append(terms)
        backs.append([grads[0]] + [swap(grads[m], "tensor", 2 * m) for m in range(1, count)])

    for q in range(chunks):
        others = [swap(grad, "tensor", 1) for grad in backs[q]]
        whole, local_terms = backward_local(
            place, backs[q], others, states, pair_states, core_trig,
            cos_table, sin_table, spread, before, q,
        )
        before = (local_terms, whole)

    terms = functools.reduce(jnp.add, cross_terms)
    natural = jnp.stack(
        [
            jnp.take(terms[bit], drop_bit(line, bit) ^ jj, axis=0) * flips[bit]
            for bit in range(cross - 1)
        ]
    )
    natural = natural.reshape(cross - 1, count // 2, 1, 2, share)
    natural = jnp.where(
        jnp.arange(2, dtype=jnp.int32)[None, None, :, None, None] == core, natural, 0.0
    )
    natural = jnp.moveaxis(natural.reshape(cross - 1, devices, share), 1, 0)
    owned = scatter_shares(natural, me, cross)

    owned = owned.reshape(cross - 1, share // LANES, LANES)
    final = jnp.concatenate([local_terms, owned], axis=0)
    angle_grad = tree_sum([final] + [swap(final, "dp", m) for m in range(1, groups)])
    angle_grad = angle_grad.reshape(sections, share)
    return (whole, angle_grad)


def chunks_of(rows, count):
    chunks = CHUNKS
    while rows // (chunks * count) < STEP:
        chunks //= 2
    return chunks


def solution(mesh):
    placed = (
        P("dp", "tensor"),
        P(None, "tensor"),
        P("dp", "tensor"),
        P("tensor", "dp"),
        P(),
        P("dp", "tensor"),
    )

    return jax.shard_map(
        body,
        mesh=mesh,
        in_specs=placed,
        out_specs=(P("dp", "tensor"), P(None, "tensor")),
        check_vma=False,
    )
```
